32 devices in a mesh: gx: 4 (over y, x), gy: 4 (over z), gz: 2 (over core).
Axes of the slice: x: 2, y: 2, z: 4, core: 2. Of those that a mesh axis runs over, the one named last changes fastest.
Arguments:
- density_scatter: float32 [16, 32, 256], P('gx', 'gy', 'gz'), may hold values from 0.8 to 1.25
- initial_velocity: float32 [3, 16, 32, 256], P(None, 'gx', 'gy', 'gz'), may hold values from -0.12 to 0.12
- bubble_mask: int32 [16, 32, 256], P('gx', 'gy', 'gz'), may hold values from 0 to 1, as said below
- wall_flags: int32 [16, 32, 256], P('gx', 'gy', 'gz'), may hold values 0 or 1
Outputs:
- density_field: float32 [16, 32, 256], P('gx', 'gy', 'gz')
- velocity_field: float32 [3, 16, 32, 256], P(None, 'gx', 'gy', 'gz')
The draws below stay inside these ranges and needn't reach their ends.
Inputs may be any that keep to these rules, and one draw needn't show every extreme that they name: `bubble_mask`: 1 at nodes inside a vapour bubble, 0 in the liquid. `wall_flags`: 1 at solid nodes, 0 at fluid nodes.
All inputs are finite; a program needn't handle non-finite values. No bound on the sum of `wall_flags` on one device may be relied on, other than what follows from the above.
Results may differ from the reference program's by a relative error of at most 0.0003.
Values sent between devices are 32-bit elements; how exact they have to be, the bound alone decides.
No kernel may reach another device: no remote copies, remote signals or barrier semaphores. Data moves between devices by JAX's collectives and lax.ppermute only.
A program may use at most 64 MiB of HBM per device.

```python
import math
import jax
import jax.numpy as jnp
import numpy as np
from jax import lax

STEPS = 4
NX = 16
NY = 32
NZ = 256


def spread_tiles(values):
    values = jnp.repeat(values, 8, axis=0)
    values = jnp.repeat(values, 8, axis=1)
    return jnp.repeat(values, 8, axis=2)


def draw_bubble_mask(key, part):
    key_centre, key_radius = jax.random.split(jax.random.fold_in(key, 17))
    tiles = (NX // 8, NY // 8, NZ // 8)
    centre = jax.random.randint(key_centre, tiles + (3,), 2, 6)
    radius = spread_tiles(jax.random.randint(key_radius, tiles, 1, 4))
    first = (jnp.arange(NX) % 8)[:, None, None] - spread_tiles(centre[..., 0])
    second = (jnp.arange(NY) % 8)[None, :, None] - spread_tiles(centre[..., 1])
    third = (jnp.arange(NZ) % 8)[None, None, :] - spread_tiles(centre[..., 2])
    distance = first * first + second * second + third * third
    return (distance <= radius * radius).astype(jnp.int32)


def touch_ends(drawn, stream_key, smallest, high):
    longest = drawn.shape.index(max(drawn.shape))
    spots = []
    for shift in (0, 1):
        where = [jax.random.randint(jax.random.fold_in(stream_key, axis), (), 0, length) for axis, length in enumerate(drawn.shape)]
        where[longest] = (where[longest] + shift) % drawn.shape[longest]
        spots.append(tuple(where))
    return drawn.at[spots[0]].set(smallest).at[spots[1]].set(high)


def steps_of(rng, extent, shards, least, top_value):
    level, own = 1.0, jax.random.fold_in(rng, 6)
    for position, blocks in shards:
        draws = jnp.exp(jax.random.uniform(jax.random.fold_in(own, position), (blocks,), jnp.float32, least / len(shards), top_value / len(shards)))
        level = level * jnp.repeat(draws, extent[position] // blocks).reshape([-1 if axis == position else 1 for axis in range(len(extent))])
    return level


def gaussian(own_key, dims, width, limit, pieces=(), kind=jnp.bfloat16):
    drawn = jax.random.normal(own_key, dims, jnp.float32) * width
    if len(pieces) > 0:
        drawn = steps_of(own_key, dims, pieces, -0.22, 0.18) * drawn
    return jnp.clip(drawn, min=-limit, max=limit).astype(kind)


def setup_inputs(seed: int = 0) -> dict:
    arg_keys = jax.random.split(jax.random.key(seed), 5)
    density_scatter = jnp.clip(jnp.exp(math.log(1.25) - 0.4462871 * jax.random.uniform(arg_keys[0], (NX, NY, NZ), jnp.float32) ** steps_of(arg_keys[0], (NX, NY, NZ), ((0, 4), (1, 4), (2, 2)), -0.2, 0.2)), 0.8, 1.25)
    initial_velocity = gaussian(arg_keys[1], (3, NX, NY, NZ), 0.04, 0.12, ((1, 4), (2, 4), (3, 2)), jnp.float32)
    bubble_mask = draw_bubble_mask(jax.random.fold_in(arg_keys[4], 71), 0)
    wall_flags = touch_ends((jax.random.randint(arg_keys[3], (NX, NY, NZ), 0, 16) < 1).astype(jnp.int32), jax.random.fold_in(arg_keys[3], 1), 0, 1)
    return dict(density_scatter=density_scatter, initial_velocity=initial_velocity, bubble_mask=bubble_mask, wall_flags=wall_flags)


lattice_velocities = np.array([[0, 0, 0], [1, 0, 0], [-1, 0, 0], [0, 1, 0], [0, -1, 0], [0, 0, 1], [0, 0, -1], [1, 1, 0], [-1, -1, 0], [1, -1, 0], [-1, 1, 0], [1, 0, 1], [-1, 0, -1], [1, 0, -1], [-1, 0, 1], [0, 1, 1], [0, -1, -1], [0, 1, -1], [0, -1, 1]])
weights = [1.0 / 3.0] + [1.0 / 18.0] * 6 + [1.0 / 36.0] * 12
opposite = [0, 2, 1, 4, 3, 6, 5, 8, 7, 10, 9, 12, 11, 14, 13, 16, 15, 18, 17]
liquid = 0.28
vapour = 0.06
wall_potential = 0.5
attractive_coupling = 1.0
critical_thermal_ratio = 0.06
viscous_rate = 1.25

def relaxation_matrix():
    table = lattice_velocities * 1.0
    first, second, third = (table[:, 0], table[:, 1], table[:, 2])
    squared_speed = first * first + second * second + third * third
    rows = [np.ones(19), 19.0 * squared_speed - 30.0, (21.0 * squared_speed * squared_speed - 53.0 * squared_speed + 24.0) / 2.0, first, (5.0 * squared_speed - 9.0) * first, second, (5.0 * squared_speed - 9.0) * second, third, (5.0 * squared_speed - 9.0) * third, 3.0 * first * first - squared_speed, (3.0 * squared_speed - 5.0) * (3.0 * first * first - squared_speed), second * second - third * third, (3.0 * squared_speed - 5.0) * (second * second - third * third), first * second, second * third, first * third, first * (second * second - third * third), second * (third * third - first * first), third * (first * first - second * second)]
    moment_space_vector = np.stack(rows)
    inverse_transform = moment_space_vector.T / np.sum(moment_space_vector * moment_space_vector, axis=1)
    rates = np.array([0.0, 1.19, 1.4, 0.0, 1.2, 0.0, 1.2, 0.0, 1.2, viscous_rate, 1.4, viscous_rate, 1.4, viscous_rate, viscous_rate, viscous_rate, 1.98, 1.98, 1.98])
    return inverse_transform * rates[None, :] @ moment_space_vector

def equilibrium(mass_per_volume, velocity):
    squared_speed = velocity[0] * velocity[0] + velocity[1] * velocity[1] + velocity[2] * velocity[2]
    rows = []
    for i in range(19):
        projection = float(lattice_velocities[i, 0]) * velocity[0] + float(lattice_velocities[i, 1]) * velocity[1] + float(lattice_velocities[i, 2]) * velocity[2]
        rows.append(weights[i] * mass_per_volume * (1.0 + 3.0 * projection + 4.5 * projection * projection - 1.5 * squared_speed))
    return jnp.stack(rows)

def moments(populations):
    return jnp.stack([sum((float(lattice_velocities[i, k]) * populations[i] for i in range(19) if lattice_velocities[i, k] != 0)) for k in range(3)])

def pseudo_potential(mass_per_volume):
    thermodynamic_stress = mass_per_volume * critical_thermal_ratio * (1.0 + mass_per_volume + mass_per_volume * mass_per_volume - mass_per_volume * mass_per_volume * mass_per_volume) / ((1.0 - mass_per_volume) * (1.0 - mass_per_volume) * (1.0 - mass_per_volume)) - attractive_coupling * mass_per_volume * mass_per_volume
    return jnp.sqrt(6.0 * (mass_per_volume / 3.0 - thermodynamic_stress))

def attraction(potential, nearby):
    parts = []
    for k in range(3):
        total = sum((weights[i] * float(lattice_velocities[i, k]) * nearby[i - 1] for i in range(1, 19) if lattice_velocities[i, k] != 0))
        parts.append(potential * total)
    return jnp.stack(parts)

def collide(populations, mass_per_volume, momentum, force, solid, kernel):
    velocity = momentum / mass_per_volume
    settled = equilibrium(mass_per_volume, velocity)
    pushed = equilibrium(mass_per_volume, velocity + force / mass_per_volume)
    relaxed = jnp.einsum('ij,jxyz->ixyz', kernel, populations - settled, precision=lax.Precision.HIGHEST)
    relaxed_distribution = populations - relaxed + pushed - settled
    bounced = populations[np.array(opposite)]
    return jnp.where(solid[None], bounced, relaxed_distribution)

def reference(density_scatter, initial_velocity, bubble_mask, wall_flags):
    kernel = jnp.asarray(relaxation_matrix(), jnp.float32)
    solid = wall_flags == 1
    mass_per_volume = jnp.where(bubble_mask == 1, vapour, liquid) * density_scatter
    populations = equilibrium(mass_per_volume, initial_velocity)
    for step in range(STEPS):
        mass_per_volume = lax.optimization_barrier(jnp.sum(populations, axis=0))
        momentum = moments(populations)
        potential = jnp.where(solid, wall_potential, pseudo_potential(mass_per_volume))
        nearby = [jnp.roll(potential, tuple((-int(v) for v in lattice_velocities[i])), axis=(0, 1, 2)) for i in range(1, 19)]
        force = attraction(potential, nearby)
        post = collide(populations, mass_per_volume, momentum, force, solid, kernel)
        populations = jnp.stack([jnp.roll(post[i], tuple((int(v) for v in lattice_velocities[i])), axis=(0, 1, 2)) for i in range(19)])
    mass_per_volume = lax.optimization_barrier(jnp.sum(populations, axis=0))
    momentum = moments(populations)
    density_field = jnp.where(solid, 0.0, mass_per_volume / liquid)
    velocity_field = jnp.where(solid[None], 0.0, math.sqrt(3.0) * momentum / mass_per_volume)
    return (density_field, velocity_field)
```

```python
import math

import jax
import jax.numpy as jnp
import numpy as np
from jax import lax
from jax.experimental import pallas as pl
from jax.experimental.pallas import tpu as pltpu
from jax.sharding import PartitionSpec as P

STEPS = 4
HALO = 2 * STEPS
LANES = 128

C = np.array(
    [
        [0, 0, 0],
        [1, 0, 0],
        [-1, 0, 0],
        [0, 1, 0],
        [0, -1, 0],
        [0, 0, 1],
        [0, 0, -1],
        [1, 1, 0],
        [-1, -1, 0],
        [1, -1, 0],
        [-1, 1, 0],
        [1, 0, 1],
        [-1, 0, -1],
        [1, 0, -1],
        [-1, 0, 1],
        [0, 1, 1],
        [0, -1, -1],
        [0, 1, -1],
        [0, -1, 1],
    ]
)
WEIGHTS = [1.0 / 3.0] + [1.0 / 18.0] * 6 + [1.0 / 36.0] * 12
OPPOSITE = [0, 2, 1, 4, 3, 6, 5, 8, 7, 10, 9, 12, 11, 14, 13, 16, 15, 18, 17]
LIQUID = 0.28
VAPOUR = 0.06
WALL_POTENTIAL = 0.5
ATTRACTION = 1.0
TEMPERATURE = 0.06

KEEP_E = 1.0 - 1.19
KEEP_P = 1.0 - 1.4
KEEP_Q = 1.0 - 1.2
KEEP_N = 1.0 - 1.25
KEEP_M = 1.0 - 1.98


def equilibrium(rho, u):
    rest = 1.0 - 1.5 * (u[0] * u[0] + u[1] * u[1] + u[2] * u[2])
    scaled = [None] * 3
    scaled[0] = rho * WEIGHTS[0]
    scaled[1] = rho * WEIGHTS[1]
    scaled[2] = rho * WEIGHTS[7]
    rows = [scaled[0] * rest]
    for i in range(1, 19, 2):
        terms = [u[k] if C[i, k] > 0 else -u[k] for k in range(3) if C[i, k] != 0]
        along = terms[0] if len(terms) == 1 else terms[0] + terms[1]
        even = rest + 4.5 * (along * along)
        odd = 3.0 * along
        w = scaled[len(terms)]
        rows += [w * (even + odd), w * (even - odd)]
    return rows


def potential(rho, solid):
    square = rho * rho
    gap = 1.0 - rho
    pressure = (
        rho * TEMPERATURE * (1.0 + rho + square - square * rho) / (gap * gap * gap)
        - ATTRACTION * square
    )
    return jnp.where(solid, WALL_POTENTIAL, jnp.sqrt(6.0 * (rho * (1.0 / 3.0) - pressure)))


def moments(f):
    d = [None] + [f[i] - f[i + 1] for i in range(1, 19, 2)]
    jx = d[1] + ((d[4] + d[5]) + (d[6] + d[7]))
    jy = d[2] + ((d[4] - d[5]) + (d[8] + d[9]))
    jz = d[3] + ((d[6] - d[7]) + (d[8] - d[9]))
    return jx, jy, jz


def collide(f, force, solid):
    s = [None] + [f[i] + f[i + 1] for i in range(1, 19, 2)]
    d = [None] + [f[i] - f[i + 1] for i in range(1, 19, 2)]
    xy, xz, yz = s[4] + s[5], s[6] + s[7], s[8] + s[9]
    axes = s[1] + s[2] + s[3]
    diagonals = xy + xz + yz
    rho = f[0] + axes + diagonals
    p_xy, q_xy = d[4] + d[5], d[4] - d[5]
    p_xz, q_xz = d[6] + d[7], d[6] - d[7]
    p_yz, q_yz = d[8] + d[9], d[8] - d[9]
    j = [d[1] + (p_xy + p_xz), d[2] + (q_xy + p_yz), d[3] + (q_xz + q_yz)]
    inverse = 1.0 / rho
    u = [j[k] * inverse for k in range(3)]
    moved = [j[k] + force[k] for k in range(3)]
    v = [moved[k] * inverse for k in range(3)]
    uu = [j[k] * u[k] for k in range(3)]
    vv = [moved[k] * v[k] for k in range(3)]
    u2 = uu[0] + uu[1] + uu[2]
    v2 = vv[0] + vv[1] + vv[2]

    energy = (
        KEEP_E * (8.0 * diagonals - 11.0 * axes - 30.0 * f[0])
        - (11.0 * (1.0 - KEEP_E)) * rho
        + 19.0 * (v2 - KEEP_E * u2)
    )
    epsilon = (
        KEEP_P * (12.0 * f[0] - 4.0 * axes + diagonals)
        + (3.0 * (1.0 - KEEP_P)) * rho
        - 5.5 * (v2 - KEEP_P * u2)
    )
    mass = rho * (1.0 / 19.0)
    even_rest = mass - (30.0 / 2394.0) * energy + (12.0 / 252.0) * epsilon
    even_axis = mass - (11.0 / 2394.0) * energy - (4.0 / 252.0) * epsilon
    even_diag = mass + (8.0 / 2394.0) * energy + (1.0 / 252.0) * epsilon

    def stress(a, b, at_v, at_u, scale):
        on_axis = (
            ((KEEP_N + 2.0 * KEEP_P) * scale) * a
            + ((KEEP_N - KEEP_P) * scale) * b
            + (1.5 * scale) * at_v
            - ((KEEP_N + 0.5 * KEEP_P) * scale) * at_u
        )
        half = 0.5 * scale
        on_diagonal = (
            ((2.0 * KEEP_N - 2.0 * KEEP_P) * half) * a
            + ((2.0 * KEEP_N + KEEP_P) * half) * b
            + (1.5 * half) * at_v
            - ((2.0 * KEEP_N - 0.5 * KEEP_P) * half) * at_u
        )
        return on_axis, on_diagonal

    h, g = stress(
        3.0 * s[1] - axes,
        diagonals - 3.0 * yz,
        3.0 * vv[0] - v2,
        3.0 * uu[0] - u2,
        1.0 / 36.0,
    )
    k, l = stress(s[2] - s[3], xy - xz, vv[1] - vv[2], uu[1] - uu[2], 1.0 / 12.0)

    def shear(a, b, pair):
        return (0.25 * KEEP_N) * (pair - j[a] * u[b]) + 0.25 * (moved[a] * v[b])

    t_xy = shear(0, 1, s[4] - s[5])
    t_xz = shear(0, 2, s[6] - s[7])
    t_yz = shear(1, 2, s[8] - s[9])

    flux_j = KEEP_Q * 5.0 / 3.0 - 2.0 / 3.0
    axis_odd = [
        ((1.0 - flux_j) / 10.0) * j[n] + (0.5 * KEEP_Q) * d[n + 1] + (1.0 / 6.0) * force[n]
        for n in range(3)
    ]
    diag_odd = [
        (0.1 + flux_j / 40.0) * j[n] - (KEEP_Q / 8.0) * d[n + 1] + (1.0 / 12.0) * force[n]
        for n in range(3)
    ]
    third = KEEP_M / 8.0
    mx, my, mz = third * (p_xy - p_xz), third * (p_yz - q_xy), third * (q_xz - q_yz)

    twist = even_axis - h
    evens = [even_axis + 2.0 * h, twist + k, twist - k]
    ring = even_diag + g
    e_xy, e_xz, e_yz = ring + l, ring - l, even_diag - 2.0 * g
    a, b = diag_odd[0] + mx, diag_odd[1] - my
    odd_xy = (a + b, a - b)
    a, b = diag_odd[0] - mx, diag_odd[2] + mz
    odd_xz = (a + b, a - b)
    a, b = diag_odd[1] + my, diag_odd[2] - mz
    odd_yz = (a + b, a - b)

    post = [even_rest]
    for n in range(3):
        post += [evens[n] + axis_odd[n], evens[n] - axis_odd[n]]
    for even, t, odd in ((e_xy, t_xy, odd_xy), (e_xz, t_xz, odd_xz), (e_yz, t_yz, odd_yz)):
        same, cross = even + t, even - t
        post += [same + odd[0], same - odd[0], cross + odd[1], cross - odd[1]]
    return [jnp.where(solid, f[OPPOSITE[i]], post[i]) for i in range(19)]


class Shape:
    def __init__(self, mesh, block):
        self.nx, self.ny, self.nz = (mesh.shape[a] for a in ("gx", "gy", "gz"))
        self.x, self.y, self.z = block
        self.slab = self.z // self.nx
        width = 1
        while width < self.slab + 2 * HALO:
            width *= 2
        self.width = width
        self.groups = LANES // width
        self.own = self.x // self.groups
        self.subs = self.x * self.nx // self.groups
        self.rows = self.y + 2 * HALO
        assert self.z == LANES and self.slab * self.nx == self.z and width <= LANES
        assert self.y == HALO and self.own * self.groups == self.x
        assert self.subs % 8 == 0 and self.slab * self.x <= LANES
        if self.nx & (self.nx - 1) == 0:
            self.peer = lambda k, slot: jnp.bitwise_xor(k, slot)
            self.perm = lambda slot: [(i, i ^ slot) for i in range(self.nx)]
            self.sender = self.peer
        else:
            self.peer = lambda k, slot: lax.rem(k + slot, self.nx)
            self.sender = lambda k, slot: lax.rem(k + self.nx - slot, self.nx)
            self.perm = lambda slot: [(i, (i + slot) % self.nx) for i in range(self.nx)]


def vmem(n):
    return [pl.BlockSpec(memory_space=pltpu.VMEM)] * n


def gather_inputs(scatter, velocity, bubbles, walls):
    def body(s_ref, u_ref, b_ref, w_ref, out):
        out[0] = jnp.where(b_ref[...] == 1, VAPOUR, LIQUID) * s_ref[...]
        for k in range(3):
            out[1 + k] = u_ref[k]
        out[4] = jnp.where(w_ref[...] == 1, 1.0, 0.0)

    return pl.pallas_call(
        body,
        name="pack_inputs",
        out_shape=jax.ShapeDtypeStruct((5,) + scatter.shape, jnp.float32),
        in_specs=vmem(4),
        out_specs=vmem(1)[0],
    )(scatter, velocity, bubbles, walls)


def cut_slabs(values, before, after, sh):
    def body(v_ref, b_ref, a_ref, *outs):
        k = lax.axis_index("gx")
        lane = lax.broadcasted_iota(jnp.int32, (sh.y, LANES), 1)
        group = lane // sh.width
        for slot, out in enumerate(outs):
            q = sh.peer(k, slot)
            low = (lane >= LANES - HALO) & (q == 0)
            high = (lane < HALO) & (q == sh.nx - 1)
            start = HALO - q * sh.slab + 2 * LANES
            for n in range(5):
                for m in range(sh.own):
                    merged = None
                    for g in range(sh.groups):
                        x = m * sh.groups + g
                        plane = jnp.where(low, b_ref[n, x], v_ref[n, x])
                        plane = jnp.where(high, a_ref[n, x], plane)
                        plane = pltpu.roll(plane, lax.rem(start + g * sh.width, LANES), 1)
                        merged = plane if g == 0 else jnp.where(group == g, plane, merged)
                    out[n, m] = merged

    return pl.pallas_call(
        body,
        name="cut_slabs",
        out_shape=[jax.ShapeDtypeStruct((5, sh.own, sh.y, LANES), jnp.float32)] * sh.nx,
        in_specs=vmem(3),
        out_specs=vmem(sh.nx),
    )(values, before, after)


def run_steps(below, middle, above, sh):
    rows, subs, width = sh.rows, sh.subs, sh.width

    def body(b_ref, m_ref, a_ref, *rest):
        outs = rest[: sh.nx]
        raw, first, second, psi_ref, solid_ref, done = rest[sh.nx :]
        k = lax.axis_index("gx")
        lane = lax.broadcasted_iota(jnp.int32, (subs, LANES), 1)
        group = lane // width

        for slot in range(sh.nx):
            base = sh.sender(k, slot) * (sh.own * rows)
            for part, ref in enumerate((b_ref, m_ref, a_ref)):
                for n in range(5):
                    for m in range(sh.own):
                        at = pl.multiple_of(base + m * rows + part * sh.y, 8)
                        raw[n, pl.ds(at, sh.y), :] = ref[slot, n, m]

        def shifted(value, cx, cz):
            if cx == 1:
                turned = pltpu.roll(value, 1, 0)
                value = jnp.where(group == sh.groups - 1, turned, value)
            if cx == -1:
                turned = pltpu.roll(value, subs - 1, 0)
                value = jnp.where(group == 0, turned, value)
            turn = (cx * width + cz) % LANES
            return pltpu.roll(value, turn, 1) if turn else value

        def start(y, _):
            read = lambda n: raw[n, pl.ds(y, subs, stride=rows), :]
            rho, u = read(0), [read(1), read(2), read(3)]
            solid_ref[y] = read(4)
            for i, row in enumerate(equilibrium(rho, u)):
                first[i, y] = row
            return 0

        lax.fori_loop(0, rows, start, 0)

        source, target = first, second
        for step in range(STEPS):

            def weigh(y, source=source):
                rho = source[0, y]
                for i in range(1, 19):
                    rho = rho + source[i, y]
                psi_ref[y] = potential(rho, solid_ref[y] > 0.5)

            def advance(y, source=source, target=target):
                here, up, down = psi_ref[y], psi_ref[y + 1], psi_ref[y - 1]
                both, rise = up + down, up - down
                doubled = 2.0 * here + both
                z_sum = doubled + (shifted(here, 0, -1) + shifted(here, 0, 1))
                x_sum = doubled + (shifted(here, -1, 0) + shifted(here, 1, 0))
                scale = here * (1.0 / 36.0)
                force = [
                    scale * (shifted(z_sum, -1, 0) - shifted(z_sum, 1, 0)),
                    scale
                    * (
                        2.0 * rise
                        + (shifted(rise, -1, 0) + shifted(rise, 1, 0))
                        + (shifted(rise, 0, -1) + shifted(rise, 0, 1))
                    ),
                    scale * (shifted(x_sum, 0, -1) - shifted(x_sum, 0, 1)),
                ]
                f = [source[i, y] for i in range(19)]
                post = collide(f, force, solid_ref[y] > 0.5)
                for i in range(19):
                    cx, cy, cz = (int(c) for c in C[i])
                    target[i, y + cy] = shifted(post[i], cx, cz)

            lo = 2 * step

            def weigh_some(n, _):
                for r in range(4):
                    weigh(lo + 4 * n + r)
                return 0

            def advance_some(n, _):
                for r in range(2):
                    advance(lo + 1 + 2 * n + r)
                return 0

            lax.fori_loop(0, (rows - 2 * lo) // 4, weigh_some, 0)
            lax.fori_loop(0, (rows - 2 * lo - 2) // 2, advance_some, 0)
            source, target = target, source

        def finish(y, _):
            f = [source[i, y + HALO] for i in range(19)]
            rho = f[0]
            for i in range(1, 19):
                rho = rho + f[i]
            fluid = solid_ref[y + HALO] < 0.5
            inverse = math.sqrt(3.0) / rho
            results = [rho * (1.0 / LIQUID)] + [c * inverse for c in moments(f)]
            for n, value in enumerate(results):
                done[n, pl.ds(y, subs, stride=sh.y), :] = jnp.where(fluid, value, 0.0)
            return 0

        lax.fori_loop(0, sh.y, finish, 0)

        lane = lax.broadcasted_iota(jnp.int32, (sh.y, LANES), 1)
        place = lane // sh.slab
        for slot, out in enumerate(outs):
            base = sh.peer(k, slot) * (sh.own * sh.y)
            for n in range(4):
                merged = None
                for x in range(sh.x):
                    m, g = divmod(x, sh.groups)
                    at = pl.multiple_of(base + m * sh.y, 8)
                    turn = (x * sh.slab - g * width - HALO) % LANES
                    value = done[n, pl.ds(at, sh.y), :]
                    value = pltpu.roll(value, turn, 1) if turn else value
                    merged = value if x == 0 else jnp.where(place == x, value, merged)
                out[n] = merged

    populations = pltpu.VMEM((19, rows, subs, LANES), jnp.float32)
    return pl.pallas_call(
        body,
        name="run_steps",
        out_shape=[jax.ShapeDtypeStruct((4, sh.y, LANES), jnp.float32)] * sh.nx,
        in_specs=vmem(3),
        out_specs=vmem(sh.nx),
        scratch_shapes=[
            pltpu.VMEM((5, subs * rows, LANES), jnp.float32),
            populations,
            populations,
            pltpu.VMEM((rows, subs, LANES), jnp.float32),
            pltpu.VMEM((rows, subs, LANES), jnp.float32),
            pltpu.VMEM((4, subs * sh.y, LANES), jnp.float32),
        ],
    )(below, middle, above)


def place_outputs(pieces, sh):
    def body(*refs):
        ins, (density, velocity) = refs[: sh.nx], refs[sh.nx :]
        k = lax.axis_index("gx")
        lane = lax.broadcasted_iota(jnp.int32, (sh.y, LANES), 1)
        place = lane // sh.slab
        for n in range(4):
            for x in range(sh.x):
                merged = None
                for slot, ref in enumerate(ins):
                    q = sh.sender(k, slot)
                    turn = lax.rem((q - x) * sh.slab + LANES, LANES)
                    value = pltpu.roll(ref[n], turn, 1)
                    merged = value if slot == 0 else jnp.where(place == q, value, merged)
                if n == 0:
                    density[x] = merged
                else:
                    velocity[n - 1, x] = merged

    block = (sh.x, sh.y, sh.z)
    return pl.pallas_call(
        body,
        name="place_outputs",
        out_shape=[
            jax.ShapeDtypeStruct(block, jnp.float32),
            jax.ShapeDtypeStruct((3,) + block, jnp.float32),
        ],
        in_specs=vmem(sh.nx),
        out_specs=vmem(2),
    )(*pieces)


def ring(size, step):
    return [(i, (i + step) % size) for i in range(size)]


def solution(mesh):
    def on_device(density_scatter, initial_velocity, bubble_mask, wall_flags):
        sh = Shape(mesh, wall_flags.shape)
        values = gather_inputs(density_scatter, initial_velocity, bubble_mask, wall_flags)
        before = lax.ppermute(values, "gz", ring(sh.nz, 1))
        after = before if sh.nz == 2 else lax.ppermute(values, "gz", ring(sh.nz, -1))
        slabs = cut_slabs(values, before, after, sh)
        got = [slabs[0]]
        for slot in range(1, sh.nx):
            got.append(lax.ppermute(slabs[slot], "gx", sh.perm(slot)))
        middle = jnp.stack(got)
        below = lax.ppermute(middle, "gy", ring(sh.ny, 1))
        above = lax.ppermute(middle, "gy", ring(sh.ny, -1))
        pieces = run_steps(below, middle, above, sh)
        back = [pieces[0]]
        for slot in range(1, sh.nx):
            back.append(lax.ppermute(pieces[slot], "gx", sh.perm(slot)))
        return tuple(place_outputs(back, sh))

    in_specs = (
        P("gx", "gy", "gz"),
        P(None, "gx", "gy", "gz"),
        P("gx", "gy", "gz"),
        P("gx", "gy", "gz"),
    )
    out_specs = (P("gx", "gy", "gz"), P(None, "gx", "gy", "gz"))
    return jax.shard_map(
        on_device, mesh=mesh, in_specs=in_specs, out_specs=out_specs, check_vma=False
    )
```

```python
import math

import jax
import jax.numpy as jnp
import numpy as np
from jax import lax
from jax.experimental import pallas as pl
from jax.experimental.pallas import tpu as pltpu
from jax.sharding import PartitionSpec as P

STEPS = 4
HALO = 2 * STEPS
LANES = 128

C = np.array(
    [
        [0, 0, 0],
        [1, 0, 0],
        [-1, 0, 0],
        [0, 1, 0],
        [0, -1, 0],
        [0, 0, 1],
        [0, 0, -1],
        [1, 1, 0],
        [-1, -1, 0],
        [1, -1, 0],
        [-1, 1, 0],
        [1, 0, 1],
        [-1, 0, -1],
        [1, 0, -1],
        [-1, 0, 1],
        [0, 1, 1],
        [0, -1, -1],
        [0, 1, -1],
        [0, -1, 1],
    ]
)
WEIGHTS = [1.0 / 3.0] + [1.0 / 18.0] * 6 + [1.0 / 36.0] * 12
OPPOSITE = [0, 2, 1, 4, 3, 6, 5, 8, 7, 10, 9, 12, 11, 14, 13, 16, 15, 18, 17]
LIQUID = 0.28
VAPOUR = 0.06
WALL_POTENTIAL = 0.5
ATTRACTION = 1.0
TEMPERATURE = 0.06

KEEP_E = 1.0 - 1.19
KEEP_P = 1.0 - 1.4
KEEP_Q = 1.0 - 1.2
KEEP_N = 1.0 - 1.25
KEEP_M = 1.0 - 1.98


def equilibrium(rho, u):
    rest = 1.0 - 1.5 * (u[0] * u[0] + u[1] * u[1] + u[2] * u[2])
    scaled = [None] * 3
    scaled[0] = rho * WEIGHTS[0]
    scaled[1] = rho * WEIGHTS[1]
    scaled[2] = rho * WEIGHTS[7]
    rows = [scaled[0] * rest]
    for i in range(1, 19, 2):
        terms = [u[k] if C[i, k] > 0 else -u[k] for k in range(3) if C[i, k] != 0]
        along = terms[0] if len(terms) == 1 else terms[0] + terms[1]
        even = rest + 4.5 * (along * along)
        odd = 3.0 * along
        w = scaled[len(terms)]
        rows += [w * (even + odd), w * (even - odd)]
    return rows


def potential(rho, solid):
    square = rho * rho
    gap = 1.0 - rho
    pressure = (
        rho * TEMPERATURE * (1.0 + rho + square - square * rho) / (gap * gap * gap)
        - ATTRACTION * square
    )
    return jnp.where(solid, WALL_POTENTIAL, jnp.sqrt(6.0 * (rho * (1.0 / 3.0) - pressure)))


def moments(f):
    d = [None] + [f[i] - f[i + 1] for i in range(1, 19, 2)]
    jx = d[1] + ((d[4] + d[5]) + (d[6] + d[7]))
    jy = d[2] + ((d[4] - d[5]) + (d[8] + d[9]))
    jz = d[3] + ((d[6] - d[7]) + (d[8] - d[9]))
    return jx, jy, jz


def collide(f, force, solid):
    s = [None] + [f[i] + f[i + 1] for i in range(1, 19, 2)]
    d = [None] + [f[i] - f[i + 1] for i in range(1, 19, 2)]
    xy, xz, yz = s[4] + s[5], s[6] + s[7], s[8] + s[9]
    axes = s[1] + s[2] + s[3]
    diagonals = xy + xz + yz
    rho = f[0] + axes + diagonals
    p_xy, q_xy = d[4] + d[5], d[4] - d[5]
    p_xz, q_xz = d[6] + d[7], d[6] - d[7]
    p_yz, q_yz = d[8] + d[9], d[8] - d[9]
    j = [d[1] + (p_xy + p_xz), d[2] + (q_xy + p_yz), d[3] + (q_xz + q_yz)]
    inverse = 1.0 / rho
    u = [j[k] * inverse for k in range(3)]
    moved = [j[k] + force[k] for k in range(3)]
    v = [moved[k] * inverse for k in range(3)]
    uu = [j[k] * u[k] for k in range(3)]
    vv = [moved[k] * v[k] for k in range(3)]
    u2 = uu[0] + uu[1] + uu[2]
    v2 = vv[0] + vv[1] + vv[2]

    energy = (
        KEEP_E * (8.0 * diagonals - 11.0 * axes - 30.0 * f[0])
        - (11.0 * (1.0 - KEEP_E)) * rho
        + 19.0 * (v2 - KEEP_E * u2)
    )
    epsilon = (
        KEEP_P * (12.0 * f[0] - 4.0 * axes + diagonals)
        + (3.0 * (1.0 - KEEP_P)) * rho
        - 5.5 * (v2 - KEEP_P * u2)
    )
    mass = rho * (1.0 / 19.0)
    even_rest = mass - (30.0 / 2394.0) * energy + (12.0 / 252.0) * epsilon
    even_axis = mass - (11.0 / 2394.0) * energy - (4.0 / 252.0) * epsilon
    even_diag = mass + (8.0 / 2394.0) * energy + (1.0 / 252.0) * epsilon

    def stress(a, b, at_v, at_u, scale):
        on_axis = (
            ((KEEP_N + 2.0 * KEEP_P) * scale) * a
            + ((KEEP_N - KEEP_P) * scale) * b
            + (1.5 * scale) * at_v
            - ((KEEP_N + 0.5 * KEEP_P) * scale) * at_u
        )
        half = 0.5 * scale
        on_diagonal = (
            ((2.0 * KEEP_N - 2.0 * KEEP_P) * half) * a
            + ((2.0 * KEEP_N + KEEP_P) * half) * b
            + (1.5 * half) * at_v
            - ((2.0 * KEEP_N - 0.5 * KEEP_P) * half) * at_u
        )
        return on_axis, on_diagonal

    h, g = stress(
        3.0 * s[1] - axes,
        diagonals - 3.0 * yz,
        3.0 * vv[0] - v2,
        3.0 * uu[0] - u2,
        1.0 / 36.0,
    )
    k, l = stress(s[2] - s[3], xy - xz, vv[1] - vv[2], uu[1] - uu[2], 1.0 / 12.0)

    def shear(a, b, pair):
        return (0.25 * KEEP_N) * (pair - j[a] * u[b]) + 0.25 * (moved[a] * v[b])

    t_xy = shear(0, 1, s[4] - s[5])
    t_xz = shear(0, 2, s[6] - s[7])
    t_yz = shear(1, 2, s[8] - s[9])

    flux_j = KEEP_Q * 5.0 / 3.0 - 2.0 / 3.0
    axis_odd = [
        ((1.0 - flux_j) / 10.0) * j[n] + (0.5 * KEEP_Q) * d[n + 1] + (1.0 / 6.0) * force[n]
        for n in range(3)
    ]
    diag_odd = [
        (0.1 + flux_j / 40.0) * j[n] - (KEEP_Q / 8.0) * d[n + 1] + (1.0 / 12.0) * force[n]
        for n in range(3)
    ]
    third = KEEP_M / 8.0
    mx, my, mz = third * (p_xy - p_xz), third * (p_yz - q_xy), third * (q_xz - q_yz)

    twist = even_axis - h
    evens = [even_axis + 2.0 * h, twist + k, twist - k]
    ring = even_diag + g
    e_xy, e_xz, e_yz = ring + l, ring - l, even_diag - 2.0 * g
    a, b = diag_odd[0] + mx, diag_odd[1] - my
    odd_xy = (a + b, a - b)
    a, b = diag_odd[0] - mx, diag_odd[2] + mz
    odd_xz = (a + b, a - b)
    a, b = diag_odd[1] + my, diag_odd[2] - mz
    odd_yz = (a + b, a - b)

    post = [even_rest]
    for n in range(3):
        post += [evens[n] + axis_odd[n], evens[n] - axis_odd[n]]
    for even, t, odd in ((e_xy, t_xy, odd_xy), (e_xz, t_xz, odd_xz), (e_yz, t_yz, odd_yz)):
        same, cross = even + t, even - t
        post += [same + odd[0], same - odd[0], cross + odd[1], cross - odd[1]]
    return [jnp.where(solid, f[OPPOSITE[i]], post[i]) for i in range(19)]


class Shape:
    def __init__(self, mesh, block):
        self.nx, self.ny, self.nz = (mesh.shape[a] for a in ("gx", "gy", "gz"))
        self.x, self.y, self.z = block
        self.slab = self.z // self.nx
        width = 1
        while width < self.slab + 2 * HALO:
            width *= 2
        self.width = width
        self.groups = LANES // width
        self.own = self.x // self.groups
        self.subs = self.x * self.nx // self.groups
        self.rows = self.y + 2 * HALO
        assert self.z == LANES and self.slab * self.nx == self.z and width <= LANES
        assert self.y == HALO and self.own * self.groups == self.x
        assert self.subs % 8 == 0 and self.slab * self.x <= LANES
        if self.nx & (self.nx - 1) == 0:
            self.peer = lambda k, slot: jnp.bitwise_xor(k, slot)
            self.perm = lambda slot: [(i, i ^ slot) for i in range(self.nx)]
            self.sender = self.peer
        else:
            self.peer = lambda k, slot: lax.rem(k + slot, self.nx)
            self.sender = lambda k, slot: lax.rem(k + self.nx - slot, self.nx)
            self.perm = lambda slot: [(i, (i + slot) % self.nx) for i in range(self.nx)]


def vmem(n):
    return [pl.BlockSpec(memory_space=pltpu.VMEM)] * n


def grant(words):
    return pltpu.CompilerParams(vmem_limit_bytes=(words * 4 * 5) // 4 + (1 << 20))


def join_slots(parts):
    def body(*refs):
        for n, ref in enumerate(refs[:-1]):
            refs[-1][n] = ref[...]

    block = parts[0].shape
    return pl.pallas_call(
        body,
        name="join_slots",
        out_shape=jax.ShapeDtypeStruct((len(parts),) + block, jnp.float32),
        in_specs=vmem(len(parts)),
        out_specs=vmem(1)[0],
        compiler_params=grant(2 * len(parts) * math.prod(block)),
    )(*parts)


def gather_inputs(scatter, velocity, bubbles, walls):
    def body(s_ref, u_ref, b_ref, w_ref, out):
        out[0] = jnp.where(b_ref[...] == 1, VAPOUR, LIQUID) * s_ref[...]
        for k in range(3):
            out[1 + k] = u_ref[k]
        out[4] = jnp.where(w_ref[...] == 1, 1.0, 0.0)

    return pl.pallas_call(
        body,
        name="pack_inputs",
        out_shape=jax.ShapeDtypeStruct((5,) + scatter.shape, jnp.float32),
        in_specs=vmem(4),
        out_specs=vmem(1)[0],
        compiler_params=grant(11 * math.prod(scatter.shape)),
    )(scatter, velocity, bubbles, walls)


def cut_slabs(values, before, after, sh):
    def body(v_ref, b_ref, a_ref, *outs):
        k = lax.axis_index("gx")
        lane = lax.broadcasted_iota(jnp.int32, (sh.y, LANES), 1)
        group = lane // sh.width
        for slot, out in enumerate(outs):
            q = sh.peer(k, slot)
            low = (lane >= LANES - HALO) & (q == 0)
            high = (lane < HALO) & (q == sh.nx - 1)
            start = HALO - q * sh.slab + 2 * LANES
            for n in range(5):
                for m in range(sh.own):
                    merged = None
                    for g in range(sh.groups):
                        x = m * sh.groups + g
                        plane = jnp.where(low, b_ref[n, x], v_ref[n, x])
                        plane = jnp.where(high, a_ref[n, x], plane)
                        plane = pltpu.roll(plane, lax.rem(start + g * sh.width, LANES), 1)
                        merged = plane if g == 0 else jnp.where(group == g, plane, merged)
                    out[n, m] = merged

    return pl.pallas_call(
        body,
        name="cut_slabs",
        out_shape=[jax.ShapeDtypeStruct((5, sh.own, sh.y, LANES), jnp.float32)] * sh.nx,
        in_specs=vmem(3),
        out_specs=vmem(sh.nx),
        compiler_params=grant((15 + 20) * math.prod(values.shape)),
    )(values, before, after)


def run_steps(below, middle, above, sh):
    rows, subs, width = sh.rows, sh.subs, sh.width

    def body(b_ref, m_ref, a_ref, *rest):
        outs = rest[: sh.nx]
        raw, first, second, psi_ref, solid_ref, done = rest[sh.nx :]
        k = lax.axis_index("gx")
        lane = lax.broadcasted_iota(jnp.int32, (subs, LANES), 1)
        group = lane // width

        for slot in range(sh.nx):
            base = sh.sender(k, slot) * (sh.own * rows)
            for part, ref in enumerate((b_ref, m_ref, a_ref)):
                for n in range(5):
                    for m in range(sh.own):
                        at = pl.multiple_of(base + m * rows + part * sh.y, 8)
                        raw[n, pl.ds(at, sh.y), :] = ref[slot, n, m]

        def shifted(value, cx, cz):
            if cx == 1:
                turned = pltpu.roll(value, 1, 0)
                value = jnp.where(group == sh.groups - 1, turned, value)
            if cx == -1:
                turned = pltpu.roll(value, subs - 1, 0)
                value = jnp.where(group == 0, turned, value)
            turn = (cx * width + cz) % LANES
            return pltpu.roll(value, turn, 1) if turn else value

        def start(y, _):
            read = lambda n: raw[n, pl.ds(y, subs, stride=rows), :]
            rho, u = read(0), [read(1), read(2), read(3)]
            solid_ref[y] = read(4)
            for i, row in enumerate(equilibrium(rho, u)):
                first[i, y] = row
            return 0

        lax.fori_loop(0, rows, start, 0)

        source, target = first, second
        for step in range(STEPS):

            def weigh(y, source=source):
                rho = source[0, y]
                for i in range(1, 19):
                    rho = rho + source[i, y]
                psi_ref[y] = potential(rho, solid_ref[y] > 0.5)

            def advance(y, source=source, target=target):
                here, up, down = psi_ref[y], psi_ref[y + 1], psi_ref[y - 1]
                both, rise = up + down, up - down
                doubled = 2.0 * here + both
                z_sum = doubled + (shifted(here, 0, -1) + shifted(here, 0, 1))
                x_sum = doubled + (shifted(here, -1, 0) + shifted(here, 1, 0))
                scale = here * (1.0 / 36.0)
                force = [
                    scale * (shifted(z_sum, -1, 0) - shifted(z_sum, 1, 0)),
                    scale
                    * (
                        2.0 * rise
                        + (shifted(rise, -1, 0) + shifted(rise, 1, 0))
                        + (shifted(rise, 0, -1) + shifted(rise, 0, 1))
                    ),
                    scale * (shifted(x_sum, 0, -1) - shifted(x_sum, 0, 1)),
                ]
                f = [source[i, y] for i in range(19)]
                post = collide(f, force, solid_ref[y] > 0.5)
                for i in range(19):
                    cx, cy, cz = (int(c) for c in C[i])
                    target[i, y + cy] = shifted(post[i], cx, cz)

            lo = 2 * step

            def weigh_some(n, _):
                for r in range(4):
                    weigh(lo + 4 * n + r)
                return 0

            def advance_some(n, _):
                for r in range(2):
                    advance(lo + 1 + 2 * n + r)
                return 0

            lax.fori_loop(0, (rows - 2 * lo) // 4, weigh_some, 0)
            lax.fori_loop(0, (rows - 2 * lo - 2) // 2, advance_some, 0)
            source, target = target, source

        def finish(y, _):
            f = [source[i, y + HALO] for i in range(19)]
            rho = f[0]
            for i in range(1, 19):
                rho = rho + f[i]
            fluid = solid_ref[y + HALO] < 0.5
            inverse = math.sqrt(3.0) / rho
            results = [rho * (1.0 / LIQUID)] + [c * inverse for c in moments(f)]
            for n, value in enumerate(results):
                done[n, pl.ds(y, subs, stride=sh.y), :] = jnp.where(fluid, value, 0.0)
            return 0

        lax.fori_loop(0, sh.y, finish, 0)

        lane = lax.broadcasted_iota(jnp.int32, (sh.y, LANES), 1)
        place = lane // sh.slab
        for slot, out in enumerate(outs):
            base = sh.peer(k, slot) * (sh.own * sh.y)
            for n in range(4):
                merged = None
                for x in range(sh.x):
                    m, g = divmod(x, sh.groups)
                    at = pl.multiple_of(base + m * sh.y, 8)
                    turn = (x * sh.slab - g * width - HALO) % LANES
                    value = done[n, pl.ds(at, sh.y), :]
                    value = pltpu.roll(value, turn, 1) if turn else value
                    merged = value if x == 0 else jnp.where(place == x, value, merged)
                out[n] = merged

    populations = pltpu.VMEM((19, rows, subs, LANES), jnp.float32)
    return pl.pallas_call(
        body,
        name="run_steps",
        out_shape=[jax.ShapeDtypeStruct((4, sh.y, LANES), jnp.float32)] * sh.nx,
        in_specs=vmem(3),
        out_specs=vmem(sh.nx),
        scratch_shapes=[
            pltpu.VMEM((5, subs * rows, LANES), jnp.float32),
            populations,
            populations,
            pltpu.VMEM((rows, subs, LANES), jnp.float32),
            pltpu.VMEM((rows, subs, LANES), jnp.float32),
            pltpu.VMEM((4, subs * sh.y, LANES), jnp.float32),
        ],
        compiler_params=grant(
            (2 * 19 + 2) * math.prod(populations.shape[1:])
            + (5 * rows + 4 * sh.y) * subs * LANES
            + 3 * math.prod(middle.shape)
            + 4 * sh.nx * sh.y * LANES
        ),
    )(below, middle, above)


def place_outputs(pieces, sh):
    def body(*refs):
        ins, (density, velocity) = refs[: sh.nx], refs[sh.nx :]
        k = lax.axis_index("gx")
        lane = lax.broadcasted_iota(jnp.int32, (sh.y, LANES), 1)
        place = lane // sh.slab
        for n in range(4):
            for x in range(sh.x):
                merged = None
                for slot, ref in enumerate(ins):
                    q = sh.sender(k, slot)
                    turn = lax.rem((q - x) * sh.slab + LANES, LANES)
                    value = pltpu.roll(ref[n], turn, 1)
                    merged = value if slot == 0 else jnp.where(place == q, value, merged)
                if n == 0:
                    density[x] = merged
                else:
                    velocity[n - 1, x] = merged

    block = (sh.x, sh.y, sh.z)
    return pl.pallas_call(
        body,
        name="place_outputs",
        out_shape=[
            jax.ShapeDtypeStruct(block, jnp.float32),
            jax.ShapeDtypeStruct((3,) + block, jnp.float32),
        ],
        in_specs=vmem(sh.nx),
        out_specs=vmem(2),
        compiler_params=grant(8 * sh.nx * sh.y * LANES + 8 * math.prod(block)),
    )(*pieces)


def ring(size, step):
    return [(i, (i + step) % size) for i in range(size)]


def solution(mesh):
    def on_device(density_scatter, initial_velocity, bubble_mask, wall_flags):
        sh = Shape(mesh, wall_flags.shape)
        values = gather_inputs(density_scatter, initial_velocity, bubble_mask, wall_flags)
        before = lax.ppermute(values, "gz", ring(sh.nz, 1))
        after = before if sh.nz == 2 else lax.ppermute(values, "gz", ring(sh.nz, -1))
        slabs = cut_slabs(values, before, after, sh)
        got = [slabs[0]]
        for slot in range(1, sh.nx):
            got.append(lax.ppermute(slabs[slot], "gx", sh.perm(slot)))
        middle = join_slots(got)
        below = lax.ppermute(middle, "gy", ring(sh.ny, 1))
        above = lax.ppermute(middle, "gy", ring(sh.ny, -1))
        pieces = run_steps(below, middle, above, sh)
        back = [pieces[0]]
        for slot in range(1, sh.nx):
            back.append(lax.ppermute(pieces[slot], "gx", sh.perm(slot)))
        return tuple(place_outputs(back, sh))

    in_specs = (
        P("gx", "gy", "gz"),
        P(None, "gx", "gy", "gz"),
        P("gx", "gy", "gz"),
        P("gx", "gy", "gz"),
    )
    out_specs = (P("gx", "gy", "gz"), P(None, "gx", "gy", "gz"))
    return jax.shard_map(
        on_device, mesh=mesh, in_specs=in_specs, out_specs=out_specs, check_vma=False
    )
```

```python
import math

import jax
import jax.numpy as jnp
import numpy as np
from jax import lax
from jax.experimental import pallas as pl
from jax.experimental.pallas import tpu as pltpu
from jax.sharding import PartitionSpec as P

STEPS = 4
HALO = 2 * STEPS
LANES = 128

START_ROWS = 12
WEIGH_ROWS = 12
PAD = 2
PIPELINE = False


C = np.array(
    [
        [0, 0, 0],
        [1, 0, 0],
        [-1, 0, 0],
        [0, 1, 0],
        [0, -1, 0],
        [0, 0, 1],
        [0, 0, -1],
        [1, 1, 0],
        [-1, -1, 0],
        [1, -1, 0],
        [-1, 1, 0],
        [1, 0, 1],
        [-1, 0, -1],
        [1, 0, -1],
        [-1, 0, 1],
        [0, 1, 1],
        [0, -1, -1],
        [0, 1, -1],
        [0, -1, 1],
    ]
)
WEIGHTS = [1.0 / 3.0] + [1.0 / 18.0] * 6 + [1.0 / 36.0] * 12
OPPOSITE = [0, 2, 1, 4, 3, 6, 5, 8, 7, 10, 9, 12, 11, 14, 13, 16, 15, 18, 17]
MIRROR = [int(np.flatnonzero((C == c * [1, -1, 1]).all(1))[0]) for c in C]
LIQUID = 0.28
VAPOUR = 0.06
WALL_POTENTIAL = 0.5
ATTRACTION = 1.0
TEMPERATURE = 0.06

KEEP_E = 1.0 - 1.19
KEEP_P = 1.0 - 1.4
KEEP_Q = 1.0 - 1.2
KEEP_N = 1.0 - 1.25
KEEP_M = 1.0 - 1.98


def equilibrium(rho, u):
    rest = 1.0 - 1.5 * (u[0] * u[0] + u[1] * u[1] + u[2] * u[2])
    rows = [(rho * WEIGHTS[0]) * rest]
    scaled = [None, rho * WEIGHTS[1], rho * WEIGHTS[7]]
    still = [None] + [w * rest for w in scaled[1:]]
    triple = [None] + [3.0 * w for w in scaled[1:]]
    for i in range(1, 19, 2):
        terms = [u[k] if C[i, k] > 0 else -u[k] for k in range(3) if C[i, k] != 0]
        n = len(terms)
        along = terms[0] if n == 1 else terms[0] + terms[1]
        odd = triple[n] * along
        even = still[n] + (1.5 * odd) * along
        rows += [even + odd, even - odd]
    return rows


def potential(rho, solid):
    square = rho * rho
    gap = 1.0 - rho
    pressure = (
        rho * TEMPERATURE * (1.0 + rho + square - square * rho) / (gap * gap * gap)
        - ATTRACTION * square
    )
    return jnp.where(solid, WALL_POTENTIAL, jnp.sqrt(6.0 * (rho * (1.0 / 3.0) - pressure)))


def times(c, value):
    c = float(np.float32(c))
    return value if c == 1.0 else -value if c == -1.0 else c * value


def moments(f):
    d = [None] + [f[i] - f[i + 1] for i in range(1, 19, 2)]
    jx = d[1] + ((d[4] + d[5]) + (d[6] + d[7]))
    jy = d[2] + ((d[4] - d[5]) + (d[8] + d[9]))
    jz = d[3] + ((d[6] - d[7]) + (d[8] - d[9]))
    return jx, jy, jz


def collide(f, force, solid):
    s = [None] + [f[i] + f[i + 1] for i in range(1, 19, 2)]
    d = [None] + [f[i] - f[i + 1] for i in range(1, 19, 2)]
    xy, xz, yz = s[4] + s[5], s[6] + s[7], s[8] + s[9]
    axes = s[1] + s[2] + s[3]
    diagonals = xy + xz + yz
    rho = f[0] + axes + diagonals
    p_xy, q_xy = d[4] + d[5], d[4] - d[5]
    p_xz, q_xz = d[6] + d[7], d[6] - d[7]
    p_yz, q_yz = d[8] + d[9], d[8] - d[9]
    j = [d[1] + (p_xy + p_xz), d[2] + (q_xy + p_yz), d[3] + (q_xz + q_yz)]
    inverse = 1.0 / rho
    u = [j[k] * inverse for k in range(3)]
    moved = [j[k] + force[k] for k in range(3)]
    v = [moved[k] * inverse for k in range(3)]
    uu = [j[k] * u[k] for k in range(3)]
    vv = [moved[k] * v[k] for k in range(3)]
    u2 = uu[0] + uu[1] + uu[2]
    v2 = vv[0] + vv[1] + vv[2]

    def isotropic(of_energy, of_epsilon):
        parts = (
            (1.0 / 19.0 - of_energy * (11.0 + 19.0 * KEEP_E) + of_epsilon * (3.0 + 9.0 * KEEP_P), rho),
            (of_energy * 19.0 * KEEP_E - of_epsilon * 16.0 * KEEP_P, axes),
            (of_energy * 38.0 * KEEP_E - of_epsilon * 11.0 * KEEP_P, diagonals),
            (of_energy * 19.0 - of_epsilon * 5.5, v2),
            (-of_energy * 19.0 * KEEP_E + of_epsilon * 5.5 * KEEP_P, u2),
        )
        return sum((c * value for c, value in parts[1:]), parts[0][0] * parts[0][1])

    even_axis = isotropic(-11.0 / 2394.0, -4.0 / 252.0)
    even_diag = isotropic(8.0 / 2394.0, 1.0 / 252.0)
    even_rest = rho - 6.0 * even_axis - 12.0 * even_diag

    def stress(a, b, at_v, at_u, scale):
        on_axis = (
            ((KEEP_N + 2.0 * KEEP_P) * scale) * a
            + ((KEEP_N - KEEP_P) * scale) * b
            + (1.5 * scale) * at_v
            - ((KEEP_N + 0.5 * KEEP_P) * scale) * at_u
        )
        half = 0.5 * scale
        on_diagonal = (
            ((2.0 * KEEP_N - 2.0 * KEEP_P) * half) * a
            + ((2.0 * KEEP_N + KEEP_P) * half) * b
            + (1.5 * half) * at_v
            - ((2.0 * KEEP_N - 0.5 * KEEP_P) * half) * at_u
        )
        return on_axis, on_diagonal

    h, g = stress(
        3.0 * s[1] - axes,
        diagonals - 3.0 * yz,
        3.0 * vv[0] - v2,
        3.0 * uu[0] - u2,
        1.0 / 36.0,
    )
    k, l = stress(s[2] - s[3], xy - xz, vv[1] - vv[2], uu[1] - uu[2], 1.0 / 12.0)

    quarter = [None, 0.25 * v[1], 0.25 * v[2]]

    def shear(a, b, pair):
        return (0.25 * KEEP_N) * (pair - j[a] * u[b]) + moved[a] * quarter[b]

    t_xy = shear(0, 1, s[4] - s[5])
    t_xz = shear(0, 2, s[6] - s[7])
    t_yz = shear(1, 2, s[8] - s[9])

    flux = [
        times(-5.0 * KEEP_Q, d[n + 1])
        + (times(KEEP_Q * 5.0 / 3.0 - 2.0 / 3.0, moved[n]) - (KEEP_Q * 5.0 / 3.0) * force[n])
        for n in range(3)
    ]
    tenth = [0.1 * moved[n] for n in range(3)]
    axis_odd = [tenth[n] - 0.1 * flux[n] for n in range(3)]
    diag_odd = [tenth[n] + 0.025 * flux[n] for n in range(3)]
    third = KEEP_M / 8.0
    mx, my, mz = third * (p_xy - p_xz), third * (p_yz - q_xy), third * (q_xz - q_yz)

    twist = even_axis - h
    evens = [even_axis + 2.0 * h, twist + k, twist - k]
    ring = even_diag + g
    e_xy, e_xz, e_yz = ring + l, ring - l, even_diag - 2.0 * g
    a, b = diag_odd[0] + mx, diag_odd[1] - my
    odd_xy = (a + b, a - b)
    a, b = diag_odd[0] - mx, diag_odd[2] + mz
    odd_xz = (a + b, a - b)
    a, b = diag_odd[1] + my, diag_odd[2] - mz
    odd_yz = (a + b, a - b)

    post = [even_rest]
    for n in range(3):
        post += [evens[n] + axis_odd[n], evens[n] - axis_odd[n]]
    for even, t, odd in ((e_xy, t_xy, odd_xy), (e_xz, t_xz, odd_xz), (e_yz, t_yz, odd_yz)):
        same, cross = even + t, even - t
        post += [same + odd[0], same - odd[0], cross + odd[1], cross - odd[1]]
    return [jnp.where(solid, f[OPPOSITE[i]], post[i]) for i in range(19)]


class Shape:
    def __init__(self, mesh, block):
        self.nx, self.ny, self.nz = (mesh.shape[a] for a in ("gx", "gy", "gz"))
        self.x, self.y, self.z = block
        self.slab = self.z // self.nx
        self.width = LANES // 2
        self.groups = 2
        self.own = self.x // self.groups
        self.subs = self.x * self.nx // self.groups
        self.rows = self.y + 2 * HALO
        assert self.z == LANES and self.slab * self.nx == self.z
        assert self.slab + 2 * HALO <= self.width and 2 * self.slab <= self.width
        assert self.y == HALO and self.own * self.groups == self.x
        assert self.subs % 8 == 0
        if self.nx & (self.nx - 1) == 0:
            self.peer = lambda k, slot: jnp.bitwise_xor(k, slot)
            self.perm = lambda slot: [(i, i ^ slot) for i in range(self.nx)]
            self.sender = self.peer
        else:
            self.peer = lambda k, slot: lax.rem(k + slot, self.nx)
            self.sender = lambda k, slot: lax.rem(k + self.nx - slot, self.nx)
            self.perm = lambda slot: [(i, (i + slot) % self.nx) for i in range(self.nx)]


def vmem(n):
    return [pl.BlockSpec(memory_space=pltpu.VMEM)] * n


def grant(words):
    return pltpu.CompilerParams(vmem_limit_bytes=(words * 4 * 5) // 4 + (1 << 20))


def join_slots(parts):
    def body(*refs):
        for n, ref in enumerate(refs[:-1]):
            refs[-1][n] = ref[...]

    block = parts[0].shape
    return pl.pallas_call(
        body,
        name="join_slots",
        out_shape=jax.ShapeDtypeStruct((len(parts),) + block, jnp.float32),
        in_specs=vmem(len(parts)),
        out_specs=vmem(1)[0],
        compiler_params=grant(2 * len(parts) * math.prod(block)),
    )(*parts)


def gather_inputs(scatter, velocity, bubbles, walls):
    rho = jnp.where(bubbles == 1, VAPOUR, LIQUID) * scatter
    solid = jnp.where(walls == 1, 1.0, 0.0)
    return jnp.concatenate([rho[None], velocity, solid[None]])


def cut_slabs(values, before, after, sh):
    def body(v_ref, b_ref, a_ref, *outs):
        k = lax.axis_index("gx")
        lane = lax.broadcasted_iota(jnp.int32, (sh.y, LANES), 1)
        group = lane // sh.width
        for slot, out in enumerate(outs):
            q = sh.peer(k, slot)
            low = (lane >= LANES - HALO) & (q == 0)
            high = (lane < HALO) & (q == sh.nx - 1)
            start = HALO - q * sh.slab + 2 * LANES
            for n in range(5):
                for m in range(sh.own):
                    merged = None
                    for g in range(sh.groups):
                        x = m * sh.groups + g
                        plane = jnp.where(low, b_ref[n, x], v_ref[n, x])
                        plane = jnp.where(high, a_ref[n, x], plane)
                        plane = pltpu.roll(plane, lax.rem(start + g * sh.width, LANES), 1)
                        merged = plane if g == 0 else jnp.where(group == g, plane, merged)
                    out[n, m] = merged

    return pl.pallas_call(
        body,
        name="cut_slabs",
        out_shape=[jax.ShapeDtypeStruct((5, sh.own, sh.y, LANES), jnp.float32)] * sh.nx,
        in_specs=vmem(3),
        out_specs=vmem(sh.nx),
        compiler_params=grant((15 + 20) * math.prod(values.shape)),
    )(values, before, after)


def run_steps(below, middle, above, sh):
    half, subs = sh.rows // 2, sh.subs
    last = PAD + half - 1

    def body(b_ref, m_ref, a_ref, *rest):
        outs = rest[: sh.nx]
        raw, first, second, psi_ref, solid_ref, force_ref, post_ref, done = rest[sh.nx :]
        k = lax.axis_index("gx")
        lane = lax.broadcasted_iota(jnp.int32, (subs, LANES), 1)
        low = lane < sh.width

        for slot in range(sh.nx):
            base = sh.sender(k, slot) * (sh.own * sh.rows)
            for part, ref in enumerate((b_ref, m_ref, a_ref)):
                for n in range(5):
                    for m in range(sh.own):
                        at = pl.multiple_of(base + m * sh.rows + part * sh.y, 8)
                        raw[n, pl.ds(at, sh.y), :] = ref[slot, n, m]

        def along_x(pair, cx):
            if cx == 1:
                return pltpu.roll(pair[1], 1, 0), pair[0]
            if cx == -1:
                return pair[1], pltpu.roll(pair[0], subs - 1, 0)
            return pair

        def along_z(value, cz):
            return pltpu.roll(value, cz % LANES, 1) if cz % LANES else value

        def over(count, at_once, step):
            at_once = min(at_once, count)
            while count % at_once:
                at_once -= 1

            def trip(n, _):
                for r in range(at_once):
                    step(n * at_once + r)
                return 0

            if count == at_once:
                trip(0, 0)
            else:
                lax.fori_loop(0, count // at_once, trip, 0)

        def weigh(f, y, p):
            psi_ref[p, y] = potential(sum(f[1:], f[0]), solid_ref[p, y] > 0.5)

        def reflect():
            for p in range(2):
                psi_ref[p, last + 1] = pltpu.roll(psi_ref[p, last], sh.width, 1)

        def start(n):
            y = PAD + n
            pairs = []
            for v in range(5):
                near = raw[v, pl.ds(n, subs, stride=sh.rows), :]
                far = raw[v, pl.ds(sh.rows - 1 - n, subs, stride=sh.rows), :]
                far = -far if v == 2 else far
                even = jnp.where(low, near, pltpu.roll(far, sh.width, 1))
                odd = jnp.where(low, pltpu.roll(near, sh.width, 1), far)
                pairs.append((even, odd))
            for p in range(2):
                rho, ux, uy, uz, solid = (pair[p] for pair in pairs)
                f = equilibrium(rho, [ux, uy, uz])
                solid_ref[p, y] = solid
                for i in range(19):
                    first[i, p, y] = f[i]
                weigh(f, y, p)

        over(half, START_ROWS, start)

        source, target = first, second
        for step in range(STEPS):
            lo = PAD + 2 * step
            if step > 0:

                def weigh_again(n, source=source, lo=lo):
                    for p in range(2):
                        weigh([source[i, p, lo + n] for i in range(19)], lo + n, p)

                over(half - 2 * step, WEIGH_ROWS, weigh_again)
            reflect()

            def push(y):
                here, up, down = (
                    [psi_ref[p, at] for p in range(2)] for at in (y, y + 1, y - 1)
                )
                rise = [up[p] - down[p] for p in range(2)]
                doubled = [2.0 * here[p] + (up[p] + down[p]) for p in range(2)]
                before, after = along_x(here, 1), along_x(here, -1)
                rise_x = [a + b for a, b in zip(along_x(rise, 1), along_x(rise, -1))]
                z_sum = [
                    doubled[p] + (along_z(here[p], 1) + along_z(here[p], -1)) for p in range(2)
                ]
                x_sum = [doubled[p] + (before[p] + after[p]) for p in range(2)]
                fx = [a - b for a, b in zip(along_x(z_sum, -1), along_x(z_sum, 1))]
                for p in range(2):
                    fy = (2.0 * rise[p] + rise_x[p]) + (
                        along_z(rise[p], 1) + along_z(rise[p], -1)
                    )
                    fz = along_z(x_sum[p], -1) - along_z(x_sum[p], 1)
                    scale = here[p] * (1.0 / 36.0)
                    for n, value in enumerate((fx[p], fy, fz)):
                        force_ref[n, p, y] = scale * value

            def stream(posts, y, at_end, target=target):
                for i in range(19):
                    cx, cy, cz = (int(c) for c in C[i])
                    to, row = i, y + cy
                    if at_end and cy == 1:
                        to, row, cz = MIRROR[i], y, cz + sh.width
                    for p, value in enumerate(along_x(posts[i], cx)):
                        target[to, p, row] = along_z(value, cz)

            def settle(y, p, forces, source=source):
                f = [source[i, p, y] for i in range(19)]
                return collide(f, forces, solid_ref[p, y] > 0.5)

            def load_forces(y):
                return [[force_ref[n, p, y] for n in range(3)] for p in range(2)]

            def load_posts():
                return [[post_ref[i, p] for p in range(2)] for i in range(19)]

            rows = half - 1 - 2 * step
            if PIPELINE:

                def advance(n, _, lo=lo, push=push, stream=stream, settle=settle):
                    y = lo + 1 + n
                    forces = load_forces(y)
                    stream(load_posts(), y - 1, False)
                    push(y + 1)
                    for p in range(2):
                        post = settle(y, p, forces[p])
                        for i in range(19):
                            post_ref[i, p] = post[i]
                    return 0

                push(lo + 1)
                lax.fori_loop(0, rows, advance, 0)
                stream(load_posts(), last, True)
            else:

                def advance(n, _, lo=lo, push=push, stream=stream, settle=settle):
                    y = lo + 1 + n
                    forces = load_forces(y)
                    push(y + 1)
                    both = [settle(y, p, forces[p]) for p in range(2)]
                    stream(list(zip(*both)), y, False)
                    return 0

                push(lo + 1)
                lax.fori_loop(0, rows - 1, advance, 0)
                forces = load_forces(last)
                both = [settle(last, p, forces[p]) for p in range(2)]
                stream(list(zip(*both)), last, True)
            source, target = target, source

        quarter = sh.y // 2
        for n in range(quarter):
            y = PAD + HALO + n
            for p in range(2):
                f = [source[i, p, y] for i in range(19)]
                rho = sum(f[1:], f[0])
                fluid = solid_ref[p, y] < 0.5
                jx, jy, jz = moments(f)
                inverse = math.sqrt(3.0) / rho
                results = [rho * (1.0 / LIQUID), jx * inverse, jy * inverse, jz * inverse]
                for v, value in enumerate(results):
                    value = jnp.where(fluid, value, 0.0)
                    done[0, v, p, pl.ds(n, subs, stride=quarter), :] = value
                    value = -value if v == 2 else value
                    done[1, v, p, pl.ds(quarter - 1 - n, subs, stride=quarter), :] = value

        size = sh.own * quarter
        lane = lax.broadcasted_iota(jnp.int32, (size, LANES), 1)
        high = lane >= sh.width
        odd = (lane % sh.width) >= sh.slab
        for slot, out in enumerate(outs):
            at = pl.ds(pl.multiple_of(sh.peer(k, slot) * size, size), size)
            for v in range(4):
                even_odd = [
                    jnp.where(high, done[1, v, p, at, :], done[0, v, p, at, :]) for p in range(2)
                ]
                out[v] = jnp.where(
                    odd,
                    along_z(even_odd[1], sh.slab - HALO),
                    along_z(even_odd[0], -HALO),
                )

    padded = half + 2 * PAD
    row = (2, padded, subs, LANES)
    scratch = [
        (5, subs * sh.rows, LANES),
        (19,) + row,
        (19,) + row,
        row,
        row,
        (3,) + row,
        (19, 2, subs, LANES),
        (2, 4, 2, subs * sh.y // 2, LANES),
    ]
    piece = (4, sh.own * sh.y // 2, LANES)
    words = sum(math.prod(shape) for shape in scratch)
    return pl.pallas_call(
        body,
        name="run_steps",
        out_shape=[jax.ShapeDtypeStruct(piece, jnp.float32)] * sh.nx,
        in_specs=vmem(3),
        out_specs=vmem(sh.nx),
        scratch_shapes=[pltpu.VMEM(shape, jnp.float32) for shape in scratch],
        compiler_params=grant(words + 3 * math.prod(middle.shape) + sh.nx * math.prod(piece)),
    )(below, middle, above)


def place_outputs(pieces, sh):
    quarter = sh.y // 2
    size = sh.own * quarter

    def body(*refs):
        ins, (density, velocity) = refs[: sh.nx], refs[sh.nx :]
        k = lax.axis_index("gx")
        place = lax.broadcasted_iota(jnp.int32, (size, LANES), 1) // sh.slab
        upper = lax.broadcasted_iota(jnp.int32, (sh.y, LANES), 0) < quarter
        for v in range(4):
            for p in range(2):
                halves = []
                for g in range(2):
                    merged = None
                    for slot, ref in enumerate(ins):
                        q = sh.sender(k, slot)
                        turn = q * sh.slab - g * sh.width - p * sh.slab + 2 * LANES
                        value = pltpu.roll(ref[v], lax.rem(turn, LANES), 1)
                        merged = value if slot == 0 else jnp.where(place == q, value, merged)
                    halves.append(merged)
                for m in range(sh.own):
                    to = density.at[2 * m + p] if v == 0 else velocity.at[v - 1, 2 * m + p]
                    for g in range(2):
                        to[g * quarter : (g + 1) * quarter, :] = halves[g][
                            m * quarter : (m + 1) * quarter
                        ]

    block = (sh.x, sh.y, sh.z)
    return pl.pallas_call(
        body,
        name="place_outputs",
        out_shape=[
            jax.ShapeDtypeStruct(block, jnp.float32),
            jax.ShapeDtypeStruct((3,) + block, jnp.float32),
        ],
        in_specs=vmem(sh.nx),
        out_specs=vmem(2),
        compiler_params=grant(8 * sh.nx * sh.y * LANES + 8 * math.prod(block)),
    )(*pieces)


def ring(size, step):
    return [(i, (i + step) % size) for i in range(size)]


def solution(mesh):
    def on_device(density_scatter, initial_velocity, bubble_mask, wall_flags):
        sh = Shape(mesh, wall_flags.shape)
        values = gather_inputs(density_scatter, initial_velocity, bubble_mask, wall_flags)
        before = lax.ppermute(values, "gz", ring(sh.nz, 1))
        after = before if sh.nz == 2 else lax.ppermute(values, "gz", ring(sh.nz, -1))
        slabs = cut_slabs(values, before, after, sh)
        got = [slabs[0]]
        for slot in range(1, sh.nx):
            got.append(lax.ppermute(slabs[slot], "gx", sh.perm(slot)))
        middle = join_slots(got)
        below = lax.ppermute(middle, "gy", ring(sh.ny, 1))
        above = lax.ppermute(middle, "gy", ring(sh.ny, -1))
        pieces = run_steps(below, middle, above, sh)
        back = [pieces[0]]
        for slot in range(1, sh.nx):
            back.append(lax.ppermute(pieces[slot], "gx", sh.perm(slot)))
        return tuple(place_outputs(back, sh))

    in_specs = (
        P("gx", "gy", "gz"),
        P(None, "gx", "gy", "gz"),
        P("gx", "gy", "gz"),
        P("gx", "gy", "gz"),
    )
    out_specs = (P("gx", "gy", "gz"), P(None, "gx", "gy", "gz"))
    return jax.shard_map(
        on_device, mesh=mesh, in_specs=in_specs, out_specs=out_specs, check_vma=False
    )
```

```python
import math

import jax
import jax.numpy as jnp
import numpy as np
from jax import lax
from jax.experimental import pallas as pl
from jax.experimental.pallas import tpu as pltpu
from jax.sharding import PartitionSpec as P

STEPS = 4
HALO = 2 * STEPS
LANES = 128

START_ROWS = 12
WEIGH_ROWS = 12
ADVANCE_ROWS = 12
AHEAD = 2
PAD = 2
ADVANCE_ROWS = 10
AHEAD = 2


C = np.array(
    [
        [0, 0, 0],
        [1, 0, 0],
        [-1, 0, 0],
        [0, 1, 0],
        [0, -1, 0],
        [0, 0, 1],
        [0, 0, -1],
        [1, 1, 0],
        [-1, -1, 0],
        [1, -1, 0],
        [-1, 1, 0],
        [1, 0, 1],
        [-1, 0, -1],
        [1, 0, -1],
        [-1, 0, 1],
        [0, 1, 1],
        [0, -1, -1],
        [0, 1, -1],
        [0, -1, 1],
    ]
)
WEIGHTS = [1.0 / 3.0] + [1.0 / 18.0] * 6 + [1.0 / 36.0] * 12
OPPOSITE = [0, 2, 1, 4, 3, 6, 5, 8, 7, 10, 9, 12, 11, 14, 13, 16, 15, 18, 17]
MIRROR = [int(np.flatnonzero((C == c * [1, -1, 1]).all(1))[0]) for c in C]
LIQUID = 0.28
VAPOUR = 0.06
WALL_POTENTIAL = 0.5
ATTRACTION = 1.0
TEMPERATURE = 0.06

KEEP_E = 1.0 - 1.19
KEEP_P = 1.0 - 1.4
KEEP_Q = 1.0 - 1.2
KEEP_N = 1.0 - 1.25
KEEP_M = 1.0 - 1.98


def equilibrium(rho, u):
    rest = 1.0 - 1.5 * (u[0] * u[0] + u[1] * u[1] + u[2] * u[2])
    rows = [(rho * WEIGHTS[0]) * rest]
    scaled = [None, rho * WEIGHTS[1], rho * WEIGHTS[7]]
    still = [None] + [w * rest for w in scaled[1:]]
    triple = [None] + [3.0 * w for w in scaled[1:]]
    for i in range(1, 19, 2):
        terms = [u[k] if C[i, k] > 0 else -u[k] for k in range(3) if C[i, k] != 0]
        n = len(terms)
        along = terms[0] if n == 1 else terms[0] + terms[1]
        odd = triple[n] * along
        even = still[n] + (1.5 * odd) * along
        rows += [even + odd, even - odd]
    return rows


def potential(rho, solid):
    square = rho * rho
    gap = 1.0 - rho
    pressure = (
        rho * TEMPERATURE * (1.0 + rho + square - square * rho) / (gap * gap * gap)
        - ATTRACTION * square
    )
    return jnp.where(solid, WALL_POTENTIAL, jnp.sqrt(6.0 * (rho * (1.0 / 3.0) - pressure)))


def times(c, value):
    c = float(np.float32(c))
    return value if c == 1.0 else -value if c == -1.0 else c * value


def moments(f):
    d = [None] + [f[i] - f[i + 1] for i in range(1, 19, 2)]
    jx = d[1] + ((d[4] + d[5]) + (d[6] + d[7]))
    jy = d[2] + ((d[4] - d[5]) + (d[8] + d[9]))
    jz = d[3] + ((d[6] - d[7]) + (d[8] - d[9]))
    return jx, jy, jz


def collide(f, force, solid):
    s = [None] + [f[i] + f[i + 1] for i in range(1, 19, 2)]
    d = [None] + [f[i] - f[i + 1] for i in range(1, 19, 2)]
    xy, xz, yz = s[4] + s[5], s[6] + s[7], s[8] + s[9]
    axes = s[1] + s[2] + s[3]
    diagonals = xy + xz + yz
    rho = f[0] + axes + diagonals
    p_xy, q_xy = d[4] + d[5], d[4] - d[5]
    p_xz, q_xz = d[6] + d[7], d[6] - d[7]
    p_yz, q_yz = d[8] + d[9], d[8] - d[9]
    j = [d[1] + (p_xy + p_xz), d[2] + (q_xy + p_yz), d[3] + (q_xz + q_yz)]
    inverse = 1.0 / rho
    u = [j[k] * inverse for k in range(3)]
    moved = [j[k] + force[k] for k in range(3)]
    v = [moved[k] * inverse for k in range(3)]
    uu = [j[k] * u[k] for k in range(3)]
    vv = [moved[k] * v[k] for k in range(3)]
    u2 = uu[0] + uu[1] + uu[2]
    v2 = vv[0] + vv[1] + vv[2]

    def isotropic(of_energy, of_epsilon):
        parts = (
            (1.0 / 19.0 - of_energy * (11.0 + 19.0 * KEEP_E) + of_epsilon * (3.0 + 9.0 * KEEP_P), rho),
            (of_energy * 19.0 * KEEP_E - of_epsilon * 16.0 * KEEP_P, axes),
            (of_energy * 38.0 * KEEP_E - of_epsilon * 11.0 * KEEP_P, diagonals),
            (of_energy * 19.0 - of_epsilon * 5.5, v2),
            (-of_energy * 19.0 * KEEP_E + of_epsilon * 5.5 * KEEP_P, u2),
        )
        return sum((c * value for c, value in parts[1:]), parts[0][0] * parts[0][1])

    even_axis = isotropic(-11.0 / 2394.0, -4.0 / 252.0)
    even_diag = isotropic(8.0 / 2394.0, 1.0 / 252.0)
    even_rest = rho - 6.0 * even_axis - 12.0 * even_diag

    def stress(a, b, at_v, at_u, scale):
        on_axis = (
            ((KEEP_N + 2.0 * KEEP_P) * scale) * a
            + ((KEEP_N - KEEP_P) * scale) * b
            + (1.5 * scale) * at_v
            - ((KEEP_N + 0.5 * KEEP_P) * scale) * at_u
        )
        half = 0.5 * scale
        on_diagonal = (
            ((2.0 * KEEP_N - 2.0 * KEEP_P) * half) * a
            + ((2.0 * KEEP_N + KEEP_P) * half) * b
            + (1.5 * half) * at_v
            - ((2.0 * KEEP_N - 0.5 * KEEP_P) * half) * at_u
        )
        return on_axis, on_diagonal

    h, g = stress(
        3.0 * s[1] - axes,
        diagonals - 3.0 * yz,
        3.0 * vv[0] - v2,
        3.0 * uu[0] - u2,
        1.0 / 36.0,
    )
    k, l = stress(s[2] - s[3], xy - xz, vv[1] - vv[2], uu[1] - uu[2], 1.0 / 12.0)

    quarter = [None, 0.25 * v[1], 0.25 * v[2]]

    def shear(a, b, pair):
        return (0.25 * KEEP_N) * (pair - j[a] * u[b]) + moved[a] * quarter[b]

    t_xy = shear(0, 1, s[4] - s[5])
    t_xz = shear(0, 2, s[6] - s[7])
    t_yz = shear(1, 2, s[8] - s[9])

    flux = [
        times(-5.0 * KEEP_Q, d[n + 1])
        + (times(KEEP_Q * 5.0 / 3.0 - 2.0 / 3.0, moved[n]) - (KEEP_Q * 5.0 / 3.0) * force[n])
        for n in range(3)
    ]
    tenth = [0.1 * moved[n] for n in range(3)]
    axis_odd = [tenth[n] - 0.1 * flux[n] for n in range(3)]
    diag_odd = [tenth[n] + 0.025 * flux[n] for n in range(3)]
    third = KEEP_M / 8.0
    mx, my, mz = third * (p_xy - p_xz), third * (p_yz - q_xy), third * (q_xz - q_yz)

    twist = even_axis - h
    evens = [even_axis + 2.0 * h, twist + k, twist - k]
    ring = even_diag + g
    e_xy, e_xz, e_yz = ring + l, ring - l, even_diag - 2.0 * g
    a, b = diag_odd[0] + mx, diag_odd[1] - my
    odd_xy = (a + b, a - b)
    a, b = diag_odd[0] - mx, diag_odd[2] + mz
    odd_xz = (a + b, a - b)
    a, b = diag_odd[1] + my, diag_odd[2] - mz
    odd_yz = (a + b, a - b)

    post = [even_rest]
    for n in range(3):
        post += [evens[n] + axis_odd[n], evens[n] - axis_odd[n]]
    for even, t, odd in ((e_xy, t_xy, odd_xy), (e_xz, t_xz, odd_xz), (e_yz, t_yz, odd_yz)):
        same, cross = even + t, even - t
        post += [same + odd[0], same - odd[0], cross + odd[1], cross - odd[1]]
    return [jnp.where(solid, f[OPPOSITE[i]], post[i]) for i in range(19)]


class Shape:
    def __init__(self, mesh, block):
        self.nx, self.ny, self.nz = (mesh.shape[a] for a in ("gx", "gy", "gz"))
        self.x, self.y, self.z = block
        self.slab = self.z // self.nx
        self.width = LANES // 2
        self.groups = 2
        self.own = self.x // self.groups
        self.subs = self.x * self.nx // self.groups
        self.rows = self.y + 2 * HALO
        assert self.z == LANES and self.slab * self.nx == self.z
        assert self.slab + 2 * HALO <= self.width and 2 * self.slab <= self.width
        assert self.y == HALO and self.own * self.groups == self.x
        assert self.subs % 8 == 0
        if self.nx & (self.nx - 1) == 0:
            self.peer = lambda k, slot: jnp.bitwise_xor(k, slot)
            self.perm = lambda slot: [(i, i ^ slot) for i in range(self.nx)]
            self.sender = self.peer
        else:
            self.peer = lambda k, slot: lax.rem(k + slot, self.nx)
            self.sender = lambda k, slot: lax.rem(k + self.nx - slot, self.nx)
            self.perm = lambda slot: [(i, (i + slot) % self.nx) for i in range(self.nx)]


def vmem(n):
    return [pl.BlockSpec(memory_space=pltpu.VMEM)] * n


def grant(words):
    return pltpu.CompilerParams(vmem_limit_bytes=(words * 4 * 5) // 4 + (1 << 20))


def join_slots(parts):
    def body(*refs):
        for n, ref in enumerate(refs[:-1]):
            refs[-1][n] = ref[...]

    block = parts[0].shape
    return pl.pallas_call(
        body,
        name="join_slots",
        out_shape=jax.ShapeDtypeStruct((len(parts),) + block, jnp.float32),
        in_specs=vmem(len(parts)),
        out_specs=vmem(1)[0],
        compiler_params=grant(2 * len(parts) * math.prod(block)),
    )(*parts)


def gather_inputs(scatter, velocity, bubbles, walls):
    rho = jnp.where(bubbles == 1, VAPOUR, LIQUID) * scatter
    solid = jnp.where(walls == 1, 1.0, 0.0)
    return jnp.concatenate([rho[None], velocity, solid[None]])


def cut_slabs(values, before, after, sh):
    def body(v_ref, b_ref, a_ref, *outs):
        k = lax.axis_index("gx")
        lane = lax.broadcasted_iota(jnp.int32, (sh.y, LANES), 1)
        group = lane // sh.width
        for slot, out in enumerate(outs):
            q = sh.peer(k, slot)
            low = (lane >= LANES - HALO) & (q == 0)
            high = (lane < HALO) & (q == sh.nx - 1)
            start = HALO - q * sh.slab + 2 * LANES
            for n in range(5):
                for m in range(sh.own):
                    merged = None
                    for g in range(sh.groups):
                        x = m * sh.groups + g
                        plane = jnp.where(low, b_ref[n, x], v_ref[n, x])
                        plane = jnp.where(high, a_ref[n, x], plane)
                        plane = pltpu.roll(plane, lax.rem(start + g * sh.width, LANES), 1)
                        merged = plane if g == 0 else jnp.where(group == g, plane, merged)
                    out[n, m] = merged

    return pl.pallas_call(
        body,
        name="cut_slabs",
        out_shape=[jax.ShapeDtypeStruct((5, sh.own, sh.y, LANES), jnp.float32)] * sh.nx,
        in_specs=vmem(3),
        out_specs=vmem(sh.nx),
        compiler_params=grant((15 + 20) * math.prod(values.shape)),
    )(values, before, after)


def run_steps(below, middle, above, sh):
    half, subs = sh.rows // 2, sh.subs
    last = PAD + half - 1

    def body(b_ref, m_ref, a_ref, *rest):
        outs = rest[: sh.nx]
        raw, first, second, psi_ref, solid_ref, force_ref, done = rest[sh.nx :]
        k = lax.axis_index("gx")
        lane = lax.broadcasted_iota(jnp.int32, (subs, LANES), 1)
        low = lane < sh.width

        for slot in range(sh.nx):
            base = sh.sender(k, slot) * (sh.own * sh.rows)
            for part, ref in enumerate((b_ref, m_ref, a_ref)):
                for n in range(5):
                    for m in range(sh.own):
                        at = pl.multiple_of(base + m * sh.rows + part * sh.y, 8)
                        raw[n, pl.ds(at, sh.y), :] = ref[slot, n, m]

        def along_x(pair, cx):
            if cx == 1:
                return pltpu.roll(pair[1], 1, 0), pair[0]
            if cx == -1:
                return pair[1], pltpu.roll(pair[0], subs - 1, 0)
            return pair

        def along_z(value, cz):
            return pltpu.roll(value, cz % LANES, 1) if cz % LANES else value

        def over(count, at_once, step):
            at_once = min(at_once, count)
            while count % at_once:
                at_once -= 1

            def trip(n, _):
                for r in range(at_once):
                    step(n * at_once + r)
                return 0

            if count == at_once:
                trip(0, 0)
            else:
                lax.fori_loop(0, count // at_once, trip, 0)

        def weigh(f, y, p):
            psi_ref[p, y] = potential(sum(f[1:], f[0]), solid_ref[p, y] > 0.5)

        def reflect():
            for p in range(2):
                psi_ref[p, last + 1] = pltpu.roll(psi_ref[p, last], sh.width, 1)

        def start(n):
            y = PAD + n
            pairs = []
            for v in range(5):
                near = raw[v, pl.ds(n, subs, stride=sh.rows), :]
                far = raw[v, pl.ds(sh.rows - 1 - n, subs, stride=sh.rows), :]
                far = -far if v == 2 else far
                even = jnp.where(low, near, pltpu.roll(far, sh.width, 1))
                odd = jnp.where(low, pltpu.roll(near, sh.width, 1), far)
                pairs.append((even, odd))
            for p in range(2):
                rho, ux, uy, uz, solid = (pair[p] for pair in pairs)
                f = equilibrium(rho, [ux, uy, uz])
                solid_ref[p, y] = solid
                for i in range(19):
                    first[i, p, y] = f[i]
                weigh(f, y, p)

        over(half, START_ROWS, start)

        source, target = first, second
        for step in range(STEPS):
            lo = PAD + 2 * step
            if step > 0:

                def weigh_again(n, source=source, lo=lo):
                    for p in range(2):
                        weigh([source[i, p, lo + n] for i in range(19)], lo + n, p)

                over(half - 2 * step, WEIGH_ROWS, weigh_again)
            reflect()

            def push(y):
                here, up, down = (
                    [psi_ref[p, at] for p in range(2)] for at in (y, y + 1, y - 1)
                )
                rise = [up[p] - down[p] for p in range(2)]
                doubled = [2.0 * here[p] + (up[p] + down[p]) for p in range(2)]
                before, after = along_x(here, 1), along_x(here, -1)
                rise_x = [a + b for a, b in zip(along_x(rise, 1), along_x(rise, -1))]
                z_sum = [
                    doubled[p] + (along_z(here[p], 1) + along_z(here[p], -1)) for p in range(2)
                ]
                x_sum = [doubled[p] + (before[p] + after[p]) for p in range(2)]
                fx = [a - b for a, b in zip(along_x(z_sum, -1), along_x(z_sum, 1))]
                for p in range(2):
                    fy = (2.0 * rise[p] + rise_x[p]) + (
                        along_z(rise[p], 1) + along_z(rise[p], -1)
                    )
                    fz = along_z(x_sum[p], -1) - along_z(x_sum[p], 1)
                    scale = here[p] * (1.0 / 36.0)
                    for n, value in enumerate((fx[p], fy, fz)):
                        force_ref[n, p, y] = scale * value

            def stream(posts, y, at_end, target=target):
                for i in range(19):
                    cx, cy, cz = (int(c) for c in C[i])
                    to, row = i, y + cy
                    if at_end and cy == 1:
                        to, row, cz = MIRROR[i], y, cz + sh.width
                    for p, value in enumerate(along_x(posts[i], cx)):
                        target[to, p, row] = along_z(value, cz)

            def settle(y, p, forces, source=source):
                f = [source[i, p, y] for i in range(19)]
                return collide(f, forces, solid_ref[p, y] > 0.5)

            def load_forces(y):
                return [[force_ref[n, p, y] for n in range(3)] for p in range(2)]

            rows = half - 1 - 2 * step
            at_once = max(d for d in range(1, ADVANCE_ROWS + 1) if (rows - 1) % d == 0)

            def advance(n, _, lo=lo, push=push, stream=stream, settle=settle, at_once=at_once):
                ys = [lo + 1 + n * at_once + r for r in range(at_once)]
                forces = [load_forces(y) for y in ys[:AHEAD]]
                for r, y in enumerate(ys):
                    force = forces[r] if r < AHEAD else load_forces(y)
                    both = [settle(y, p, force[p]) for p in range(2)]
                    push(y + AHEAD)
                    stream(list(zip(*both)), y, False)
                return 0

            for r in range(AHEAD):
                push(lo + 1 + r)
            if at_once == rows - 1:
                advance(0, 0)
            else:
                lax.fori_loop(0, (rows - 1) // at_once, advance, 0)
            forces = load_forces(last)
            both = [settle(last, p, forces[p]) for p in range(2)]
            stream(list(zip(*both)), last, True)
            source, target = target, source

        quarter = sh.y // 2
        for n in range(quarter):
            y = PAD + HALO + n
            for p in range(2):
                f = [source[i, p, y] for i in range(19)]
                rho = sum(f[1:], f[0])
                fluid = solid_ref[p, y] < 0.5
                jx, jy, jz = moments(f)
                inverse = math.sqrt(3.0) / rho
                results = [rho * (1.0 / LIQUID), jx * inverse, jy * inverse, jz * inverse]
                for v, value in enumerate(results):
                    value = jnp.where(fluid, value, 0.0)
                    done[0, v, p, pl.ds(n, subs, stride=quarter), :] = value
                    value = -value if v == 2 else value
                    done[1, v, p, pl.ds(quarter - 1 - n, subs, stride=quarter), :] = value

        size = sh.own * quarter
        lane = lax.broadcasted_iota(jnp.int32, (size, LANES), 1)
        high = lane >= sh.width
        odd = (lane % sh.width) >= sh.slab
        for slot, out in enumerate(outs):
            at = pl.ds(pl.multiple_of(sh.peer(k, slot) * size, size), size)
            for v in range(4):
                even_odd = [
                    jnp.where(high, done[1, v, p, at, :], done[0, v, p, at, :]) for p in range(2)
                ]
                out[v] = jnp.where(
                    odd,
                    along_z(even_odd[1], sh.slab - HALO),
                    along_z(even_odd[0], -HALO),
                )

    padded = half + 2 * PAD
    row = (2, padded, subs, LANES)
    scratch = [
        (5, subs * sh.rows, LANES),
        (19,) + row,
        (19,) + row,
        row,
        row,
        (3,) + row,
        (2, 4, 2, subs * sh.y // 2, LANES),
    ]
    piece = (4, sh.own * sh.y // 2, LANES)
    words = sum(math.prod(shape) for shape in scratch)
    return pl.pallas_call(
        body,
        name="run_steps",
        out_shape=[jax.ShapeDtypeStruct(piece, jnp.float32)] * sh.nx,
        in_specs=vmem(3),
        out_specs=vmem(sh.nx),
        scratch_shapes=[pltpu.VMEM(shape, jnp.float32) for shape in scratch],
        compiler_params=grant(words + 3 * math.prod(middle.shape) + sh.nx * math.prod(piece)),
    )(below, middle, above)


def place_outputs(pieces, sh):
    quarter = sh.y // 2
    size = sh.own * quarter

    def body(*refs):
        ins, (density, velocity) = refs[: sh.nx], refs[sh.nx :]
        k = lax.axis_index("gx")
        place = lax.broadcasted_iota(jnp.int32, (size, LANES), 1) // sh.slab
        upper = lax.broadcasted_iota(jnp.int32, (sh.y, LANES), 0) < quarter
        for v in range(4):
            for p in range(2):
                halves = []
                for g in range(2):
                    merged = None
                    for slot, ref in enumerate(ins):
                        q = sh.sender(k, slot)
                        turn = q * sh.slab - g * sh.width - p * sh.slab + 2 * LANES
                        value = pltpu.roll(ref[v], lax.rem(turn, LANES), 1)
                        merged = value if slot == 0 else jnp.where(place == q, value, merged)
                    halves.append(merged)
                for m in range(sh.own):
                    to = density.at[2 * m + p] if v == 0 else velocity.at[v - 1, 2 * m + p]
                    for g in range(2):
                        to[g * quarter : (g + 1) * quarter, :] = halves[g][
                            m * quarter : (m + 1) * quarter
                        ]

    block = (sh.x, sh.y, sh.z)
    return pl.pallas_call(
        body,
        name="place_outputs",
        out_shape=[
            jax.ShapeDtypeStruct(block, jnp.float32),
            jax.ShapeDtypeStruct((3,) + block, jnp.float32),
        ],
        in_specs=vmem(sh.nx),
        out_specs=vmem(2),
        compiler_params=grant(8 * sh.nx * sh.y * LANES + 8 * math.prod(block)),
    )(*pieces)


def ring(size, step):
    return [(i, (i + step) % size) for i in range(size)]


def solution(mesh):
    def on_device(density_scatter, initial_velocity, bubble_mask, wall_flags):
        sh = Shape(mesh, wall_flags.shape)
        values = gather_inputs(density_scatter, initial_velocity, bubble_mask, wall_flags)
        before = lax.ppermute(values, "gz", ring(sh.nz, 1))
        after = before if sh.nz == 2 else lax.ppermute(values, "gz", ring(sh.nz, -1))
        slabs = cut_slabs(values, before, after, sh)
        got = [slabs[0]]
        for slot in range(1, sh.nx):
            got.append(lax.ppermute(slabs[slot], "gx", sh.perm(slot)))
        middle = join_slots(got)
        below = lax.ppermute(middle, "gy", ring(sh.ny, 1))
        above = lax.ppermute(middle, "gy", ring(sh.ny, -1))
        pieces = run_steps(below, middle, above, sh)
        back = [pieces[0]]
        for slot in range(1, sh.nx):
            back.append(lax.ppermute(pieces[slot], "gx", sh.perm(slot)))
        return tuple(place_outputs(back, sh))

    in_specs = (
        P("gx", "gy", "gz"),
        P(None, "gx", "gy", "gz"),
        P("gx", "gy", "gz"),
        P("gx", "gy", "gz"),
    )
    out_specs = (P("gx", "gy", "gz"), P(None, "gx", "gy", "gz"))
    return jax.shard_map(
        on_device, mesh=mesh, in_specs=in_specs, out_specs=out_specs, check_vma=False
    )
```

```python
import math

import jax
import jax.numpy as jnp
import numpy as np
from jax import lax
from jax.experimental import pallas as pl
from jax.experimental.pallas import tpu as pltpu
from jax.sharding import PartitionSpec as P

STEPS = 4
HALO = 2 * STEPS
LANES = 128

AHEAD = 2


C = np.array(
    [
        [0, 0, 0],
        [1, 0, 0],
        [-1, 0, 0],
        [0, 1, 0],
        [0, -1, 0],
        [0, 0, 1],
        [0, 0, -1],
        [1, 1, 0],
        [-1, -1, 0],
        [1, -1, 0],
        [-1, 1, 0],
        [1, 0, 1],
        [-1, 0, -1],
        [1, 0, -1],
        [-1, 0, 1],
        [0, 1, 1],
        [0, -1, -1],
        [0, 1, -1],
        [0, -1, 1],
    ]
)
WEIGHTS = [1.0 / 3.0] + [1.0 / 18.0] * 6 + [1.0 / 36.0] * 12
OPPOSITE = [0, 2, 1, 4, 3, 6, 5, 8, 7, 10, 9, 12, 11, 14, 13, 16, 15, 18, 17]
MIRROR = [int(np.flatnonzero((C == c * [1, -1, 1]).all(1))[0]) for c in C]
LIQUID = 0.28
VAPOUR = 0.06
WALL_POTENTIAL = 0.5
ATTRACTION = 1.0
TEMPERATURE = 0.06

KEEP_E = 1.0 - 1.19
KEEP_P = 1.0 - 1.4
KEEP_Q = 1.0 - 1.2
KEEP_N = 1.0 - 1.25
KEEP_M = 1.0 - 1.98


def equilibrium(rho, u):
    rest = 1.0 - 1.5 * (u[0] * u[0] + u[1] * u[1] + u[2] * u[2])
    rows = [(rho * WEIGHTS[0]) * rest]
    scaled = [None, rho * WEIGHTS[1], rho * WEIGHTS[7]]
    still = [None] + [w * rest for w in scaled[1:]]
    triple = [None] + [3.0 * w for w in scaled[1:]]
    for i in range(1, 19, 2):
        terms = [u[k] if C[i, k] > 0 else -u[k] for k in range(3) if C[i, k] != 0]
        n = len(terms)
        along = terms[0] if n == 1 else terms[0] + terms[1]
        odd = triple[n] * along
        even = still[n] + (1.5 * odd) * along
        rows += [even + odd, even - odd]
    return rows


def potential(rho, solid):
    square = rho * rho
    gap = 1.0 - rho
    pressure = (
        rho * TEMPERATURE * (1.0 + rho + square - square * rho) / (gap * gap * gap)
        - ATTRACTION * square
    )
    return jnp.where(solid, WALL_POTENTIAL, jnp.sqrt(6.0 * (rho * (1.0 / 3.0) - pressure)))


def times(c, value):
    c = float(np.float32(c))
    return value if c == 1.0 else -value if c == -1.0 else c * value


def moments(f):
    d = [None] + [f[i] - f[i + 1] for i in range(1, 19, 2)]
    jx = d[1] + ((d[4] + d[5]) + (d[6] + d[7]))
    jy = d[2] + ((d[4] - d[5]) + (d[8] + d[9]))
    jz = d[3] + ((d[6] - d[7]) + (d[8] - d[9]))
    return jx, jy, jz


def collide(f, force, solid):
    s = [None] + [f[i] + f[i + 1] for i in range(1, 19, 2)]
    d = [None] + [f[i] - f[i + 1] for i in range(1, 19, 2)]
    xy, xz, yz = s[4] + s[5], s[6] + s[7], s[8] + s[9]
    axes = s[1] + s[2] + s[3]
    diagonals = xy + xz + yz
    rho = f[0] + axes + diagonals
    p_xy, q_xy = d[4] + d[5], d[4] - d[5]
    p_xz, q_xz = d[6] + d[7], d[6] - d[7]
    p_yz, q_yz = d[8] + d[9], d[8] - d[9]
    j = [d[1] + (p_xy + p_xz), d[2] + (q_xy + p_yz), d[3] + (q_xz + q_yz)]
    inverse = 1.0 / rho
    u = [j[k] * inverse for k in range(3)]
    moved = [j[k] + force[k] for k in range(3)]
    v = [moved[k] * inverse for k in range(3)]
    uu = [j[k] * u[k] for k in range(3)]
    vv = [moved[k] * v[k] for k in range(3)]
    u2 = uu[0] + uu[1] + uu[2]
    v2 = vv[0] + vv[1] + vv[2]

    def isotropic(of_energy, of_epsilon):
        parts = (
            (1.0 / 19.0 - of_energy * (11.0 + 19.0 * KEEP_E) + of_epsilon * (3.0 + 9.0 * KEEP_P), rho),
            (of_energy * 19.0 * KEEP_E - of_epsilon * 16.0 * KEEP_P, axes),
            (of_energy * 38.0 * KEEP_E - of_epsilon * 11.0 * KEEP_P, diagonals),
            (of_energy * 19.0 - of_epsilon * 5.5, v2),
            (-of_energy * 19.0 * KEEP_E + of_epsilon * 5.5 * KEEP_P, u2),
        )
        return sum((c * value for c, value in parts[1:]), parts[0][0] * parts[0][1])

    even_axis = isotropic(-11.0 / 2394.0, -4.0 / 252.0)
    even_diag = isotropic(8.0 / 2394.0, 1.0 / 252.0)
    even_rest = rho - 6.0 * even_axis - 12.0 * even_diag

    def stress(a, b, at_v, at_u, scale):
        on_axis = (
            ((KEEP_N + 2.0 * KEEP_P) * scale) * a
            + ((KEEP_N - KEEP_P) * scale) * b
            + (1.5 * scale) * at_v
            - ((KEEP_N + 0.5 * KEEP_P) * scale) * at_u
        )
        half = 0.5 * scale
        on_diagonal = (
            ((2.0 * KEEP_N - 2.0 * KEEP_P) * half) * a
            + ((2.0 * KEEP_N + KEEP_P) * half) * b
            + (1.5 * half) * at_v
            - ((2.0 * KEEP_N - 0.5 * KEEP_P) * half) * at_u
        )
        return on_axis, on_diagonal

    h, g = stress(
        3.0 * s[1] - axes,
        diagonals - 3.0 * yz,
        3.0 * vv[0] - v2,
        3.0 * uu[0] - u2,
        1.0 / 36.0,
    )
    k, l = stress(s[2] - s[3], xy - xz, vv[1] - vv[2], uu[1] - uu[2], 1.0 / 12.0)

    quarter = [None, 0.25 * v[1], 0.25 * v[2]]

    def shear(a, b, pair):
        return (0.25 * KEEP_N) * (pair - j[a] * u[b]) + moved[a] * quarter[b]

    t_xy = shear(0, 1, s[4] - s[5])
    t_xz = shear(0, 2, s[6] - s[7])
    t_yz = shear(1, 2, s[8] - s[9])

    flux = [
        times(-5.0 * KEEP_Q, d[n + 1])
        + (times(KEEP_Q * 5.0 / 3.0 - 2.0 / 3.0, moved[n]) - (KEEP_Q * 5.0 / 3.0) * force[n])
        for n in range(3)
    ]
    tenth = [0.1 * moved[n] for n in range(3)]
    axis_odd = [tenth[n] - 0.1 * flux[n] for n in range(3)]
    diag_odd = [tenth[n] + 0.025 * flux[n] for n in range(3)]
    third = KEEP_M / 8.0
    mx, my, mz = third * (p_xy - p_xz), third * (p_yz - q_xy), third * (q_xz - q_yz)

    twist = even_axis - h
    evens = [even_axis + 2.0 * h, twist + k, twist - k]
    ring = even_diag + g
    e_xy, e_xz, e_yz = ring + l, ring - l, even_diag - 2.0 * g
    a, b = diag_odd[0] + mx, diag_odd[1] - my
    odd_xy = (a + b, a - b)
    a, b = diag_odd[0] - mx, diag_odd[2] + mz
    odd_xz = (a + b, a - b)
    a, b = diag_odd[1] + my, diag_odd[2] - mz
    odd_yz = (a + b, a - b)

    post = [even_rest]
    for n in range(3):
        post += [evens[n] + axis_odd[n], evens[n] - axis_odd[n]]
    for even, t, odd in ((e_xy, t_xy, odd_xy), (e_xz, t_xz, odd_xz), (e_yz, t_yz, odd_yz)):
        same, cross = even + t, even - t
        post += [same + odd[0], same - odd[0], cross + odd[1], cross - odd[1]]
    return [jnp.where(solid, f[OPPOSITE[i]], post[i]) for i in range(19)]


class Shape:
    def __init__(self, mesh, block):
        self.nx, self.ny, self.nz = (mesh.shape[a] for a in ("gx", "gy", "gz"))
        self.x, self.y, self.z = block
        self.slab = self.z // self.nx
        self.width = LANES // 2
        self.groups = 2
        self.own = self.x // self.groups
        self.subs = self.x * self.nx // self.groups
        self.span = self.slab + 2 * HALO
        self.tiles = -(-5 * self.x * self.span // LANES)
        self.rows = self.y + 2 * HALO
        assert self.z == LANES and self.slab * self.nx == self.z
        assert self.slab + 2 * HALO <= self.width and 2 * self.slab <= self.width
        assert self.y == HALO and self.own * self.groups == self.x
        assert self.subs % 8 == 0
        if self.nx & (self.nx - 1) == 0:
            self.peer = lambda k, slot: jnp.bitwise_xor(k, slot)
            self.perm = lambda slot: [(i, i ^ slot) for i in range(self.nx)]
            self.sender = self.peer
        else:
            self.peer = lambda k, slot: lax.rem(k + slot, self.nx)
            self.sender = lambda k, slot: lax.rem(k + self.nx - slot, self.nx)
            self.perm = lambda slot: [(i, (i + slot) % self.nx) for i in range(self.nx)]

    def window(self, n, x):
        return divmod((n * self.x + x) * self.span, LANES)


def vmem(n):
    return [pl.BlockSpec(memory_space=pltpu.VMEM)] * n


def grant(words):
    return pltpu.CompilerParams(vmem_limit_bytes=(words * 4 * 5) // 4 + (1 << 20))


def join_slots(parts):
    def body(*refs):
        for n, ref in enumerate(refs[:-1]):
            refs[-1][n] = ref[...]

    block = parts[0].shape
    return pl.pallas_call(
        body,
        name="join_slots",
        out_shape=jax.ShapeDtypeStruct((len(parts),) + block, jnp.float32),
        in_specs=vmem(len(parts)),
        out_specs=vmem(1)[0],
        compiler_params=grant(2 * len(parts) * math.prod(block)),
    )(*parts)


def gather_inputs(scatter, velocity, bubbles, walls):
    rho = jnp.where(bubbles == 1, VAPOUR, LIQUID) * scatter
    solid = jnp.where(walls == 1, 1.0, 0.0)
    return jnp.concatenate([rho[None], velocity, solid[None]])


def cut_slabs(values, before, after, sh):
    def body(v_ref, b_ref, a_ref, *outs):
        k = lax.axis_index("gx")
        lane = lax.broadcasted_iota(jnp.int32, (sh.y, LANES), 1)
        for slot, out in enumerate(outs):
            q = sh.peer(k, slot)
            low = (lane >= LANES - HALO) & (q == 0)
            high = (lane < HALO) & (q == sh.nx - 1)
            start = HALO - q * sh.slab + 2 * LANES
            tile = None
            for n in range(5):
                for x in range(sh.x):
                    plane = jnp.where(low, b_ref[n, x], v_ref[n, x])
                    plane = jnp.where(high, a_ref[n, x], plane)
                    at, off = sh.window(n, x)
                    plane = pltpu.roll(plane, lax.rem(start + off, LANES), 1)
                    tile = plane if tile is None else jnp.where(lane >= off, plane, tile)
                    if off + sh.span >= LANES:
                        out[at] = tile
                        tile = plane if off + sh.span > LANES else None
            if tile is not None:
                out[sh.tiles - 1] = tile

    shape = (sh.tiles, sh.y, LANES)
    return pl.pallas_call(
        body,
        name="cut_slabs",
        out_shape=[jax.ShapeDtypeStruct(shape, jnp.float32)] * sh.nx,
        in_specs=vmem(3),
        out_specs=vmem(sh.nx),
        compiler_params=grant(3 * math.prod(values.shape) + sh.nx * math.prod(shape)),
    )(values, before, after)


class Rows:
    def __init__(self, sh):
        self.sh = sh
        self.half, self.own = sh.rows // 2, HALO
        self.last = self.half - 1
        self.shape = lambda *lead: pltpu.VMEM(lead + (sh.subs, LANES), jnp.float32)
        self.out = lambda *lead: jax.ShapeDtypeStruct(lead + (sh.subs, LANES), jnp.float32)
        lane = lax.broadcasted_iota(jnp.int32, (sh.subs, LANES), 1)
        self.low = lane < sh.width
        self.early = [s for s in range(STEPS) if self.own + 2 * s + 1 <= self.last]

    def split(self, step):
        return self.own + 2 * step + 1 if step in self.early else self.half

    def writer(self, i, y):
        cy = int(C[i, 1])
        return self.last if y == self.last and cy == -1 else y - cy

    def along_x(self, pair, cx):
        if cx == 1:
            return pltpu.roll(pair[1], 1, 0), pair[0]
        if cx == -1:
            return pair[1], pltpu.roll(pair[0], self.sh.subs - 1, 0)
        return pair

    def along_z(self, value, cz):
        return pltpu.roll(value, cz % LANES, 1) if cz % LANES else value

    def unpack(self, raw, parts, k):
        sh = self.sh
        wide = lax.broadcasted_iota(jnp.int32, (sh.y, LANES), 1)
        near_half = lax.broadcasted_iota(jnp.int32, (sh.y, LANES), 0) < sh.y // 2
        rows = len(parts) * sh.y
        for slot in range(sh.nx):
            base = sh.sender(k, slot) * (sh.own * rows)
            for part, ref in enumerate(parts):
                for n in range(5):
                    for x in range(sh.x):
                        at, off = sh.window(n, x)
                        value = ref[slot, at]
                        if off + sh.span > LANES:
                            value = jnp.where(wide >= off, value, ref[slot, at + 1])
                        to_low = lambda: self.along_z(value, -off)
                        to_high = lambda: self.along_z(value, sh.width - off)
                        if len(parts) == 1:
                            value = jnp.where(near_half, to_low(), to_high())
                        else:
                            value = to_high() if part else to_low()
                        m, p = divmod(x, 2)
                        to = pl.multiple_of(base + m * rows + part * sh.y, 8)
                        raw[n, p, pl.ds(to, sh.y), :] = value

    def start(self, raw, rows, n, p):
        near, far = (
            [raw[v, p, pl.ds(at, self.sh.subs, stride=rows), :] for v in range(5)]
            for at in (n, rows - 1 - n)
        )
        far[2] = -far[2]
        return [jnp.where(self.low, a, b) for a, b in zip(near, far)]

    def weigh(self, f, solid):
        return potential(sum(f[1:], f[0]), solid > 0.5)

    def reflect(self, value):
        return self.along_z(value, self.sh.width)

    def push(self, psi, y):
        along_x, along_z = self.along_x, self.along_z
        here, up, down = ([psi(p, at) for p in range(2)] for at in (y, y + 1, y - 1))
        rise = [up[p] - down[p] for p in range(2)]
        doubled = [2.0 * here[p] + (up[p] + down[p]) for p in range(2)]
        before, after = along_x(here, 1), along_x(here, -1)
        rise_x = [a + b for a, b in zip(along_x(rise, 1), along_x(rise, -1))]
        z_sum = [doubled[p] + (along_z(here[p], 1) + along_z(here[p], -1)) for p in range(2)]
        x_sum = [doubled[p] + (before[p] + after[p]) for p in range(2)]
        fx = [a - b for a, b in zip(along_x(z_sum, -1), along_x(z_sum, 1))]
        forces = []
        for p in range(2):
            fy = (2.0 * rise[p] + rise_x[p]) + (along_z(rise[p], 1) + along_z(rise[p], -1))
            fz = along_z(x_sum[p], -1) - along_z(x_sum[p], 1)
            scale = here[p] * (1.0 / 36.0)
            forces.append([scale * value for value in (fx[p], fy, fz)])
        return forces

    def collide_rows(self, ys, psi, f, solid, store, force_ref):
        def form(y):
            for p, force in enumerate(self.push(psi, y)):
                for n in range(3):
                    force_ref[n, p, y] = force[n]

        for y in ys[:AHEAD]:
            form(y)
        for at, y in enumerate(ys):
            both = []
            for p in range(2):
                force = [force_ref[n, p, y] for n in range(3)]
                both.append(collide([f(i, p, y) for i in range(19)], force, solid(p, y) > 0.5))
            if at + AHEAD < len(ys):
                form(ys[at + AHEAD])
            for i, pair in enumerate(zip(*both)):
                cx, cy, cz = (int(c) for c in C[i])
                to, row = i, y + cy
                if y == self.last and cy == 1:
                    to, row, cz = MIRROR[i], y, cz + self.sh.width
                for p, value in enumerate(self.along_x(pair, cx)):
                    store(to, p, row, self.along_z(value, cz))


def kernel_call(body, name, operands, outs, scratch, flops):
    words = sum(math.prod(a.shape) for a in list(operands) + list(outs) + list(scratch))
    return pl.pallas_call(
        body,
        name=name,
        out_shape=outs,
        in_specs=vmem(len(operands)),
        out_specs=vmem(len(outs)),
        scratch_shapes=scratch,
        compiler_params=grant(words),
        cost_estimate=pl.CostEstimate(flops=flops, transcendentals=0, bytes_accessed=words * 4),
    )(*operands)


def prepare(middle, sh):
    rows = Rows(sh)
    own, last, early = rows.own, rows.last, rows.early
    count = rows.half - own

    def body(m_ref, solid_ref, first, *rest):
        psis, targets = rest[: len(early)], rest[len(early) : 2 * len(early)]
        raw, force_ref = rest[2 * len(early) :]
        low = Rows(sh)
        low.unpack(raw, [m_ref], lax.axis_index("gx"))
        solid = lambda p, y: solid_ref[p, y - own]
        for n in range(count):
            for p in range(2):
                rho, ux, uy, uz, wall = low.start(raw, sh.y, n, p)
                solid_ref[p, n] = wall
                for i, row in enumerate(equilibrium(rho, [ux, uy, uz])):
                    first[i, p, n] = row
        source, base = first, own
        for step in early:
            psi_ref, target, top = psis[step], targets[step], own + 2 * step
            f = lambda i, p, y, source=source, base=base: source[i, p, y - base]
            psi = lambda p, y, psi_ref=psi_ref, top=top: psi_ref[p, y - top]
            for p in range(2):
                for y in range(top, last + 1):
                    psi_ref[p, y - top] = low.weigh([f(i, p, y) for i in range(19)], solid(p, y))
                psi_ref[p, last + 1 - top] = low.reflect(psi_ref[p, last - top])

            def store(i, p, y, value, target=target, top=top):
                target[i, p, y - top] = value

            low.collide_rows(list(range(top + 1, last + 1)), psi, f, solid, store, force_ref)
            source, base = target, top

    lengths = [rows.half - own - 2 * step for step in early]
    outs = [rows.out(2, count), rows.out(19, 2, count)]
    outs += [rows.out(2, n + 1) for n in lengths] + [rows.out(19, 2, n) for n in lengths]
    scratch = [
        pltpu.VMEM((5, 2, sh.subs * sh.y, LANES), jnp.float32),
        rows.shape(3, 2, rows.half + 1),
    ]
    return kernel_call(body, "prepare", (middle,), outs, scratch, 5_000_000)


def run_steps(below, above, prepared, sh):
    rows = Rows(sh)
    half, own, last, early = rows.half, rows.own, rows.last, rows.early

    def body(b_ref, a_ref, solid_own, first_own, *rest):
        psis, gifts = rest[: len(early)], rest[len(early) : 2 * len(early)]
        outs = rest[2 * len(early) : 2 * len(early) + sh.nx]
        raw, one, other, psi_ref, solid_ref, force_ref, done = rest[2 * len(early) + sh.nx :]
        k = lax.axis_index("gx")
        low = Rows(sh)
        low.unpack(raw, [b_ref, a_ref], k)

        def solid(p, y):
            return solid_ref[p, y] if y < own else solid_own[p, y - own]

        for y in range(own):
            for p in range(2):
                rho, ux, uy, uz, wall = low.start(raw, 2 * sh.y, y, p)
                f = equilibrium(rho, [ux, uy, uz])
                solid_ref[p, y] = wall
                for i in range(19):
                    one[i, p, y] = f[i]
                psi_ref[p, y] = low.weigh(f, wall)

        source, target = one, other
        for step in range(STEPS):
            top = own + 2 * step

            def f(i, p, y, step=step, source=source):
                if step == 0 and y >= own:
                    return first_own[i, p, y - own]
                if step > 0 and rows.writer(i, y) >= rows.split(step - 1):
                    return gifts[step - 1][i, p, y - (top_of(step - 1))]
                return source[i, p, y]

            def top_of(step):
                return own + 2 * step

            def psi(p, y, step=step):
                if step in early and y >= top_of(step):
                    return psis[step][p, y - top_of(step)]
                return psi_ref[p, y]

            stop = top if step in early else half
            if step > 0:
                for y in range(2 * step, stop):
                    for p in range(2):
                        psi_ref[p, y] = low.weigh([f(i, p, y) for i in range(19)], solid(p, y))
            if step not in early:
                for p in range(2):
                    psi_ref[p, half] = low.reflect(psi_ref[p, last])

            def store(i, p, y, value, target=target):
                target[i, p, y] = value

            ys = list(range(2 * step + 1, rows.split(step)))
            low.collide_rows(ys, psi, f, solid, store, force_ref)
            source, target = target, source

        quarter = sh.y // 2
        for n in range(quarter):
            y = own + n
            for p in range(2):
                f = [source[i, p, y] for i in range(19)]
                rho = sum(f[1:], f[0])
                fluid = solid(p, y) < 0.5
                jx, jy, jz = moments(f)
                inverse = math.sqrt(3.0) / rho
                results = [rho * (1.0 / LIQUID), jx * inverse, jy * inverse, jz * inverse]
                for v, value in enumerate(results):
                    value = jnp.where(fluid, value, 0.0)
                    done[0, v, p, pl.ds(n, sh.subs, stride=quarter), :] = value
                    value = -value if v == 2 else value
                    done[1, v, p, pl.ds(quarter - 1 - n, sh.subs, stride=quarter), :] = value

        size = sh.own * quarter
        lane = lax.broadcasted_iota(jnp.int32, (size, LANES), 1)
        high = lane >= sh.width
        odd = (lane % sh.width) >= sh.slab
        for slot, out in enumerate(outs):
            at = pl.ds(pl.multiple_of(sh.peer(k, slot) * size, size), size)
            for v in range(4):
                even_odd = [
                    jnp.where(high, done[1, v, p, at, :], done[0, v, p, at, :]) for p in range(2)
                ]
                out[v] = jnp.where(
                    odd,
                    low.along_z(even_odd[1], sh.slab - HALO),
                    low.along_z(even_odd[0], -HALO),
                )

    scratch = [
        pltpu.VMEM((5, 2, sh.subs * 2 * sh.y, LANES), jnp.float32),
        rows.shape(19, 2, half),
        rows.shape(19, 2, half),
        rows.shape(2, half + 1),
        rows.shape(2, own),
        rows.shape(3, 2, half + 1),
        pltpu.VMEM((2, 4, 2, sh.subs * sh.y // 2, LANES), jnp.float32),
    ]
    piece = jax.ShapeDtypeStruct((4, sh.own * sh.y // 2, LANES), jnp.float32)
    operands = (below, above) + tuple(prepared)
    return kernel_call(body, "run_steps", operands, [piece] * sh.nx, scratch, 50_000_000)


def place_outputs(pieces, sh):
    quarter = sh.y // 2
    size = sh.own * quarter

    def body(*refs):
        ins, (density, velocity) = refs[: sh.nx], refs[sh.nx :]
        k = lax.axis_index("gx")
        place = lax.broadcasted_iota(jnp.int32, (size, LANES), 1) // sh.slab
        upper = lax.broadcasted_iota(jnp.int32, (sh.y, LANES), 0) < quarter
        for v in range(4):
            for p in range(2):
                halves = []
                for g in range(2):
                    merged = None
                    for slot, ref in enumerate(ins):
                        q = sh.sender(k, slot)
                        turn = q * sh.slab - g * sh.width - p * sh.slab + 2 * LANES
                        value = pltpu.roll(ref[v], lax.rem(turn, LANES), 1)
                        merged = value if slot == 0 else jnp.where(place == q, value, merged)
                    halves.append(merged)
                for m in range(sh.own):
                    to = density.at[2 * m + p] if v == 0 else velocity.at[v - 1, 2 * m + p]
                    for g in range(2):
                        to[g * quarter : (g + 1) * quarter, :] = halves[g][
                            m * quarter : (m + 1) * quarter
                        ]

    block = (sh.x, sh.y, sh.z)
    return pl.pallas_call(
        body,
        name="place_outputs",
        out_shape=[
            jax.ShapeDtypeStruct(block, jnp.float32),
            jax.ShapeDtypeStruct((3,) + block, jnp.float32),
        ],
        in_specs=vmem(sh.nx),
        out_specs=vmem(2),
        compiler_params=grant(8 * sh.nx * sh.y * LANES + 8 * math.prod(block)),
    )(*pieces)


def ring(size, step):
    return [(i, (i + step) % size) for i in range(size)]


def solution(mesh):
    def on_device(density_scatter, initial_velocity, bubble_mask, wall_flags):
        sh = Shape(mesh, wall_flags.shape)
        values = gather_inputs(density_scatter, initial_velocity, bubble_mask, wall_flags)
        before = lax.ppermute(values, "gz", ring(sh.nz, 1))
        after = before if sh.nz == 2 else lax.ppermute(values, "gz", ring(sh.nz, -1))
        slabs = cut_slabs(values, before, after, sh)
        got = [slabs[0]]
        for slot in range(1, sh.nx):
            got.append(lax.ppermute(slabs[slot], "gx", sh.perm(slot)))
        middle = join_slots(got)
        below = lax.ppermute(middle, "gy", ring(sh.ny, 1))
        above = lax.ppermute(middle, "gy", ring(sh.ny, -1))
        pieces = run_steps(below, above, prepare(middle, sh), sh)
        back = [pieces[0]]
        for slot in range(1, sh.nx):
            back.append(lax.ppermute(pieces[slot], "gx", sh.perm(slot)))
        return tuple(place_outputs(back, sh))

    in_specs = (
        P("gx", "gy", "gz"),
        P(None, "gx", "gy", "gz"),
        P("gx", "gy", "gz"),
        P("gx", "gy", "gz"),
    )
    out_specs = (P("gx", "gy", "gz"), P(None, "gx", "gy", "gz"))
    return jax.shard_map(
        on_device, mesh=mesh, in_specs=in_specs, out_specs=out_specs, check_vma=False
    )
```

```python
import math

import jax
import jax.numpy as jnp
import numpy as np
from jax import lax
from jax.experimental import pallas as pl
from jax.experimental.pallas import tpu as pltpu
from jax.sharding import PartitionSpec as P

STEPS = 4
HALO = 2 * STEPS
LANES = 128

AHEAD = 2


C = np.array(
    [
        [0, 0, 0],
        [1, 0, 0],
        [-1, 0, 0],
        [0, 1, 0],
        [0, -1, 0],
        [0, 0, 1],
        [0, 0, -1],
        [1, 1, 0],
        [-1, -1, 0],
        [1, -1, 0],
        [-1, 1, 0],
        [1, 0, 1],
        [-1, 0, -1],
        [1, 0, -1],
        [-1, 0, 1],
        [0, 1, 1],
        [0, -1, -1],
        [0, 1, -1],
        [0, -1, 1],
    ]
)
WEIGHTS = [1.0 / 3.0] + [1.0 / 18.0] * 6 + [1.0 / 36.0] * 12
OPPOSITE = [0, 2, 1, 4, 3, 6, 5, 8, 7, 10, 9, 12, 11, 14, 13, 16, 15, 18, 17]
LIQUID = 0.28
VAPOUR = 0.06
WALL_POTENTIAL = 0.5
ATTRACTION = 1.0
TEMPERATURE = 0.06

KEEP_E = 1.0 - 1.19
KEEP_P = 1.0 - 1.4
KEEP_Q = 1.0 - 1.2
KEEP_N = 1.0 - 1.25
KEEP_M = 1.0 - 1.98


def equilibrium(rho, u):
    rest = 1.0 - 1.5 * (u[0] * u[0] + u[1] * u[1] + u[2] * u[2])
    rows = [(rho * WEIGHTS[0]) * rest]
    scaled = [None, rho * WEIGHTS[1], rho * WEIGHTS[7]]
    still = [None] + [w * rest for w in scaled[1:]]
    triple = [None] + [3.0 * w for w in scaled[1:]]
    for i in range(1, 19, 2):
        terms = [u[k] if C[i, k] > 0 else -u[k] for k in range(3) if C[i, k] != 0]
        n = len(terms)
        along = terms[0] if n == 1 else terms[0] + terms[1]
        odd = triple[n] * along
        even = still[n] + (1.5 * odd) * along
        rows += [even + odd, even - odd]
    return rows


def potential(rho):
    square = rho * rho
    gap = 1.0 - rho
    pressure = (
        rho * TEMPERATURE * (1.0 + rho + square - square * rho) / (gap * gap * gap)
        - ATTRACTION * square
    )
    return jnp.sqrt(6.0 * (rho * (1.0 / 3.0) - pressure))


def times(c, value):
    c = float(np.float32(c))
    return value if c == 1.0 else -value if c == -1.0 else c * value


def moments(f):
    d = [None] + [f[i] - f[i + 1] for i in range(1, 19, 2)]
    jx = d[1] + ((d[4] + d[5]) + (d[6] + d[7]))
    jy = d[2] + ((d[4] - d[5]) + (d[8] + d[9]))
    jz = d[3] + ((d[6] - d[7]) + (d[8] - d[9]))
    return jx, jy, jz


def collide(f, force, solid):
    s = [None] + [f[i] + f[i + 1] for i in range(1, 19, 2)]
    d = [None] + [f[i] - f[i + 1] for i in range(1, 19, 2)]
    xy, xz, yz = s[4] + s[5], s[6] + s[7], s[8] + s[9]
    axes = s[1] + s[2] + s[3]
    diagonals = xy + xz + yz
    rho = f[0] + axes + diagonals
    p_xy, q_xy = d[4] + d[5], d[4] - d[5]
    p_xz, q_xz = d[6] + d[7], d[6] - d[7]
    p_yz, q_yz = d[8] + d[9], d[8] - d[9]
    j = [d[1] + (p_xy + p_xz), d[2] + (q_xy + p_yz), d[3] + (q_xz + q_yz)]
    inverse = 1.0 / rho
    u = [j[k] * inverse for k in range(3)]
    moved = [j[k] + force[k] for k in range(3)]
    v = [moved[k] * inverse for k in range(3)]
    uu = [j[k] * u[k] for k in range(3)]
    vv = [moved[k] * v[k] for k in range(3)]
    u2 = uu[0] + uu[1] + uu[2]
    v2 = vv[0] + vv[1] + vv[2]

    def isotropic(of_energy, of_epsilon):
        parts = (
            (1.0 / 19.0 - of_energy * (11.0 + 19.0 * KEEP_E) + of_epsilon * (3.0 + 9.0 * KEEP_P), rho),
            (of_energy * 19.0 * KEEP_E - of_epsilon * 16.0 * KEEP_P, axes),
            (of_energy * 38.0 * KEEP_E - of_epsilon * 11.0 * KEEP_P, diagonals),
            (of_energy * 19.0 - of_epsilon * 5.5, v2),
            (-of_energy * 19.0 * KEEP_E + of_epsilon * 5.5 * KEEP_P, u2),
        )
        return sum((c * value for c, value in parts[1:]), parts[0][0] * parts[0][1])

    even_axis = isotropic(-11.0 / 2394.0, -4.0 / 252.0)
    even_diag = isotropic(8.0 / 2394.0, 1.0 / 252.0)
    even_rest = rho - 6.0 * even_axis - 12.0 * even_diag

    def stress(a, b, at_v, at_u, scale):
        on_axis = (
            ((KEEP_N + 2.0 * KEEP_P) * scale) * a
            + ((KEEP_N - KEEP_P) * scale) * b
            + (1.5 * scale) * at_v
            - ((KEEP_N + 0.5 * KEEP_P) * scale) * at_u
        )
        half = 0.5 * scale
        on_diagonal = (
            ((2.0 * KEEP_N - 2.0 * KEEP_P) * half) * a
            + ((2.0 * KEEP_N + KEEP_P) * half) * b
            + (1.5 * half) * at_v
            - ((2.0 * KEEP_N - 0.5 * KEEP_P) * half) * at_u
        )
        return on_axis, on_diagonal

    h, g = stress(
        3.0 * s[1] - axes,
        diagonals - 3.0 * yz,
        3.0 * vv[0] - v2,
        3.0 * uu[0] - u2,
        1.0 / 36.0,
    )
    k, l = stress(s[2] - s[3], xy - xz, vv[1] - vv[2], uu[1] - uu[2], 1.0 / 12.0)

    quarter = [None, 0.25 * v[1], 0.25 * v[2]]

    def shear(a, b, pair):
        return (0.25 * KEEP_N) * (pair - j[a] * u[b]) + moved[a] * quarter[b]

    t_xy = shear(0, 1, s[4] - s[5])
    t_xz = shear(0, 2, s[6] - s[7])
    t_yz = shear(1, 2, s[8] - s[9])

    flux = [
        times(-5.0 * KEEP_Q, d[n + 1])
        + (times(KEEP_Q * 5.0 / 3.0 - 2.0 / 3.0, moved[n]) - (KEEP_Q * 5.0 / 3.0) * force[n])
        for n in range(3)
    ]
    tenth = [0.1 * moved[n] for n in range(3)]
    axis_odd = [tenth[n] - 0.1 * flux[n] for n in range(3)]
    diag_odd = [tenth[n] + 0.025 * flux[n] for n in range(3)]
    third = KEEP_M / 8.0
    mx, my, mz = third * (p_xy - p_xz), third * (p_yz - q_xy), third * (q_xz - q_yz)

    twist = even_axis - h
    evens = [even_axis + 2.0 * h, twist + k, twist - k]
    ring = even_diag + g
    e_xy, e_xz, e_yz = ring + l, ring - l, even_diag - 2.0 * g
    a, b = diag_odd[0] + mx, diag_odd[1] - my
    odd_xy = (a + b, a - b)
    a, b = diag_odd[0] - mx, diag_odd[2] + mz
    odd_xz = (a + b, a - b)
    a, b = diag_odd[1] + my, diag_odd[2] - mz
    odd_yz = (a + b, a - b)

    post = [even_rest]
    for n in range(3):
        post += [evens[n] + axis_odd[n], evens[n] - axis_odd[n]]
    for even, t, odd in ((e_xy, t_xy, odd_xy), (e_xz, t_xz, odd_xz), (e_yz, t_yz, odd_yz)):
        same, cross = even + t, even - t
        post += [same + odd[0], same - odd[0], cross + odd[1], cross - odd[1]]
    return [jnp.where(solid, f[OPPOSITE[i]], post[i]) for i in range(19)]


class Shape:
    def __init__(self, mesh, block):
        self.nx, self.ny, self.nz = (mesh.shape[a] for a in ("gx", "gy", "gz"))
        self.x, self.y, self.z = block
        self.slab = self.z // self.nx
        self.width = LANES // 2
        self.groups = 2
        self.own = self.x // self.groups
        self.subs = self.x * self.nx // self.groups
        self.span = self.slab + 2 * HALO
        self.tiles = -(-5 * self.x * self.span // LANES)
        self.rows = self.y + 2 * HALO
        assert self.z == LANES and self.slab * self.nx == self.z
        assert self.slab + 2 * HALO <= self.width and 2 * self.slab <= self.width
        assert self.y == HALO and self.own * self.groups == self.x
        assert self.subs % 8 == 0
        if self.nx & (self.nx - 1) == 0:
            self.peer = lambda k, slot: jnp.bitwise_xor(k, slot)
            self.perm = lambda slot: [(i, i ^ slot) for i in range(self.nx)]
            self.sender = self.peer
        else:
            self.peer = lambda k, slot: lax.rem(k + slot, self.nx)
            self.sender = lambda k, slot: lax.rem(k + self.nx - slot, self.nx)
            self.perm = lambda slot: [(i, (i + slot) % self.nx) for i in range(self.nx)]

    def window(self, n, x):
        return divmod((n * self.x + x) * self.span, LANES)


def vmem(n):
    return [pl.BlockSpec(memory_space=pltpu.VMEM)] * n


def grant(words):
    return pltpu.CompilerParams(vmem_limit_bytes=(words * 4 * 5) // 4 + (1 << 20))


def join_slots(parts):
    def body(*refs):
        for n, ref in enumerate(refs[:-1]):
            refs[-1][n] = ref[...]

    block = parts[0].shape
    return pl.pallas_call(
        body,
        name="join_slots",
        out_shape=jax.ShapeDtypeStruct((len(parts),) + block, jnp.float32),
        in_specs=vmem(len(parts)),
        out_specs=vmem(1)[0],
        compiler_params=grant(2 * len(parts) * math.prod(block)),
    )(*parts)


def gather_inputs(scatter, velocity, bubbles, walls):
    rho = jnp.where(bubbles == 1, VAPOUR, LIQUID) * scatter
    solid = jnp.where(walls == 1, 1.0, 0.0)
    return jnp.concatenate([rho[None], velocity, solid[None]])


def cut_slabs(values, before, after, sh):
    def body(v_ref, b_ref, a_ref, *outs):
        k = lax.axis_index("gx")
        lane = lax.broadcasted_iota(jnp.int32, (sh.y, LANES), 1)
        for slot, out in enumerate(outs):
            q = sh.peer(k, slot)
            low = (lane >= LANES - HALO) & (q == 0)
            high = (lane < HALO) & (q == sh.nx - 1)
            start = HALO - q * sh.slab + 2 * LANES
            tile = None
            for n in range(5):
                for x in range(sh.x):
                    plane = jnp.where(low, b_ref[n, x], v_ref[n, x])
                    plane = jnp.where(high, a_ref[n, x], plane)
                    at, off = sh.window(n, x)
                    plane = pltpu.roll(plane, lax.rem(start + off, LANES), 1)
                    tile = plane if tile is None else jnp.where(lane >= off, plane, tile)
                    if off + sh.span >= LANES:
                        out[at] = tile
                        tile = plane if off + sh.span > LANES else None
            if tile is not None:
                out[sh.tiles - 1] = tile

    shape = (sh.tiles, sh.y, LANES)
    return pl.pallas_call(
        body,
        name="cut_slabs",
        out_shape=[jax.ShapeDtypeStruct(shape, jnp.float32)] * sh.nx,
        in_specs=vmem(3),
        out_specs=vmem(sh.nx),
        compiler_params=grant(3 * math.prod(values.shape) + sh.nx * math.prod(shape)),
    )(values, before, after)


STAGES = ("own", "above", "below")


class Rows:
    def __init__(self, sh):
        self.sh = sh
        self.own, self.end = HALO, HALO + sh.y
        lane = lax.broadcasted_iota(jnp.int32, (sh.subs, LANES), 1)
        self.odd = lane >= sh.width

    def inputs(self, stage):
        first = {"own": self.own, "above": self.end, "below": 0}[stage]
        return first, first + self.sh.y - 1

    def weighed(self, stage, s):
        own, end, rows = self.own, self.end, self.sh.rows
        return {
            "own": (own + 2 * s, end - 1 - 2 * s),
            "above": (max(own + 2 * s, end - 2 * s), rows - 1 - 2 * s),
            "below": (2 * s, own - 1 + 2 * s),
        }[stage]

    def collided(self, stage, s):
        own, end, rows = self.own, self.end, self.sh.rows
        return {
            "own": (own + 1 + 2 * s, end - 2 - 2 * s),
            "above": (max(own + 1 + 2 * s, end - 1 - 2 * s), rows - 2 - 2 * s),
            "below": (1 + 2 * s, own + 2 * s),
        }[stage]

    def steps(self, stage):
        ranges = [self.collided(stage, s) for s in range(STEPS)]
        return [s for s, (first, last) in enumerate(ranges) if first <= last]

    def buffers(self, stage):
        left = {("solid",): ((),) + self.inputs(stage), ("f", 0): ((19,),) + self.inputs(stage)}
        for s in self.steps(stage):
            left["psi", s] = ((),) + self.weighed(stage, s)
            first, last = self.collided(stage, s)
            left["f", s + 1] = ((19,), first - 1, last + 1)
        return left

    def shapes(self, stage):
        return [
            lead + (last + 1 - first, self.sh.subs, LANES)
            for lead, first, last in self.buffers(stage).values()
        ]

    def shifted(self, value, cx, cz):
        if cx == 1:
            value = jnp.where(self.odd, pltpu.roll(value, 1, 0), value)
        if cx == -1:
            value = jnp.where(self.odd, value, pltpu.roll(value, self.sh.subs - 1, 0))
        turn = (cx * self.sh.width + cz) % LANES
        return pltpu.roll(value, turn, 1) if turn else value

    def unpack(self, raw, ref, k):
        sh = self.sh
        wide = lax.broadcasted_iota(jnp.int32, (sh.y, LANES), 1)

        def plane(slot, n, x):
            at, off = sh.window(n, x)
            value = ref[slot, at]
            if off + sh.span > LANES:
                value = jnp.where(wide >= off, value, ref[slot, at + 1])
            turn = (x % 2 * sh.width - off) % LANES
            return pltpu.roll(value, turn, 1) if turn else value

        for slot in range(sh.nx):
            base = sh.sender(k, slot) * (sh.own * sh.y)
            for n in range(5):
                for m in range(sh.own):
                    value = jnp.where(
                        wide < sh.width, plane(slot, n, 2 * m), plane(slot, n, 2 * m + 1)
                    )
                    raw[n, pl.ds(pl.multiple_of(base + m * sh.y, 8), sh.y), :] = value

    def push(self, psi, y):
        shifted = self.shifted
        here, up, down = psi(y), psi(y + 1), psi(y - 1)
        rise = up - down
        doubled = 2.0 * here + (up + down)
        z_sum = doubled + (shifted(here, 0, 1) + shifted(here, 0, -1))
        x_sum = doubled + (shifted(here, 1, 0) + shifted(here, -1, 0))
        fy = (2.0 * rise + (shifted(rise, 1, 0) + shifted(rise, -1, 0))) + (
            shifted(rise, 0, 1) + shifted(rise, 0, -1)
        )
        fx = shifted(z_sum, -1, 0) - shifted(z_sum, 1, 0)
        fz = shifted(x_sum, 0, -1) - shifted(x_sum, 0, 1)
        scale = here * (1.0 / 36.0)
        return [scale * value for value in (fx, fy, fz)]

    def run(self, stage, held, raw, force_ref, fresh, k):
        sh = self.sh
        table = {other: self.buffers(other) for other in STAGES}

        def at(owner, name, y):
            return held[owner, name], y - table[owner][name][1]

        def owner_of(ranges, y):
            for other in STAGES:
                first, last = ranges(other)
                if first <= y <= last:
                    return other
            raise AssertionError(y)

        def solid(y):
            ref, row = at(owner_of(self.inputs, y), ("solid",), y)
            return ref[row] > 0.5

        def psi_of(s):
            def psi(y):
                ref, row = at(owner_of(lambda o: self.weighed(o, s), y), ("psi", s), y)
                return ref[row]

            return psi

        def f(s, i, y):
            if s == 0:
                owner = owner_of(self.inputs, y)
            else:
                from_row = y - int(C[i, 1])
                owner = owner_of(lambda o: self.collided(o, s - 1), from_row)
            ref, row = at(owner, ("f", s), y)
            return ref[i, row]

        self.unpack(raw, fresh, k)
        first, last = self.inputs(stage)
        for n in range(sh.y):
            rho, ux, uy, uz, wall = (raw[v, pl.ds(n, sh.subs, stride=sh.y), :] for v in range(5))
            held[stage, ("solid",)][n] = wall
            for i, row in enumerate(equilibrium(rho, [ux, uy, uz])):
                held[stage, ("f", 0)][i, n] = row

        for s in self.steps(stage):
            first, last = self.weighed(stage, s)
            for y in range(first, last + 1):
                rows = [f(s, i, y) for i in range(19)]
                held[stage, ("psi", s)][y - first] = jnp.where(
                    solid(y), WALL_POTENTIAL, potential(sum(rows[1:], rows[0]))
                )
            first, last = self.collided(stage, s)
            psi, ys = psi_of(s), list(range(first, last + 1))

            def form(y, psi=psi):
                for n, value in enumerate(self.push(psi, y)):
                    force_ref[n, y] = value

            for y in ys[:AHEAD]:
                form(y)
            for n, y in enumerate(ys):
                force = [force_ref[axis, y] for axis in range(3)]
                post = collide([f(s, i, y) for i in range(19)], force, solid(y))
                if n + AHEAD < len(ys):
                    form(ys[n + AHEAD])
                for i in range(19):
                    cx, cy, cz = (int(c) for c in C[i])
                    held[stage, ("f", s + 1)][i, y + cy - (first - 1)] = self.shifted(
                        post[i], cx, cz
                    )
        return f, solid


def run_stage(stage, fresh, left, sh, flops):
    rows = Rows(sh)
    before = STAGES[: STAGES.index(stage)]
    names = [(o, name) for o in before for name in rows.buffers(o)]
    own = [(stage, name) for name in rows.buffers(stage)]
    last_stage = stage == STAGES[-1]

    def body(fresh_ref, *refs):
        held = dict(zip(names, refs))
        refs = refs[len(names) :]
        outs = ()
        if last_stage:
            outs, refs = refs[: sh.nx], refs[sh.nx :]
        held.update(zip(own, refs))
        raw, force_ref, done = refs[len(own) :]
        k = lax.axis_index("gx")
        low = Rows(sh)
        f, solid = low.run(stage, held, raw, force_ref, fresh_ref, k)
        if not last_stage:
            return
        for n in range(sh.y):
            y = low.own + n
            g = [f(STEPS, i, y) for i in range(19)]
            rho, wall = sum(g[1:], g[0]), solid(y)
            inverse = math.sqrt(3.0) / rho
            results = [rho * (1.0 / LIQUID)] + [c * inverse for c in moments(g)]
            for v, value in enumerate(results):
                done[v, pl.ds(n, sh.subs, stride=sh.y), :] = jnp.where(wall, 0.0, value)
        lane = lax.broadcasted_iota(jnp.int32, (sh.y, LANES), 1)
        place = (lane % sh.width) // sh.slab
        for slot, out in enumerate(outs):
            base = sh.peer(k, slot) * (sh.own * sh.y)
            for v in range(4):
                merged = None
                for m in range(sh.own):
                    value = done[v, pl.ds(pl.multiple_of(base + m * sh.y, 8), sh.y), :]
                    value = pltpu.roll(value, (m * sh.slab - HALO) % LANES, 1)
                    merged = value if m == 0 else jnp.where(place == m, value, merged)
                out[v] = merged

    shapes = rows.shapes(stage)
    piece = jax.ShapeDtypeStruct((4, sh.y, LANES), jnp.float32)
    scratch = [pltpu.VMEM(shape, jnp.float32) for shape in shapes]
    extra = [
        pltpu.VMEM((5, sh.subs * sh.y, LANES), jnp.float32),
        pltpu.VMEM((3, sh.rows, sh.subs, LANES), jnp.float32),
        pltpu.VMEM((4, sh.subs * sh.y, LANES), jnp.float32),
    ]
    outs = [jax.ShapeDtypeStruct(shape, jnp.float32) for shape in shapes]
    if last_stage:
        outs, extra = [piece] * sh.nx, scratch + extra
    operands = (fresh,) + tuple(left)
    words = sum(math.prod(a.shape) for a in list(operands) + list(outs) + list(extra))
    return pl.pallas_call(
        body,
        name="stage_" + stage,
        out_shape=outs,
        in_specs=vmem(len(operands)),
        out_specs=vmem(len(outs)),
        scratch_shapes=extra,
        compiler_params=grant(words),
        cost_estimate=pl.CostEstimate(flops=flops, transcendentals=0, bytes_accessed=words * 4),
    )(*operands)


def place_outputs(pieces, sh):
    def body(*refs):
        ins, (density, velocity) = refs[: sh.nx], refs[sh.nx :]
        k = lax.axis_index("gx")
        place = lax.broadcasted_iota(jnp.int32, (sh.y, LANES), 1) // sh.slab
        for v in range(4):
            for x in range(sh.x):
                m, g = divmod(x, 2)
                merged = None
                for slot, ref in enumerate(ins):
                    q = sh.sender(k, slot)
                    turn = (q - m) * sh.slab - g * sh.width + 2 * LANES
                    value = pltpu.roll(ref[v], lax.rem(turn, LANES), 1)
                    merged = value if slot == 0 else jnp.where(place == q, value, merged)
                if v == 0:
                    density[x] = merged
                else:
                    velocity[v - 1, x] = merged

    block = (sh.x, sh.y, sh.z)
    return pl.pallas_call(
        body,
        name="place_outputs",
        out_shape=[
            jax.ShapeDtypeStruct(block, jnp.float32),
            jax.ShapeDtypeStruct((3,) + block, jnp.float32),
        ],
        in_specs=vmem(sh.nx),
        out_specs=vmem(2),
        compiler_params=grant(8 * sh.nx * sh.y * LANES + 8 * math.prod(block)),
    )(*pieces)


def ring(size, step):
    return [(i, (i + step) % size) for i in range(size)]


def solution(mesh):
    def on_device(density_scatter, initial_velocity, bubble_mask, wall_flags):
        sh = Shape(mesh, wall_flags.shape)
        values = gather_inputs(density_scatter, initial_velocity, bubble_mask, wall_flags)
        before = lax.ppermute(values, "gz", ring(sh.nz, 1))
        after = before if sh.nz == 2 else lax.ppermute(values, "gz", ring(sh.nz, -1))
        slabs = cut_slabs(values, before, after, sh)
        got = [slabs[0]]
        for slot in range(1, sh.nx):
            got.append(lax.ppermute(slabs[slot], "gx", sh.perm(slot)))
        middle = join_slots(got)
        below = lax.ppermute(middle, "gy", ring(sh.ny, 1))
        above = lax.ppermute(middle, "gy", ring(sh.ny, -1))
        left = run_stage("own", middle, (), sh, 5_000_000)
        left = left + run_stage("above", above, left, sh, 20_000_000)
        pieces = run_stage("below", below, left, sh, 30_000_000)
        back = [pieces[0]]
        for slot in range(1, sh.nx):
            back.append(lax.ppermute(pieces[slot], "gx", sh.perm(slot)))
        return tuple(place_outputs(back, sh))

    in_specs = (
        P("gx", "gy", "gz"),
        P(None, "gx", "gy", "gz"),
        P("gx", "gy", "gz"),
        P("gx", "gy", "gz"),
    )
    out_specs = (P("gx", "gy", "gz"), P(None, "gx", "gy", "gz"))
    return jax.shard_map(
        on_device, mesh=mesh, in_specs=in_specs, out_specs=out_specs, check_vma=False
    )
```

```python
import math

import jax
import jax.numpy as jnp
import numpy as np
from jax import lax
from jax.experimental import pallas as pl
from jax.experimental.pallas import tpu as pltpu
from jax.sharding import PartitionSpec as P

STEPS = 4
HALO = 2 * STEPS
LANES = 128

LAG = 4
AHEAD = 2


C = np.array(
    [
        [0, 0, 0],
        [1, 0, 0],
        [-1, 0, 0],
        [0, 1, 0],
        [0, -1, 0],
        [0, 0, 1],
        [0, 0, -1],
        [1, 1, 0],
        [-1, -1, 0],
        [1, -1, 0],
        [-1, 1, 0],
        [1, 0, 1],
        [-1, 0, -1],
        [1, 0, -1],
        [-1, 0, 1],
        [0, 1, 1],
        [0, -1, -1],
        [0, 1, -1],
        [0, -1, 1],
    ]
)
WEIGHTS = [1.0 / 3.0] + [1.0 / 18.0] * 6 + [1.0 / 36.0] * 12
OPPOSITE = [0, 2, 1, 4, 3, 6, 5, 8, 7, 10, 9, 12, 11, 14, 13, 16, 15, 18, 17]
LIQUID = 0.28
VAPOUR = 0.06
WALL_POTENTIAL = 0.5
ATTRACTION = 1.0
TEMPERATURE = 0.06

KEEP_E = 1.0 - 1.19
KEEP_P = 1.0 - 1.4
KEEP_Q = 1.0 - 1.2
KEEP_N = 1.0 - 1.25
KEEP_M = 1.0 - 1.98


def equilibrium(rho, u):
    rest = 1.0 - 1.5 * (u[0] * u[0] + u[1] * u[1] + u[2] * u[2])
    rows = [(rho * WEIGHTS[0]) * rest]
    scaled = [None, rho * WEIGHTS[1], rho * WEIGHTS[7]]
    still = [None] + [w * rest for w in scaled[1:]]
    triple = [None] + [3.0 * w for w in scaled[1:]]
    for i in range(1, 19, 2):
        terms = [u[k] if C[i, k] > 0 else -u[k] for k in range(3) if C[i, k] != 0]
        n = len(terms)
        along = terms[0] if n == 1 else terms[0] + terms[1]
        odd = triple[n] * along
        even = still[n] + (1.5 * odd) * along
        rows += [even + odd, even - odd]
    return rows


def potential(rho):
    square = rho * rho
    gap = 1.0 - rho
    pressure = (
        rho * TEMPERATURE * (1.0 + rho + square - square * rho) / (gap * gap * gap)
        - ATTRACTION * square
    )
    return jnp.sqrt(6.0 * (rho * (1.0 / 3.0) - pressure))


def times(c, value):
    c = float(np.float32(c))
    return value if c == 1.0 else -value if c == -1.0 else c * value


def moments(f):
    d = [None] + [f[i] - f[i + 1] for i in range(1, 19, 2)]
    jx = d[1] + ((d[4] + d[5]) + (d[6] + d[7]))
    jy = d[2] + ((d[4] - d[5]) + (d[8] + d[9]))
    jz = d[3] + ((d[6] - d[7]) + (d[8] - d[9]))
    return jx, jy, jz


def collide(f, force, solid):
    s = [None] + [f[i] + f[i + 1] for i in range(1, 19, 2)]
    d = [None] + [f[i] - f[i + 1] for i in range(1, 19, 2)]
    xy, xz, yz = s[4] + s[5], s[6] + s[7], s[8] + s[9]
    axes = s[1] + s[2] + s[3]
    diagonals = xy + xz + yz
    rho = f[0] + axes + diagonals
    p_xy, q_xy = d[4] + d[5], d[4] - d[5]
    p_xz, q_xz = d[6] + d[7], d[6] - d[7]
    p_yz, q_yz = d[8] + d[9], d[8] - d[9]
    j = [d[1] + (p_xy + p_xz), d[2] + (q_xy + p_yz), d[3] + (q_xz + q_yz)]
    inverse = 1.0 / rho
    u = [j[k] * inverse for k in range(3)]
    moved = [j[k] + force[k] for k in range(3)]
    v = [moved[k] * inverse for k in range(3)]
    uu = [j[k] * u[k] for k in range(3)]
    vv = [moved[k] * v[k] for k in range(3)]
    u2 = uu[0] + uu[1] + uu[2]
    v2 = vv[0] + vv[1] + vv[2]

    def isotropic(of_energy, of_epsilon):
        parts = (
            (1.0 / 19.0 - of_energy * (11.0 + 19.0 * KEEP_E) + of_epsilon * (3.0 + 9.0 * KEEP_P), rho),
            (of_energy * 19.0 * KEEP_E - of_epsilon * 16.0 * KEEP_P, axes),
            (of_energy * 38.0 * KEEP_E - of_epsilon * 11.0 * KEEP_P, diagonals),
            (of_energy * 19.0 - of_epsilon * 5.5, v2),
            (-of_energy * 19.0 * KEEP_E + of_epsilon * 5.5 * KEEP_P, u2),
        )
        return sum((c * value for c, value in parts[1:]), parts[0][0] * parts[0][1])

    even_axis = isotropic(-11.0 / 2394.0, -4.0 / 252.0)
    even_diag = isotropic(8.0 / 2394.0, 1.0 / 252.0)
    even_rest = rho - 6.0 * even_axis - 12.0 * even_diag

    def stress(a, b, at_v, at_u, scale):
        on_axis = (
            ((KEEP_N + 2.0 * KEEP_P) * scale) * a
            + ((KEEP_N - KEEP_P) * scale) * b
            + (1.5 * scale) * at_v
            - ((KEEP_N + 0.5 * KEEP_P) * scale) * at_u
        )
        half = 0.5 * scale
        on_diagonal = (
            ((2.0 * KEEP_N - 2.0 * KEEP_P) * half) * a
            + ((2.0 * KEEP_N + KEEP_P) * half) * b
            + (1.5 * half) * at_v
            - ((2.0 * KEEP_N - 0.5 * KEEP_P) * half) * at_u
        )
        return on_axis, on_diagonal

    h, g = stress(
        3.0 * s[1] - axes,
        diagonals - 3.0 * yz,
        3.0 * vv[0] - v2,
        3.0 * uu[0] - u2,
        1.0 / 36.0,
    )
    k, l = stress(s[2] - s[3], xy - xz, vv[1] - vv[2], uu[1] - uu[2], 1.0 / 12.0)

    quarter = [None, 0.25 * v[1], 0.25 * v[2]]

    def shear(a, b, pair):
        return (0.25 * KEEP_N) * (pair - j[a] * u[b]) + moved[a] * quarter[b]

    t_xy = shear(0, 1, s[4] - s[5])
    t_xz = shear(0, 2, s[6] - s[7])
    t_yz = shear(1, 2, s[8] - s[9])

    flux = [
        times(-5.0 * KEEP_Q, d[n + 1])
        + (times(KEEP_Q * 5.0 / 3.0 - 2.0 / 3.0, moved[n]) - (KEEP_Q * 5.0 / 3.0) * force[n])
        for n in range(3)
    ]
    tenth = [0.1 * moved[n] for n in range(3)]
    axis_odd = [tenth[n] - 0.1 * flux[n] for n in range(3)]
    diag_odd = [tenth[n] + 0.025 * flux[n] for n in range(3)]
    third = KEEP_M / 8.0
    mx, my, mz = third * (p_xy - p_xz), third * (p_yz - q_xy), third * (q_xz - q_yz)

    twist = even_axis - h
    evens = [even_axis + 2.0 * h, twist + k, twist - k]
    ring = even_diag + g
    e_xy, e_xz, e_yz = ring + l, ring - l, even_diag - 2.0 * g
    a, b = diag_odd[0] + mx, diag_odd[1] - my
    odd_xy = (a + b, a - b)
    a, b = diag_odd[0] - mx, diag_odd[2] + mz
    odd_xz = (a + b, a - b)
    a, b = diag_odd[1] + my, diag_odd[2] - mz
    odd_yz = (a + b, a - b)

    post = [even_rest]
    for n in range(3):
        post += [evens[n] + axis_odd[n], evens[n] - axis_odd[n]]
    for even, t, odd in ((e_xy, t_xy, odd_xy), (e_xz, t_xz, odd_xz), (e_yz, t_yz, odd_yz)):
        same, cross = even + t, even - t
        post += [same + odd[0], same - odd[0], cross + odd[1], cross - odd[1]]
    return [jnp.where(solid, f[OPPOSITE[i]], post[i]) for i in range(19)]


class Shape:
    def __init__(self, mesh, block):
        self.nx, self.ny, self.nz = (mesh.shape[a] for a in ("gx", "gy", "gz"))
        self.x, self.y, self.z = block
        self.slab = self.z // self.nx
        self.width = LANES // 2
        self.groups = 2
        self.own = self.x // self.groups
        self.subs = self.x * self.nx // self.groups
        self.span = self.slab + 2 * HALO
        self.tiles = -(-5 * self.x * self.span // LANES)
        self.rows = self.y + 2 * HALO
        assert self.z == LANES and self.slab * self.nx == self.z
        assert self.slab + 2 * HALO <= self.width and 2 * self.slab <= self.width
        assert self.y == HALO and self.own * self.groups == self.x
        assert self.subs % 8 == 0
        if self.nx & (self.nx - 1) == 0:
            self.peer = lambda k, slot: jnp.bitwise_xor(k, slot)
            self.perm = lambda slot: [(i, i ^ slot) for i in range(self.nx)]
            self.sender = self.peer
        else:
            self.peer = lambda k, slot: lax.rem(k + slot, self.nx)
            self.sender = lambda k, slot: lax.rem(k + self.nx - slot, self.nx)
            self.perm = lambda slot: [(i, (i + slot) % self.nx) for i in range(self.nx)]

    def window(self, n, x):
        return divmod((n * self.x + x) * self.span, LANES)


def vmem(n):
    return [pl.BlockSpec(memory_space=pltpu.VMEM)] * n


def grant(words):
    return pltpu.CompilerParams(vmem_limit_bytes=(words * 4 * 5) // 4 + (1 << 20))


def join_slots(parts):
    def body(*refs):
        for n, ref in enumerate(refs[:-1]):
            refs[-1][n] = ref[...]

    block = parts[0].shape
    return pl.pallas_call(
        body,
        name="join_slots",
        out_shape=jax.ShapeDtypeStruct((len(parts),) + block, jnp.float32),
        in_specs=vmem(len(parts)),
        out_specs=vmem(1)[0],
        compiler_params=grant(2 * len(parts) * math.prod(block)),
    )(*parts)


def gather_inputs(scatter, velocity, bubbles, walls):
    rho = jnp.where(bubbles == 1, VAPOUR, LIQUID) * scatter
    solid = jnp.where(walls == 1, 1.0, 0.0)
    return jnp.concatenate([rho[None], velocity, solid[None]])


def cut_slabs(values, before, after, sh):
    def body(v_ref, b_ref, a_ref, *outs):
        k = lax.axis_index("gx")
        lane = lax.broadcasted_iota(jnp.int32, (sh.y, LANES), 1)
        for slot, out in enumerate(outs):
            q = sh.peer(k, slot)
            low = (lane >= LANES - HALO) & (q == 0)
            high = (lane < HALO) & (q == sh.nx - 1)
            start = HALO - q * sh.slab + 2 * LANES
            tile = None
            for n in range(5):
                for x in range(sh.x):
                    plane = jnp.where(low, b_ref[n, x], v_ref[n, x])
                    plane = jnp.where(high, a_ref[n, x], plane)
                    at, off = sh.window(n, x)
                    plane = pltpu.roll(plane, lax.rem(start + off, LANES), 1)
                    tile = plane if tile is None else jnp.where(lane >= off, plane, tile)
                    if off + sh.span >= LANES:
                        out[at] = tile
                        tile = plane if off + sh.span > LANES else None
            if tile is not None:
                out[sh.tiles - 1] = tile

    shape = (sh.tiles, sh.y, LANES)
    return pl.pallas_call(
        body,
        name="cut_slabs",
        out_shape=[jax.ShapeDtypeStruct(shape, jnp.float32)] * sh.nx,
        in_specs=vmem(3),
        out_specs=vmem(sh.nx),
        compiler_params=grant(3 * math.prod(values.shape) + sh.nx * math.prod(shape)),
    )(values, before, after)


STAGES = ("own", "above", "below")


class Rows:
    def __init__(self, sh):
        self.sh = sh
        self.own, self.end = HALO, HALO + sh.y
        lane = lax.broadcasted_iota(jnp.int32, (sh.subs, LANES), 1)
        self.odd = lane >= sh.width

    def inputs(self, stage):
        first = {"own": self.own, "above": self.end, "below": 0}[stage]
        return first, first + self.sh.y - 1

    def weighed(self, stage, s):
        own, end, rows = self.own, self.end, self.sh.rows
        return {
            "own": (own + 2 * s, end - 1 - 2 * s),
            "above": (max(own + 2 * s, end - 2 * s), rows - 1 - 2 * s),
            "below": (2 * s, own - 1 + 2 * s),
        }[stage]

    def collided(self, stage, s):
        own, end, rows = self.own, self.end, self.sh.rows
        return {
            "own": (own + 1 + 2 * s, end - 2 - 2 * s),
            "above": (max(own + 1 + 2 * s, end - 1 - 2 * s), rows - 2 - 2 * s),
            "below": (1 + 2 * s, own + 2 * s),
        }[stage]

    def steps(self, stage):
        ranges = [self.collided(stage, s) for s in range(STEPS)]
        return [s for s, (first, last) in enumerate(ranges) if first <= last]

    def buffers(self, stage):
        left = {("solid",): ((),) + self.inputs(stage), ("f", 0): ((19,),) + self.inputs(stage)}
        for s in self.steps(stage):
            left["psi", s] = ((),) + self.weighed(stage, s)
            first, last = self.collided(stage, s)
            left["f", s + 1] = ((19,), first - 1, last + 1)
        return left

    def shapes(self, stage):
        return [
            lead + (last + 1 - first, self.sh.subs, LANES)
            for lead, first, last in self.buffers(stage).values()
        ]

    def shifted(self, value, cx, cz):
        if cx == 1:
            value = jnp.where(self.odd, pltpu.roll(value, 1, 0), value)
        if cx == -1:
            value = jnp.where(self.odd, value, pltpu.roll(value, self.sh.subs - 1, 0))
        turn = (cx * self.sh.width + cz) % LANES
        return pltpu.roll(value, turn, 1) if turn else value

    def unpack(self, raw, ref, k):
        sh = self.sh
        wide = lax.broadcasted_iota(jnp.int32, (sh.y, LANES), 1)

        def plane(slot, n, x):
            at, off = sh.window(n, x)
            value = ref[slot, at]
            if off + sh.span > LANES:
                value = jnp.where(wide >= off, value, ref[slot, at + 1])
            turn = (x % 2 * sh.width - off) % LANES
            return pltpu.roll(value, turn, 1) if turn else value

        for slot in range(sh.nx):
            base = sh.sender(k, slot) * (sh.own * sh.y)
            for n in range(5):
                for m in range(sh.own):
                    value = jnp.where(
                        wide < sh.width, plane(slot, n, 2 * m), plane(slot, n, 2 * m + 1)
                    )
                    raw[n, pl.ds(pl.multiple_of(base + m * sh.y, 8), sh.y), :] = value

    def push(self, psi, y):
        shifted = self.shifted
        here, up, down = psi(y), psi(y + 1), psi(y - 1)
        rise = up - down
        doubled = 2.0 * here + (up + down)
        z_sum = doubled + (shifted(here, 0, 1) + shifted(here, 0, -1))
        x_sum = doubled + (shifted(here, 1, 0) + shifted(here, -1, 0))
        fy = (2.0 * rise + (shifted(rise, 1, 0) + shifted(rise, -1, 0))) + (
            shifted(rise, 0, 1) + shifted(rise, 0, -1)
        )
        fx = shifted(z_sum, -1, 0) - shifted(z_sum, 1, 0)
        fz = shifted(x_sum, 0, -1) - shifted(x_sum, 0, 1)
        scale = here * (1.0 / 36.0)
        return [scale * value for value in (fx, fy, fz)]

    def run(self, stage, held, raw, force_ref, fresh, k, finish):
        sh = self.sh
        table = {other: self.buffers(other) for other in STAGES}

        def at(owner, name, y):
            return held[owner, name], y - table[owner][name][1]

        def owner_of(ranges, y):
            for other in STAGES:
                first, last = ranges(other)
                if first <= y <= last:
                    return other
            raise AssertionError(y)

        def solid(y):
            ref, row = at(owner_of(self.inputs, y), ("solid",), y)
            return ref[row] > 0.5

        def psi_of(s):
            def psi(y):
                ref, row = at(owner_of(lambda o: self.weighed(o, s), y), ("psi", s), y)
                return ref[row]

            return psi

        def f(s, i, y):
            if s == 0:
                owner = owner_of(self.inputs, y)
            else:
                from_row = y - int(C[i, 1])
                owner = owner_of(lambda o: self.collided(o, s - 1), from_row)
            ref, row = at(owner, ("f", s), y)
            return ref[i, row]

        def begin(y):
            n = y - self.inputs(stage)[0]
            rho, ux, uy, uz, wall = (raw[v, pl.ds(n, sh.subs, stride=sh.y), :] for v in range(5))
            held[stage, ("solid",)][n] = wall
            for i, row in enumerate(equilibrium(rho, [ux, uy, uz])):
                held[stage, ("f", 0)][i, n] = row

        def weigh(s, y):
            rows = [f(s, i, y) for i in range(19)]
            psi = potential(sum(rows[1:], rows[0]))
            to = held[stage, ("psi", s)]
            to[y - self.weighed(stage, s)[0]] = jnp.where(solid(y), WALL_POTENTIAL, psi)

        def form(s, y):
            for n, value in enumerate(self.push(psi_of(s), y)):
                force_ref[s, n, y] = value

        def advance(s, y):
            force = [force_ref[s, axis, y] for axis in range(3)]
            post = collide([f(s, i, y) for i in range(19)], force, solid(y))
            base = self.collided(stage, s)[0] - 1
            for i in range(19):
                cx, cy, cz = (int(c) for c in C[i])
                held[stage, ("f", s + 1)][i, y + cy - base] = self.shifted(post[i], cx, cz)

        self.unpack(raw, fresh, k)
        if stage == STAGES[-1]:
            count = sh.y

            def at_tick(tick):
                items = [(s, self.own + 2 * s - (tick - LAG * s)) for s in range(STEPS)]
                return [(s, y) for s, y in items if 0 <= tick - LAG * s < count]

            for tick in range(-1, count + LAG * (STEPS - 1)):
                for s, y in at_tick(tick + 1):
                    if s == 0:
                        begin(y - 1)
                    weigh(s, y - 1)
                    form(s, y)
                for s, y in at_tick(tick):
                    advance(s, y)
                row = self.end - 1 - (tick - LAG * (STEPS - 1) - 1)
                if self.own <= row < self.end:
                    finish(f, solid, row)
            finish(f, solid, self.own)
            return

        first, last = self.inputs(stage)
        for y in range(first, last + 1):
            begin(y)
        for s in self.steps(stage):
            first, last = self.weighed(stage, s)
            for y in range(first, last + 1):
                weigh(s, y)
            first, last = self.collided(stage, s)
            ys = list(range(first, last + 1))
            for y in ys[:AHEAD]:
                form(s, y)
            for n, y in enumerate(ys):
                advance(s, y)
                if n + AHEAD < len(ys):
                    form(s, ys[n + AHEAD])


def run_stage(stage, fresh, left, sh, flops):
    rows = Rows(sh)
    before = STAGES[: STAGES.index(stage)]
    names = [(o, name) for o in before for name in rows.buffers(o)]
    own = [(stage, name) for name in rows.buffers(stage)]
    last_stage = stage == STAGES[-1]

    def body(fresh_ref, *refs):
        held = dict(zip(names, refs))
        refs = refs[len(names) :]
        outs = ()
        if last_stage:
            outs, refs = refs[: sh.nx], refs[sh.nx :]
        held.update(zip(own, refs))
        raw, force_ref, done = refs[len(own) :]
        k = lax.axis_index("gx")
        low = Rows(sh)

        def finish(f, solid, y):
            g = [f(STEPS, i, y) for i in range(19)]
            rho, wall = sum(g[1:], g[0]), solid(y)
            inverse = math.sqrt(3.0) / rho
            results = [rho * (1.0 / LIQUID)] + [c * inverse for c in moments(g)]
            for v, value in enumerate(results):
                at = pl.ds(y - low.own, sh.subs, stride=sh.y)
                done[v, at, :] = jnp.where(wall, 0.0, value)

        low.run(stage, held, raw, force_ref, fresh_ref, k, finish)
        if not last_stage:
            return
        lane = lax.broadcasted_iota(jnp.int32, (sh.y, LANES), 1)
        place = (lane % sh.width) // sh.slab
        for slot, out in enumerate(outs):
            base = sh.peer(k, slot) * (sh.own * sh.y)
            for v in range(4):
                merged = None
                for m in range(sh.own):
                    value = done[v, pl.ds(pl.multiple_of(base + m * sh.y, 8), sh.y), :]
                    value = pltpu.roll(value, (m * sh.slab - HALO) % LANES, 1)
                    merged = value if m == 0 else jnp.where(place == m, value, merged)
                out[v] = merged

    shapes = rows.shapes(stage)
    piece = jax.ShapeDtypeStruct((4, sh.y, LANES), jnp.float32)
    scratch = [pltpu.VMEM(shape, jnp.float32) for shape in shapes]
    extra = [
        pltpu.VMEM((5, sh.subs * sh.y, LANES), jnp.float32),
        pltpu.VMEM((STEPS, 3, sh.rows, sh.subs, LANES), jnp.float32),
        pltpu.VMEM((4, sh.subs * sh.y, LANES), jnp.float32),
    ]
    outs = [jax.ShapeDtypeStruct(shape, jnp.float32) for shape in shapes]
    if last_stage:
        outs, extra = [piece] * sh.nx, scratch + extra
    operands = (fresh,) + tuple(left)
    words = sum(math.prod(a.shape) for a in list(operands) + list(outs) + list(extra))
    return pl.pallas_call(
        body,
        name="stage_" + stage,
        out_shape=outs,
        in_specs=vmem(len(operands)),
        out_specs=vmem(len(outs)),
        scratch_shapes=extra,
        compiler_params=grant(words),
        cost_estimate=pl.CostEstimate(flops=flops, transcendentals=0, bytes_accessed=words * 4),
    )(*operands)


def place_outputs(pieces, sh):
    def body(*refs):
        ins, (density, velocity) = refs[: sh.nx], refs[sh.nx :]
        k = lax.axis_index("gx")
        place = lax.broadcasted_iota(jnp.int32, (sh.y, LANES), 1) // sh.slab
        for v in range(4):
            for x in range(sh.x):
                m, g = divmod(x, 2)
                merged = None
                for slot, ref in enumerate(ins):
                    q = sh.sender(k, slot)
                    turn = (q - m) * sh.slab - g * sh.width + 2 * LANES
                    value = pltpu.roll(ref[v], lax.rem(turn, LANES), 1)
                    merged = value if slot == 0 else jnp.where(place == q, value, merged)
                if v == 0:
                    density[x] = merged
                else:
                    velocity[v - 1, x] = merged

    block = (sh.x, sh.y, sh.z)
    return pl.pallas_call(
        body,
        name="place_outputs",
        out_shape=[
            jax.ShapeDtypeStruct(block, jnp.float32),
            jax.ShapeDtypeStruct((3,) + block, jnp.float32),
        ],
        in_specs=vmem(sh.nx),
        out_specs=vmem(2),
        compiler_params=grant(8 * sh.nx * sh.y * LANES + 8 * math.prod(block)),
    )(*pieces)


def ring(size, step):
    return [(i, (i + step) % size) for i in range(size)]


def solution(mesh):
    def on_device(density_scatter, initial_velocity, bubble_mask, wall_flags):
        sh = Shape(mesh, wall_flags.shape)
        values = gather_inputs(density_scatter, initial_velocity, bubble_mask, wall_flags)
        before = lax.ppermute(values, "gz", ring(sh.nz, 1))
        after = before if sh.nz == 2 else lax.ppermute(values, "gz", ring(sh.nz, -1))
        slabs = cut_slabs(values, before, after, sh)
        got = [slabs[0]]
        for slot in range(1, sh.nx):
            got.append(lax.ppermute(slabs[slot], "gx", sh.perm(slot)))
        middle = join_slots(got)
        below = lax.ppermute(middle, "gy", ring(sh.ny, 1))
        above = lax.ppermute(middle, "gy", ring(sh.ny, -1))
        left = run_stage("own", middle, (), sh, 5_000_000)
        left = left + run_stage("above", above, left, sh, 20_000_000)
        pieces = run_stage("below", below, left, sh, 30_000_000)
        back = [pieces[0]]
        for slot in range(1, sh.nx):
            back.append(lax.ppermute(pieces[slot], "gx", sh.perm(slot)))
        return tuple(place_outputs(back, sh))

    in_specs = (
        P("gx", "gy", "gz"),
        P(None, "gx", "gy", "gz"),
        P("gx", "gy", "gz"),
        P("gx", "gy", "gz"),
    )
    out_specs = (P("gx", "gy", "gz"), P(None, "gx", "gy", "gz"))
    return jax.shard_map(
        on_device, mesh=mesh, in_specs=in_specs, out_specs=out_specs, check_vma=False
    )
```

```python
import math

import jax
import jax.numpy as jnp
import numpy as np
from jax import lax
from jax.experimental import pallas as pl
from jax.experimental.pallas import tpu as pltpu
from jax.sharding import PartitionSpec as P

STEPS = 4
HALO = 2 * STEPS
LANES = 128

LAG = 4
AHEAD = 2


C = np.array(
    [
        [0, 0, 0],
        [1, 0, 0],
        [-1, 0, 0],
        [0, 1, 0],
        [0, -1, 0],
        [0, 0, 1],
        [0, 0, -1],
        [1, 1, 0],
        [-1, -1, 0],
        [1, -1, 0],
        [-1, 1, 0],
        [1, 0, 1],
        [-1, 0, -1],
        [1, 0, -1],
        [-1, 0, 1],
        [0, 1, 1],
        [0, -1, -1],
        [0, 1, -1],
        [0, -1, 1],
    ]
)
WEIGHTS = [1.0 / 3.0] + [1.0 / 18.0] * 6 + [1.0 / 36.0] * 12
OPPOSITE = [0, 2, 1, 4, 3, 6, 5, 8, 7, 10, 9, 12, 11, 14, 13, 16, 15, 18, 17]
LIQUID = 0.28
VAPOUR = 0.06
WALL_POTENTIAL = 0.5
ATTRACTION = 1.0
TEMPERATURE = 0.06

KEEP_E = 1.0 - 1.19
KEEP_P = 1.0 - 1.4
KEEP_Q = 1.0 - 1.2
KEEP_N = 1.0 - 1.25
KEEP_M = 1.0 - 1.98


def equilibrium(rho, u):
    rest = 1.0 - 1.5 * (u[0] * u[0] + u[1] * u[1] + u[2] * u[2])
    rows = [(rho * WEIGHTS[0]) * rest]
    scaled = [None, rho * WEIGHTS[1], rho * WEIGHTS[7]]
    still = [None] + [w * rest for w in scaled[1:]]
    triple = [None] + [3.0 * w for w in scaled[1:]]
    for i in range(1, 19, 2):
        terms = [u[k] if C[i, k] > 0 else -u[k] for k in range(3) if C[i, k] != 0]
        n = len(terms)
        along = terms[0] if n == 1 else terms[0] + terms[1]
        odd = triple[n] * along
        even = still[n] + (1.5 * odd) * along
        rows += [even + odd, even - odd]
    return rows


def potential(rho):
    square = rho * rho
    gap = 1.0 - rho
    pressure = (
        rho * TEMPERATURE * (1.0 + rho + square - square * rho) / (gap * gap * gap)
        - ATTRACTION * square
    )
    return jnp.sqrt(6.0 * (rho * (1.0 / 3.0) - pressure))


def times(c, value):
    c = float(np.float32(c))
    return value if c == 1.0 else -value if c == -1.0 else c * value


def moments(f):
    d = [None] + [f[i] - f[i + 1] for i in range(1, 19, 2)]
    jx = d[1] + ((d[4] + d[5]) + (d[6] + d[7]))
    jy = d[2] + ((d[4] - d[5]) + (d[8] + d[9]))
    jz = d[3] + ((d[6] - d[7]) + (d[8] - d[9]))
    return jx, jy, jz


def collide(f, force, solid):
    s = [None] + [f[i] + f[i + 1] for i in range(1, 19, 2)]
    d = [None] + [f[i] - f[i + 1] for i in range(1, 19, 2)]
    xy, xz, yz = s[4] + s[5], s[6] + s[7], s[8] + s[9]
    axes = s[1] + s[2] + s[3]
    diagonals = xy + xz + yz
    rho = f[0] + axes + diagonals
    p_xy, q_xy = d[4] + d[5], d[4] - d[5]
    p_xz, q_xz = d[6] + d[7], d[6] - d[7]
    p_yz, q_yz = d[8] + d[9], d[8] - d[9]
    j = [d[1] + (p_xy + p_xz), d[2] + (q_xy + p_yz), d[3] + (q_xz + q_yz)]
    inverse = 1.0 / rho
    u = [j[k] * inverse for k in range(3)]
    moved = [j[k] + force[k] for k in range(3)]
    v = [moved[k] * inverse for k in range(3)]
    uu = [j[k] * u[k] for k in range(3)]
    vv = [moved[k] * v[k] for k in range(3)]
    u2 = uu[0] + uu[1] + uu[2]
    v2 = vv[0] + vv[1] + vv[2]

    def isotropic(of_energy, of_epsilon):
        parts = (
            (1.0 / 19.0 - of_energy * (11.0 + 19.0 * KEEP_E) + of_epsilon * (3.0 + 9.0 * KEEP_P), rho),
            (of_energy * 19.0 * KEEP_E - of_epsilon * 16.0 * KEEP_P, axes),
            (of_energy * 38.0 * KEEP_E - of_epsilon * 11.0 * KEEP_P, diagonals),
            (of_energy * 19.0 - of_epsilon * 5.5, v2),
            (-of_energy * 19.0 * KEEP_E + of_epsilon * 5.5 * KEEP_P, u2),
        )
        return sum((c * value for c, value in parts[1:]), parts[0][0] * parts[0][1])

    even_axis = isotropic(-11.0 / 2394.0, -4.0 / 252.0)
    even_diag = isotropic(8.0 / 2394.0, 1.0 / 252.0)
    even_rest = rho - 6.0 * even_axis - 12.0 * even_diag

    def stress(a, b, at_v, at_u, scale):
        on_axis = (
            ((KEEP_N + 2.0 * KEEP_P) * scale) * a
            + ((KEEP_N - KEEP_P) * scale) * b
            + (1.5 * scale) * at_v
            - ((KEEP_N + 0.5 * KEEP_P) * scale) * at_u
        )
        half = 0.5 * scale
        on_diagonal = (
            ((2.0 * KEEP_N - 2.0 * KEEP_P) * half) * a
            + ((2.0 * KEEP_N + KEEP_P) * half) * b
            + (1.5 * half) * at_v
            - ((2.0 * KEEP_N - 0.5 * KEEP_P) * half) * at_u
        )
        return on_axis, on_diagonal

    h, g = stress(
        3.0 * s[1] - axes,
        diagonals - 3.0 * yz,
        3.0 * vv[0] - v2,
        3.0 * uu[0] - u2,
        1.0 / 36.0,
    )
    k, l = stress(s[2] - s[3], xy - xz, vv[1] - vv[2], uu[1] - uu[2], 1.0 / 12.0)

    quarter = [None, 0.25 * v[1], 0.25 * v[2]]

    def shear(a, b, pair):
        return (0.25 * KEEP_N) * (pair - j[a] * u[b]) + moved[a] * quarter[b]

    t_xy = shear(0, 1, s[4] - s[5])
    t_xz = shear(0, 2, s[6] - s[7])
    t_yz = shear(1, 2, s[8] - s[9])

    flux = [
        times(-5.0 * KEEP_Q, d[n + 1])
        + (times(KEEP_Q * 5.0 / 3.0 - 2.0 / 3.0, moved[n]) - (KEEP_Q * 5.0 / 3.0) * force[n])
        for n in range(3)
    ]
    tenth = [0.1 * moved[n] for n in range(3)]
    axis_odd = [tenth[n] - 0.1 * flux[n] for n in range(3)]
    diag_odd = [tenth[n] + 0.025 * flux[n] for n in range(3)]
    third = KEEP_M / 8.0
    mx, my, mz = third * (p_xy - p_xz), third * (p_yz - q_xy), third * (q_xz - q_yz)

    twist = even_axis - h
    evens = [even_axis + 2.0 * h, twist + k, twist - k]
    ring = even_diag + g
    e_xy, e_xz, e_yz = ring + l, ring - l, even_diag - 2.0 * g
    a, b = diag_odd[0] + mx, diag_odd[1] - my
    odd_xy = (a + b, a - b)
    a, b = diag_odd[0] - mx, diag_odd[2] + mz
    odd_xz = (a + b, a - b)
    a, b = diag_odd[1] + my, diag_odd[2] - mz
    odd_yz = (a + b, a - b)

    post = [even_rest]
    for n in range(3):
        post += [evens[n] + axis_odd[n], evens[n] - axis_odd[n]]
    for even, t, odd in ((e_xy, t_xy, odd_xy), (e_xz, t_xz, odd_xz), (e_yz, t_yz, odd_yz)):
        same, cross = even + t, even - t
        post += [same + odd[0], same - odd[0], cross + odd[1], cross - odd[1]]
    return [jnp.where(solid, f[OPPOSITE[i]], post[i]) for i in range(19)]


class Shape:
    def __init__(self, mesh, block):
        self.nx, self.ny, self.nz = (mesh.shape[a] for a in ("gx", "gy", "gz"))
        self.x, self.y, self.z = block
        self.slab = self.z // self.nx
        self.width = LANES // 2
        self.groups = 2
        self.own = self.x // self.groups
        self.subs = self.x * self.nx // self.groups
        self.span = self.slab + 2 * HALO
        self.tiles = -(-5 * self.x * self.span // LANES)
        self.rows = self.y + 2 * HALO
        assert self.z == LANES and self.slab * self.nx == self.z
        assert self.slab + 2 * HALO <= self.width and 2 * self.slab <= self.width
        assert self.y == HALO and self.own * self.groups == self.x
        assert self.subs % 8 == 0
        if self.nx & (self.nx - 1) == 0:
            self.peer = lambda k, slot: jnp.bitwise_xor(k, slot)
            self.perm = lambda slot: [(i, i ^ slot) for i in range(self.nx)]
            self.sender = self.slot_of = self.peer
        else:
            self.peer = lambda k, slot: lax.rem(k + slot, self.nx)
            self.sender = lambda k, slot: lax.rem(k + self.nx - slot, self.nx)
            self.slot_of = self.sender
            self.perm = lambda slot: [(i, (i + slot) % self.nx) for i in range(self.nx)]

    def window(self, n, x):
        return divmod((n * self.x + x) * self.span, LANES)


def vmem(n):
    return [pl.BlockSpec(memory_space=pltpu.VMEM)] * n


def grant(words):
    return pltpu.CompilerParams(vmem_limit_bytes=(words * 4 * 5) // 4 + (1 << 20))


def join_slots(parts):
    def body(*refs):
        for n, ref in enumerate(refs[:-1]):
            refs[-1][n] = ref[...]

    block = parts[0].shape
    return pl.pallas_call(
        body,
        name="join_slots",
        out_shape=jax.ShapeDtypeStruct((len(parts),) + block, jnp.float32),
        in_specs=vmem(len(parts)),
        out_specs=vmem(1)[0],
        compiler_params=grant(2 * len(parts) * math.prod(block)),
    )(*parts)


def gather_inputs(scatter, velocity, bubbles, walls):
    rho = jnp.where(bubbles == 1, VAPOUR, LIQUID) * scatter
    solid = jnp.where(walls == 1, 1.0, 0.0)
    return jnp.concatenate([rho[None], velocity, solid[None]])


def cut_slabs(values, before, after, sh):
    def body(v_ref, b_ref, a_ref, *outs):
        k = lax.axis_index("gx")
        lane = lax.broadcasted_iota(jnp.int32, (sh.y, LANES), 1)
        for slot, out in enumerate(outs):
            q = sh.peer(k, slot)
            low = (lane >= LANES - HALO) & (q == 0)
            high = (lane < HALO) & (q == sh.nx - 1)
            start = HALO - q * sh.slab + 2 * LANES
            tile = None
            for n in range(5):
                for x in range(sh.x):
                    plane = jnp.where(low, b_ref[n, x], v_ref[n, x])
                    plane = jnp.where(high, a_ref[n, x], plane)
                    at, off = sh.window(n, x)
                    plane = pltpu.roll(plane, lax.rem(start + off, LANES), 1)
                    tile = plane if tile is None else jnp.where(lane >= off, plane, tile)
                    if off + sh.span >= LANES:
                        out[at] = tile
                        tile = plane if off + sh.span > LANES else None
            if tile is not None:
                out[sh.tiles - 1] = tile

    shape = (sh.tiles, sh.y, LANES)
    return pl.pallas_call(
        body,
        name="cut_slabs",
        out_shape=[jax.ShapeDtypeStruct(shape, jnp.float32)] * sh.nx,
        in_specs=vmem(3),
        out_specs=vmem(sh.nx),
        compiler_params=grant(3 * math.prod(values.shape) + sh.nx * math.prod(shape)),
    )(values, before, after)


STAGES = ("own", "above", "below")


class Rows:
    def __init__(self, sh):
        self.sh = sh
        self.own, self.end = HALO, HALO + sh.y
        lane = lax.broadcasted_iota(jnp.int32, (sh.subs, LANES), 1)
        self.odd = lane >= sh.width

    def inputs(self, stage):
        first = {"own": self.own, "above": self.end, "below": 0}[stage]
        return first, first + self.sh.y - 1

    def weighed(self, stage, s):
        own, end, rows = self.own, self.end, self.sh.rows
        return {
            "own": (own + 2 * s, end - 1 - 2 * s),
            "above": (max(own + 2 * s, end - 2 * s), rows - 1 - 2 * s),
            "below": (2 * s, own - 1 + 2 * s),
        }[stage]

    def collided(self, stage, s):
        own, end, rows = self.own, self.end, self.sh.rows
        return {
            "own": (own + 1 + 2 * s, end - 2 - 2 * s),
            "above": (max(own + 1 + 2 * s, end - 1 - 2 * s), rows - 2 - 2 * s),
            "below": (1 + 2 * s, own + 2 * s),
        }[stage]

    def steps(self, stage):
        ranges = [self.collided(stage, s) for s in range(STEPS)]
        return [s for s, (first, last) in enumerate(ranges) if first <= last]

    def buffers(self, stage):
        left = {("solid",): ((),) + self.inputs(stage), ("f", 0): ((19,),) + self.inputs(stage)}
        for s in self.steps(stage):
            left["psi", s] = ((),) + self.weighed(stage, s)
            first, last = self.collided(stage, s)
            left["f", s + 1] = ((19,), first - 1, last + 1)
        return left

    def shapes(self, stage):
        return [
            lead + (last + 1 - first, self.sh.subs, LANES)
            for lead, first, last in self.buffers(stage).values()
        ]

    def shifted(self, value, cx, cz):
        if cx == 1:
            value = jnp.where(self.odd, pltpu.roll(value, 1, 0), value)
        if cx == -1:
            value = jnp.where(self.odd, value, pltpu.roll(value, self.sh.subs - 1, 0))
        turn = (cx * self.sh.width + cz) % LANES
        return pltpu.roll(value, turn, 1) if turn else value

    def unpack(self, raw, ref, k):
        sh = self.sh
        wide = lax.broadcasted_iota(jnp.int32, (sh.y, LANES), 1)

        def plane(slot, n, x):
            at, off = sh.window(n, x)
            value = ref[slot, at]
            if off + sh.span > LANES:
                value = jnp.where(wide >= off, value, ref[slot, at + 1])
            turn = (x % 2 * sh.width - off) % LANES
            return pltpu.roll(value, turn, 1) if turn else value

        slots = [sh.slot_of(k, q) for q in range(sh.nx)]
        for n in range(5):
            for q, slot in enumerate(slots):
                for m in range(sh.own):
                    value = jnp.where(
                        wide < sh.width, plane(slot, n, 2 * m), plane(slot, n, 2 * m + 1)
                    )
                    at = (q * sh.own + m) * sh.y
                    raw[n, at : at + sh.y, :] = value

    def push(self, psi, y):
        shifted = self.shifted
        here, up, down = psi(y), psi(y + 1), psi(y - 1)
        rise = up - down
        doubled = 2.0 * here + (up + down)
        z_sum = doubled + (shifted(here, 0, 1) + shifted(here, 0, -1))
        x_sum = doubled + (shifted(here, 1, 0) + shifted(here, -1, 0))
        fy = (2.0 * rise + (shifted(rise, 1, 0) + shifted(rise, -1, 0))) + (
            shifted(rise, 0, 1) + shifted(rise, 0, -1)
        )
        fx = shifted(z_sum, -1, 0) - shifted(z_sum, 1, 0)
        fz = shifted(x_sum, 0, -1) - shifted(x_sum, 0, 1)
        scale = here * (1.0 / 36.0)
        return [scale * value for value in (fx, fy, fz)]

    def run(self, stage, held, raw, force_ref, fresh, k, finish):
        sh = self.sh
        table = {other: self.buffers(other) for other in STAGES}

        def at(owner, name, y):
            return held[owner, name], y - table[owner][name][1]

        def owner_of(ranges, y):
            for other in STAGES:
                first, last = ranges(other)
                if first <= y <= last:
                    return other
            raise AssertionError(y)

        def solid(y):
            ref, row = at(owner_of(self.inputs, y), ("solid",), y)
            return ref[row] > 0.5

        def psi_of(s):
            def psi(y):
                ref, row = at(owner_of(lambda o: self.weighed(o, s), y), ("psi", s), y)
                return ref[row]

            return psi

        def f(s, i, y):
            if s == 0:
                owner = owner_of(self.inputs, y)
            else:
                from_row = y - int(C[i, 1])
                owner = owner_of(lambda o: self.collided(o, s - 1), from_row)
            ref, row = at(owner, ("f", s), y)
            return ref[i, row]

        def begin(y):
            n = y - self.inputs(stage)[0]
            rho, ux, uy, uz, wall = (raw[v, pl.ds(n, sh.subs, stride=sh.y), :] for v in range(5))
            held[stage, ("solid",)][n] = wall
            for i, row in enumerate(equilibrium(rho, [ux, uy, uz])):
                held[stage, ("f", 0)][i, n] = row

        def weigh(s, y):
            rows = [f(s, i, y) for i in range(19)]
            psi = potential(sum(rows[1:], rows[0]))
            to = held[stage, ("psi", s)]
            to[y - self.weighed(stage, s)[0]] = jnp.where(solid(y), WALL_POTENTIAL, psi)

        def form(s, y):
            for n, value in enumerate(self.push(psi_of(s), y)):
                force_ref[s, n, y] = value

        def advance(s, y):
            force = [force_ref[s, axis, y] for axis in range(3)]
            post = collide([f(s, i, y) for i in range(19)], force, solid(y))
            base = self.collided(stage, s)[0] - 1
            for i in range(19):
                cx, cy, cz = (int(c) for c in C[i])
                held[stage, ("f", s + 1)][i, y + cy - base] = self.shifted(post[i], cx, cz)

        self.unpack(raw, fresh, k)
        if stage == STAGES[-1]:
            count = sh.y

            def at_tick(tick):
                items = [(s, self.own + 2 * s - (tick - LAG * s)) for s in range(STEPS)]
                return [(s, y) for s, y in items if 0 <= tick - LAG * s < count]

            for tick in range(-1, count + LAG * (STEPS - 1)):
                for s, y in at_tick(tick + 1):
                    if s == 0:
                        begin(y - 1)
                    weigh(s, y - 1)
                    form(s, y)
                for s, y in at_tick(tick):
                    advance(s, y)
                row = self.end - 1 - (tick - LAG * (STEPS - 1) - 1)
                if self.own <= row < self.end:
                    finish(f, solid, row)
            finish(f, solid, self.own)
            return

        first, last = self.inputs(stage)
        for y in range(first, last + 1):
            begin(y)
        for s in self.steps(stage):
            first, last = self.weighed(stage, s)
            for y in range(first, last + 1):
                weigh(s, y)
            first, last = self.collided(stage, s)
            ys = list(range(first, last + 1))
            for y in ys[:AHEAD]:
                form(s, y)
            for n, y in enumerate(ys):
                advance(s, y)
                if n + AHEAD < len(ys):
                    form(s, ys[n + AHEAD])


def run_stage(stage, fresh, left, sh, flops):
    rows = Rows(sh)
    before = STAGES[: STAGES.index(stage)]
    names = [(o, name) for o in before for name in rows.buffers(o)]
    own = [(stage, name) for name in rows.buffers(stage)]
    last_stage = stage == STAGES[-1]

    def body(fresh_ref, *refs):
        held = dict(zip(names, refs))
        refs = refs[len(names) :]
        outs = ()
        if last_stage:
            outs, refs = refs[: sh.nx], refs[sh.nx :]
        held.update(zip(own, refs))
        raw, force_ref, done = refs[len(own) :]
        k = lax.axis_index("gx")
        low = Rows(sh)

        def finish(f, solid, y):
            g = [f(STEPS, i, y) for i in range(19)]
            rho, wall = sum(g[1:], g[0]), solid(y)
            inverse = math.sqrt(3.0) / rho
            results = [rho * (1.0 / LIQUID)] + [c * inverse for c in moments(g)]
            for v, value in enumerate(results):
                at = pl.ds(y - low.own, sh.subs, stride=sh.y)
                done[v, at, :] = jnp.where(wall, 0.0, value)

        low.run(stage, held, raw, force_ref, fresh_ref, k, finish)
        if not last_stage:
            return
        lane = lax.broadcasted_iota(jnp.int32, (sh.y, LANES), 1)
        place = (lane % sh.width) // sh.slab
        for slot, out in enumerate(outs):
            base = sh.peer(k, slot) * (sh.own * sh.y)
            for v in range(4):
                merged = None
                for m in range(sh.own):
                    value = done[v, pl.ds(pl.multiple_of(base + m * sh.y, 8), sh.y), :]
                    value = pltpu.roll(value, (m * sh.slab - HALO) % LANES, 1)
                    merged = value if m == 0 else jnp.where(place == m, value, merged)
                out[v] = merged

    shapes = rows.shapes(stage)
    piece = jax.ShapeDtypeStruct((4, sh.y, LANES), jnp.float32)
    scratch = [pltpu.VMEM(shape, jnp.float32) for shape in shapes]
    extra = [
        pltpu.VMEM((5, sh.subs * sh.y, LANES), jnp.float32),
        pltpu.VMEM((STEPS, 3, sh.rows, sh.subs, LANES), jnp.float32),
        pltpu.VMEM((4, sh.subs * sh.y, LANES), jnp.float32),
    ]
    outs = [jax.ShapeDtypeStruct(shape, jnp.float32) for shape in shapes]
    if last_stage:
        outs, extra = [piece] * sh.nx, scratch + extra
    operands = (fresh,) + tuple(left)
    words = sum(math.prod(a.shape) for a in list(operands) + list(outs) + list(extra))
    return pl.pallas_call(
        body,
        name="stage_" + stage,
        out_shape=outs,
        in_specs=vmem(len(operands)),
        out_specs=vmem(len(outs)),
        scratch_shapes=extra,
        compiler_params=grant(words),
        cost_estimate=pl.CostEstimate(flops=flops, transcendentals=0, bytes_accessed=words * 4),
    )(*operands)


def place_outputs(pieces, sh):
    def body(*refs):
        ins, (density, velocity) = refs[: sh.nx], refs[sh.nx :]
        k = lax.axis_index("gx")
        place = lax.broadcasted_iota(jnp.int32, (sh.y, LANES), 1) // sh.slab
        for v in range(4):
            for x in range(sh.x):
                m, g = divmod(x, 2)
                merged = None
                for slot, ref in enumerate(ins):
                    q = sh.sender(k, slot)
                    turn = (q - m) * sh.slab - g * sh.width + 2 * LANES
                    value = pltpu.roll(ref[v], lax.rem(turn, LANES), 1)
                    merged = value if slot == 0 else jnp.where(place == q, value, merged)
                if v == 0:
                    density[x] = merged
                else:
                    velocity[v - 1, x] = merged

    block = (sh.x, sh.y, sh.z)
    return pl.pallas_call(
        body,
        name="place_outputs",
        out_shape=[
            jax.ShapeDtypeStruct(block, jnp.float32),
            jax.ShapeDtypeStruct((3,) + block, jnp.float32),
        ],
        in_specs=vmem(sh.nx),
        out_specs=vmem(2),
        compiler_params=grant(8 * sh.nx * sh.y * LANES + 8 * math.prod(block)),
    )(*pieces)


def ring(size, step):
    return [(i, (i + step) % size) for i in range(size)]


def solution(mesh):
    def on_device(density_scatter, initial_velocity, bubble_mask, wall_flags):
        sh = Shape(mesh, wall_flags.shape)
        values = gather_inputs(density_scatter, initial_velocity, bubble_mask, wall_flags)
        before = lax.ppermute(values, "gz", ring(sh.nz, 1))
        after = before if sh.nz == 2 else lax.ppermute(values, "gz", ring(sh.nz, -1))
        slabs = cut_slabs(values, before, after, sh)
        got = [slabs[0]]
        for slot in range(1, sh.nx):
            got.append(lax.ppermute(slabs[slot], "gx", sh.perm(slot)))
        middle = join_slots(got)
        below = lax.ppermute(middle, "gy", ring(sh.ny, 1))
        above = lax.ppermute(middle, "gy", ring(sh.ny, -1))
        left = run_stage("own", middle, (), sh, 5_000_000)
        left = left + run_stage("above", above, left, sh, 20_000_000)
        pieces = run_stage("below", below, left, sh, 30_000_000)
        back = [pieces[0]]
        for slot in range(1, sh.nx):
            back.append(lax.ppermute(pieces[slot], "gx", sh.perm(slot)))
        return tuple(place_outputs(back, sh))

    in_specs = (
        P("gx", "gy", "gz"),
        P(None, "gx", "gy", "gz"),
        P("gx", "gy", "gz"),
        P("gx", "gy", "gz"),
    )
    out_specs = (P("gx", "gy", "gz"), P(None, "gx", "gy", "gz"))
    return jax.shard_map(
        on_device, mesh=mesh, in_specs=in_specs, out_specs=out_specs, check_vma=False
    )
```

```python
import math

import jax
import jax.numpy as jnp
import numpy as np
from jax import lax
from jax.experimental import pallas as pl
from jax.experimental.pallas import tpu as pltpu
from jax.sharding import PartitionSpec as P

STEPS = 4
HALO = 2 * STEPS
LANES = 128

LAG = 4
AHEAD = 2


C = np.array(
    [
        [0, 0, 0],
        [1, 0, 0],
        [-1, 0, 0],
        [0, 1, 0],
        [0, -1, 0],
        [0, 0, 1],
        [0, 0, -1],
        [1, 1, 0],
        [-1, -1, 0],
        [1, -1, 0],
        [-1, 1, 0],
        [1, 0, 1],
        [-1, 0, -1],
        [1, 0, -1],
        [-1, 0, 1],
        [0, 1, 1],
        [0, -1, -1],
        [0, 1, -1],
        [0, -1, 1],
    ]
)
WEIGHTS = [1.0 / 3.0] + [1.0 / 18.0] * 6 + [1.0 / 36.0] * 12
OPPOSITE = [0, 2, 1, 4, 3, 6, 5, 8, 7, 10, 9, 12, 11, 14, 13, 16, 15, 18, 17]
LIQUID = 0.28
VAPOUR = 0.06
WALL_POTENTIAL = 0.5
ATTRACTION = 1.0
TEMPERATURE = 0.06

KEEP_E = 1.0 - 1.19
KEEP_P = 1.0 - 1.4
KEEP_Q = 1.0 - 1.2
KEEP_N = 1.0 - 1.25
KEEP_M = 1.0 - 1.98


def equilibrium(rho, u):
    rest = 1.0 - 1.5 * (u[0] * u[0] + u[1] * u[1] + u[2] * u[2])
    rows = [(rho * WEIGHTS[0]) * rest]
    scaled = [None, rho * WEIGHTS[1], rho * WEIGHTS[7]]
    still = [None] + [w * rest for w in scaled[1:]]
    triple = [None] + [3.0 * w for w in scaled[1:]]
    for i in range(1, 19, 2):
        terms = [u[k] if C[i, k] > 0 else -u[k] for k in range(3) if C[i, k] != 0]
        n = len(terms)
        along = terms[0] if n == 1 else terms[0] + terms[1]
        odd = triple[n] * along
        even = still[n] + (1.5 * odd) * along
        rows += [even + odd, even - odd]
    return rows


def potential(rho):
    square = rho * rho
    gap = 1.0 - rho
    pressure = (
        rho * TEMPERATURE * (1.0 + rho + square - square * rho) / (gap * gap * gap)
        - ATTRACTION * square
    )
    return jnp.sqrt(6.0 * (rho * (1.0 / 3.0) - pressure))


def times(c, value):
    c = float(np.float32(c))
    return value if c == 1.0 else -value if c == -1.0 else c * value


def pair_sums(f):
    s = [f[i] + f[i + 1] for i in range(1, 19, 2)]
    xy, xz, yz = s[3] + s[4], s[5] + s[6], s[7] + s[8]
    axes, diagonals = s[0] + s[1] + s[2], xy + xz + yz
    return s + [xy, xz, yz, axes, diagonals, f[0] + axes + diagonals]


def moments(f):
    d = [None] + [f[i] - f[i + 1] for i in range(1, 19, 2)]
    jx = d[1] + ((d[4] + d[5]) + (d[6] + d[7]))
    jy = d[2] + ((d[4] - d[5]) + (d[8] + d[9]))
    jz = d[3] + ((d[6] - d[7]) + (d[8] - d[9]))
    return jx, jy, jz


def collide(f, sums, force, solid):
    s = [None] + sums[:9]
    d = [None] + [f[i] - f[i + 1] for i in range(1, 19, 2)]
    xy, xz, yz, axes, diagonals, rho = sums[9:]
    p_xy, q_xy = d[4] + d[5], d[4] - d[5]
    p_xz, q_xz = d[6] + d[7], d[6] - d[7]
    p_yz, q_yz = d[8] + d[9], d[8] - d[9]
    j = [d[1] + (p_xy + p_xz), d[2] + (q_xy + p_yz), d[3] + (q_xz + q_yz)]
    inverse = 1.0 / rho
    u = [j[k] * inverse for k in range(3)]
    moved = [j[k] + force[k] for k in range(3)]
    v = [moved[k] * inverse for k in range(3)]
    uu = [j[k] * u[k] for k in range(3)]
    vv = [moved[k] * v[k] for k in range(3)]
    u2 = uu[0] + uu[1] + uu[2]
    v2 = vv[0] + vv[1] + vv[2]

    def isotropic(of_energy, of_epsilon):
        parts = (
            (1.0 / 19.0 - of_energy * (11.0 + 19.0 * KEEP_E) + of_epsilon * (3.0 + 9.0 * KEEP_P), rho),
            (of_energy * 19.0 * KEEP_E - of_epsilon * 16.0 * KEEP_P, axes),
            (of_energy * 38.0 * KEEP_E - of_epsilon * 11.0 * KEEP_P, diagonals),
            (of_energy * 19.0 - of_epsilon * 5.5, v2),
            (-of_energy * 19.0 * KEEP_E + of_epsilon * 5.5 * KEEP_P, u2),
        )
        return sum((c * value for c, value in parts[1:]), parts[0][0] * parts[0][1])

    even_axis = isotropic(-11.0 / 2394.0, -4.0 / 252.0)
    even_diag = isotropic(8.0 / 2394.0, 1.0 / 252.0)
    even_rest = rho - 6.0 * even_axis - 12.0 * even_diag

    def stress(a, b, at_v, at_u, scale):
        on_axis = (
            ((KEEP_N + 2.0 * KEEP_P) * scale) * a
            + ((KEEP_N - KEEP_P) * scale) * b
            + (1.5 * scale) * at_v
            - ((KEEP_N + 0.5 * KEEP_P) * scale) * at_u
        )
        half = 0.5 * scale
        on_diagonal = (
            ((2.0 * KEEP_N - 2.0 * KEEP_P) * half) * a
            + ((2.0 * KEEP_N + KEEP_P) * half) * b
            + (1.5 * half) * at_v
            - ((2.0 * KEEP_N - 0.5 * KEEP_P) * half) * at_u
        )
        return on_axis, on_diagonal

    h, g = stress(
        3.0 * s[1] - axes,
        diagonals - 3.0 * yz,
        3.0 * vv[0] - v2,
        3.0 * uu[0] - u2,
        1.0 / 36.0,
    )
    k, l = stress(s[2] - s[3], xy - xz, vv[1] - vv[2], uu[1] - uu[2], 1.0 / 12.0)

    quarter = [None, 0.25 * v[1], 0.25 * v[2]]

    def shear(a, b, pair):
        return (0.25 * KEEP_N) * (pair - j[a] * u[b]) + moved[a] * quarter[b]

    t_xy = shear(0, 1, s[4] - s[5])
    t_xz = shear(0, 2, s[6] - s[7])
    t_yz = shear(1, 2, s[8] - s[9])

    flux = [
        times(-5.0 * KEEP_Q, d[n + 1])
        + (times(KEEP_Q * 5.0 / 3.0 - 2.0 / 3.0, moved[n]) - (KEEP_Q * 5.0 / 3.0) * force[n])
        for n in range(3)
    ]
    tenth = [0.1 * moved[n] for n in range(3)]
    axis_odd = [tenth[n] - 0.1 * flux[n] for n in range(3)]
    diag_odd = [tenth[n] + 0.025 * flux[n] for n in range(3)]
    third = KEEP_M / 8.0
    mx, my, mz = third * (p_xy - p_xz), third * (p_yz - q_xy), third * (q_xz - q_yz)

    twist = even_axis - h
    evens = [even_axis + 2.0 * h, twist + k, twist - k]
    ring = even_diag + g
    e_xy, e_xz, e_yz = ring + l, ring - l, even_diag - 2.0 * g
    a, b = diag_odd[0] + mx, diag_odd[1] - my
    odd_xy = (a + b, a - b)
    a, b = diag_odd[0] - mx, diag_odd[2] + mz
    odd_xz = (a + b, a - b)
    a, b = diag_odd[1] + my, diag_odd[2] - mz
    odd_yz = (a + b, a - b)

    post = [even_rest]
    for n in range(3):
        post += [evens[n] + axis_odd[n], evens[n] - axis_odd[n]]
    for even, t, odd in ((e_xy, t_xy, odd_xy), (e_xz, t_xz, odd_xz), (e_yz, t_yz, odd_yz)):
        same, cross = even + t, even - t
        post += [same + odd[0], same - odd[0], cross + odd[1], cross - odd[1]]
    return [jnp.where(solid, f[OPPOSITE[i]], post[i]) for i in range(19)]


class Shape:
    def __init__(self, mesh, block):
        self.nx, self.ny, self.nz = (mesh.shape[a] for a in ("gx", "gy", "gz"))
        self.x, self.y, self.z = block
        self.slab = self.z // self.nx
        self.width = LANES // 2
        self.groups = 2
        self.own = self.x // self.groups
        self.subs = self.x * self.nx // self.groups
        self.span = self.slab + 2 * HALO
        self.tiles = -(-5 * self.x * self.span // LANES)
        self.rows = self.y + 2 * HALO
        assert self.z == LANES and self.slab * self.nx == self.z
        assert self.slab + 2 * HALO <= self.width and 2 * self.slab <= self.width
        assert self.y == HALO and self.own * self.groups == self.x
        assert self.subs % 8 == 0
        if self.nx & (self.nx - 1) == 0:
            self.peer = lambda k, slot: jnp.bitwise_xor(k, slot)
            self.perm = lambda slot: [(i, i ^ slot) for i in range(self.nx)]
            self.sender = self.peer
        else:
            self.peer = lambda k, slot: lax.rem(k + slot, self.nx)
            self.sender = lambda k, slot: lax.rem(k + self.nx - slot, self.nx)
            self.perm = lambda slot: [(i, (i + slot) % self.nx) for i in range(self.nx)]

    def window(self, n, x):
        return divmod((n * self.x + x) * self.span, LANES)


def vmem(n):
    return [pl.BlockSpec(memory_space=pltpu.VMEM)] * n


def grant(words):
    return pltpu.CompilerParams(vmem_limit_bytes=(words * 4 * 5) // 4 + (1 << 20))


def join_slots(parts):
    def body(*refs):
        for n, ref in enumerate(refs[:-1]):
            refs[-1][n] = ref[...]

    block = parts[0].shape
    return pl.pallas_call(
        body,
        name="join_slots",
        out_shape=jax.ShapeDtypeStruct((len(parts),) + block, jnp.float32),
        in_specs=vmem(len(parts)),
        out_specs=vmem(1)[0],
        compiler_params=grant(2 * len(parts) * math.prod(block)),
    )(*parts)


def gather_inputs(scatter, velocity, bubbles, walls):
    rho = jnp.where(bubbles == 1, VAPOUR, LIQUID) * scatter
    solid = jnp.where(walls == 1, 1.0, 0.0)
    return jnp.concatenate([rho[None], velocity, solid[None]])


def cut_slabs(values, before, after, sh):
    def body(v_ref, b_ref, a_ref, *outs):
        k = lax.axis_index("gx")
        lane = lax.broadcasted_iota(jnp.int32, (sh.y, LANES), 1)
        for slot, out in enumerate(outs):
            q = sh.peer(k, slot)
            low = (lane >= LANES - HALO) & (q == 0)
            high = (lane < HALO) & (q == sh.nx - 1)
            start = HALO - q * sh.slab + 2 * LANES
            tile = None
            for n in range(5):
                for x in range(sh.x):
                    plane = jnp.where(low, b_ref[n, x], v_ref[n, x])
                    plane = jnp.where(high, a_ref[n, x], plane)
                    at, off = sh.window(n, x)
                    plane = pltpu.roll(plane, lax.rem(start + off, LANES), 1)
                    tile = plane if tile is None else jnp.where(lane >= off, plane, tile)
                    if off + sh.span >= LANES:
                        out[at] = tile
                        tile = plane if off + sh.span > LANES else None
            if tile is not None:
                out[sh.tiles - 1] = tile

    shape = (sh.tiles, sh.y, LANES)
    return pl.pallas_call(
        body,
        name="cut_slabs",
        out_shape=[jax.ShapeDtypeStruct(shape, jnp.float32)] * sh.nx,
        in_specs=vmem(3),
        out_specs=vmem(sh.nx),
        compiler_params=grant(3 * math.prod(values.shape) + sh.nx * math.prod(shape)),
    )(values, before, after)


STAGES = ("own", "above", "below")


class Rows:
    def __init__(self, sh):
        self.sh = sh
        self.own, self.end = HALO, HALO + sh.y
        lane = lax.broadcasted_iota(jnp.int32, (sh.subs, LANES), 1)
        self.odd = lane >= sh.width

    def inputs(self, stage):
        first = {"own": self.own, "above": self.end, "below": 0}[stage]
        return first, first + self.sh.y - 1

    def weighed(self, stage, s):
        own, end, rows = self.own, self.end, self.sh.rows
        return {
            "own": (own + 2 * s, end - 1 - 2 * s),
            "above": (max(own + 2 * s, end - 2 * s), rows - 1 - 2 * s),
            "below": (2 * s, own - 1 + 2 * s),
        }[stage]

    def collided(self, stage, s):
        own, end, rows = self.own, self.end, self.sh.rows
        return {
            "own": (own + 1 + 2 * s, end - 2 - 2 * s),
            "above": (max(own + 1 + 2 * s, end - 1 - 2 * s), rows - 2 - 2 * s),
            "below": (1 + 2 * s, own + 2 * s),
        }[stage]

    def steps(self, stage):
        ranges = [self.collided(stage, s) for s in range(STEPS)]
        return [s for s, (first, last) in enumerate(ranges) if first <= last]

    def buffers(self, stage):
        left = {("solid",): ((),) + self.inputs(stage), ("f", 0): ((19,),) + self.inputs(stage)}
        for s in self.steps(stage):
            left["psi", s] = ((),) + self.weighed(stage, s)
            first, last = self.collided(stage, s)
            left["f", s + 1] = ((19,), first - 1, last + 1)
        return left

    def shapes(self, stage):
        return [
            lead + (last + 1 - first, self.sh.subs, LANES)
            for lead, first, last in self.buffers(stage).values()
        ]

    def shifted(self, value, cx, cz):
        if cx == 1:
            value = jnp.where(self.odd, pltpu.roll(value, 1, 0), value)
        if cx == -1:
            value = jnp.where(self.odd, value, pltpu.roll(value, self.sh.subs - 1, 0))
        turn = (cx * self.sh.width + cz) % LANES
        return pltpu.roll(value, turn, 1) if turn else value

    def unpack(self, raw, ref, k):
        sh = self.sh
        wide = lax.broadcasted_iota(jnp.int32, (sh.y, LANES), 1)

        def plane(slot, n, x):
            at, off = sh.window(n, x)
            value = ref[slot, at]
            if off + sh.span > LANES:
                value = jnp.where(wide >= off, value, ref[slot, at + 1])
            turn = (x % 2 * sh.width - off) % LANES
            return pltpu.roll(value, turn, 1) if turn else value

        for slot in range(sh.nx):
            base = sh.sender(k, slot) * (sh.own * sh.y)
            for n in range(5):
                for m in range(sh.own):
                    value = jnp.where(
                        wide < sh.width, plane(slot, n, 2 * m), plane(slot, n, 2 * m + 1)
                    )
                    raw[n, pl.ds(pl.multiple_of(base + m * sh.y, 8), sh.y), :] = value

    def push(self, psi, y):
        shifted = self.shifted
        here, up, down = psi(y), psi(y + 1), psi(y - 1)
        rise = up - down
        doubled = 2.0 * here + (up + down)
        z_sum = doubled + (shifted(here, 0, 1) + shifted(here, 0, -1))
        x_sum = doubled + (shifted(here, 1, 0) + shifted(here, -1, 0))
        fy = (2.0 * rise + (shifted(rise, 1, 0) + shifted(rise, -1, 0))) + (
            shifted(rise, 0, 1) + shifted(rise, 0, -1)
        )
        fx = shifted(z_sum, -1, 0) - shifted(z_sum, 1, 0)
        fz = shifted(x_sum, 0, -1) - shifted(x_sum, 0, 1)
        scale = here * (1.0 / 36.0)
        return [scale * value for value in (fx, fy, fz)]

    def run(self, stage, held, raw, force_ref, sums_ref, fresh, k, finish):
        sh = self.sh
        table = {other: self.buffers(other) for other in STAGES}
        keep = stage == STAGES[-1]

        def at(owner, name, y):
            return held[owner, name], y - table[owner][name][1]

        def owner_of(ranges, y):
            for other in STAGES:
                first, last = ranges(other)
                if first <= y <= last:
                    return other
            raise AssertionError(y)

        def solid(y):
            ref, row = at(owner_of(self.inputs, y), ("solid",), y)
            return ref[row] > 0.5

        def psi_of(s):
            def psi(y):
                ref, row = at(owner_of(lambda o: self.weighed(o, s), y), ("psi", s), y)
                return ref[row]

            return psi

        def f(s, i, y):
            if s == 0:
                owner = owner_of(self.inputs, y)
            else:
                from_row = y - int(C[i, 1])
                owner = owner_of(lambda o: self.collided(o, s - 1), from_row)
            ref, row = at(owner, ("f", s), y)
            return ref[i, row]

        def begin(y):
            n = y - self.inputs(stage)[0]
            rho, ux, uy, uz, wall = (raw[v, pl.ds(n, sh.subs, stride=sh.y), :] for v in range(5))
            held[stage, ("solid",)][n] = wall
            for i, row in enumerate(equilibrium(rho, [ux, uy, uz])):
                held[stage, ("f", 0)][i, n] = row

        def weigh(s, y):
            sums = pair_sums([f(s, i, y) for i in range(19)])
            psi = potential(sums[-1])
            if keep:
                for n, value in enumerate(sums):
                    sums_ref[s, n, y - self.weighed(stage, s)[0]] = value
            to = held[stage, ("psi", s)]
            to[y - self.weighed(stage, s)[0]] = jnp.where(solid(y), WALL_POTENTIAL, psi)

        def form(s, y):
            for n, value in enumerate(self.push(psi_of(s), y)):
                force_ref[s, n, y] = value

        def advance(s, y):
            force = [force_ref[s, axis, y] for axis in range(3)]
            row = [f(s, i, y) for i in range(19)]
            first, last = self.weighed(stage, s)
            if keep and first <= y <= last:
                sums = [sums_ref[s, n, y - first] for n in range(15)]
            else:
                sums = pair_sums(row)
            post = collide(row, sums, force, solid(y))
            base = self.collided(stage, s)[0] - 1
            for i in range(19):
                cx, cy, cz = (int(c) for c in C[i])
                held[stage, ("f", s + 1)][i, y + cy - base] = self.shifted(post[i], cx, cz)

        self.unpack(raw, fresh, k)
        if stage == STAGES[-1]:
            count = sh.y

            def at_tick(tick):
                items = [(s, self.own + 2 * s - (tick - LAG * s)) for s in range(STEPS)]
                return [(s, y) for s, y in items if 0 <= tick - LAG * s < count]

            for tick in range(-1, count + LAG * (STEPS - 1)):
                for s, y in at_tick(tick + 1):
                    if s == 0:
                        begin(y - 1)
                    weigh(s, y - 1)
                    form(s, y)
                for s, y in at_tick(tick):
                    advance(s, y)
                row = self.end - 1 - (tick - LAG * (STEPS - 1) - 1)
                if self.own <= row < self.end:
                    finish(f, solid, row)
            finish(f, solid, self.own)
            return

        first, last = self.inputs(stage)
        for y in range(first, last + 1):
            begin(y)
        for s in self.steps(stage):
            first, last = self.weighed(stage, s)
            for y in range(first, last + 1):
                weigh(s, y)
            first, last = self.collided(stage, s)
            ys = list(range(first, last + 1))
            for y in ys[:AHEAD]:
                form(s, y)
            for n, y in enumerate(ys):
                advance(s, y)
                if n + AHEAD < len(ys):
                    form(s, ys[n + AHEAD])


def run_stage(stage, fresh, left, sh, flops):
    rows = Rows(sh)
    before = STAGES[: STAGES.index(stage)]
    names = [(o, name) for o in before for name in rows.buffers(o)]
    own = [(stage, name) for name in rows.buffers(stage)]
    last_stage = stage == STAGES[-1]

    def body(fresh_ref, *refs):
        held = dict(zip(names, refs))
        refs = refs[len(names) :]
        outs = ()
        if last_stage:
            outs, refs = refs[: sh.nx], refs[sh.nx :]
        held.update(zip(own, refs))
        raw, force_ref, sums_ref, done = refs[len(own) :]
        k = lax.axis_index("gx")
        low = Rows(sh)

        def finish(f, solid, y):
            g = [f(STEPS, i, y) for i in range(19)]
            rho, wall = sum(g[1:], g[0]), solid(y)
            inverse = math.sqrt(3.0) / rho
            results = [rho * (1.0 / LIQUID)] + [c * inverse for c in moments(g)]
            for v, value in enumerate(results):
                at = pl.ds(y - low.own, sh.subs, stride=sh.y)
                done[v, at, :] = jnp.where(wall, 0.0, value)

        low.run(stage, held, raw, force_ref, sums_ref, fresh_ref, k, finish)
        if not last_stage:
            return
        lane = lax.broadcasted_iota(jnp.int32, (sh.y, LANES), 1)
        place = (lane % sh.width) // sh.slab
        for slot, out in enumerate(outs):
            base = sh.peer(k, slot) * (sh.own * sh.y)
            for v in range(4):
                merged = None
                for m in range(sh.own):
                    value = done[v, pl.ds(pl.multiple_of(base + m * sh.y, 8), sh.y), :]
                    value = pltpu.roll(value, (m * sh.slab - HALO) % LANES, 1)
                    merged = value if m == 0 else jnp.where(place == m, value, merged)
                out[v] = merged

    shapes = rows.shapes(stage)
    piece = jax.ShapeDtypeStruct((4, sh.y, LANES), jnp.float32)
    scratch = [pltpu.VMEM(shape, jnp.float32) for shape in shapes]
    extra = [
        pltpu.VMEM((5, sh.subs * sh.y, LANES), jnp.float32),
        pltpu.VMEM((STEPS, 3, sh.rows, sh.subs, LANES), jnp.float32),
        pltpu.VMEM((STEPS, 15, sh.y, sh.subs, LANES), jnp.float32),
        pltpu.VMEM((4, sh.subs * sh.y, LANES), jnp.float32),
    ]
    outs = [jax.ShapeDtypeStruct(shape, jnp.float32) for shape in shapes]
    if last_stage:
        outs, extra = [piece] * sh.nx, scratch + extra
    operands = (fresh,) + tuple(left)
    words = sum(math.prod(a.shape) for a in list(operands) + list(outs) + list(extra))
    return pl.pallas_call(
        body,
        name="stage_" + stage,
        out_shape=outs,
        in_specs=vmem(len(operands)),
        out_specs=vmem(len(outs)),
        scratch_shapes=extra,
        compiler_params=grant(words),
        cost_estimate=pl.CostEstimate(flops=flops, transcendentals=0, bytes_accessed=words * 4),
    )(*operands)


def place_outputs(pieces, sh):
    def body(*refs):
        ins, (density, velocity) = refs[: sh.nx], refs[sh.nx :]
        k = lax.axis_index("gx")
        place = lax.broadcasted_iota(jnp.int32, (sh.y, LANES), 1) // sh.slab
        for v in range(4):
            for x in range(sh.x):
                m, g = divmod(x, 2)
                merged = None
                for slot, ref in enumerate(ins):
                    q = sh.sender(k, slot)
                    turn = (q - m) * sh.slab - g * sh.width + 2 * LANES
                    value = pltpu.roll(ref[v], lax.rem(turn, LANES), 1)
                    merged = value if slot == 0 else jnp.where(place == q, value, merged)
                if v == 0:
                    density[x] = merged
                else:
                    velocity[v - 1, x] = merged

    block = (sh.x, sh.y, sh.z)
    return pl.pallas_call(
        body,
        name="place_outputs",
        out_shape=[
            jax.ShapeDtypeStruct(block, jnp.float32),
            jax.ShapeDtypeStruct((3,) + block, jnp.float32),
        ],
        in_specs=vmem(sh.nx),
        out_specs=vmem(2),
        compiler_params=grant(8 * sh.nx * sh.y * LANES + 8 * math.prod(block)),
    )(*pieces)


def ring(size, step):
    return [(i, (i + step) % size) for i in range(size)]


def solution(mesh):
    def on_device(density_scatter, initial_velocity, bubble_mask, wall_flags):
        sh = Shape(mesh, wall_flags.shape)
        values = gather_inputs(density_scatter, initial_velocity, bubble_mask, wall_flags)
        before = lax.ppermute(values, "gz", ring(sh.nz, 1))
        after = before if sh.nz == 2 else lax.ppermute(values, "gz", ring(sh.nz, -1))
        slabs = cut_slabs(values, before, after, sh)
        got = [slabs[0]]
        for slot in range(1, sh.nx):
            got.append(lax.ppermute(slabs[slot], "gx", sh.perm(slot)))
        middle = join_slots(got)
        below = lax.ppermute(middle, "gy", ring(sh.ny, 1))
        above = lax.ppermute(middle, "gy", ring(sh.ny, -1))
        left = run_stage("own", middle, (), sh, 5_000_000)
        left = left + run_stage("above", above, left, sh, 20_000_000)
        pieces = run_stage("below", below, left, sh, 30_000_000)
        back = [pieces[0]]
        for slot in range(1, sh.nx):
            back.append(lax.ppermute(pieces[slot], "gx", sh.perm(slot)))
        return tuple(place_outputs(back, sh))

    in_specs = (
        P("gx", "gy", "gz"),
        P(None, "gx", "gy", "gz"),
        P("gx", "gy", "gz"),
        P("gx", "gy", "gz"),
    )
    out_specs = (P("gx", "gy", "gz"), P(None, "gx", "gy", "gz"))
    return jax.shard_map(
        on_device, mesh=mesh, in_specs=in_specs, out_specs=out_specs, check_vma=False
    )
```
